256 devices in a mesh: req: 32 (over z, x), tp: 8 (over y, core).
Axes of the slice: x: 4, y: 4, z: 8, core: 2. Of those that a mesh axis runs over, the one named last changes fastest.
Arguments:
- hidden_in: bfloat16 [32768, 2048], P('req'), may hold values from -6 to 6
- qkv_weight: bfloat16 [2048, 3, 2048], P(None, None, 'tp'), may hold values from -0.125 to 0.125
- out_weight: bfloat16 [2048, 2048], P('tp'), may hold values from -1.5 to 1.5
- kv_pool: bfloat16 [512, 2, 128, 2048], P('req', None, None, 'tp'), may hold values from -48 to 48
- cached_len: int32 [32], replicated, may hold values from 3585 to 4096, as said below
- page_slot: int32 [32, 32], replicated, may hold values from 0 to 15
- page_holder: int32 [32, 32, 1], replicated, may hold values from 0 to 31; in each aligned block of 32 rows (0 to 31, 32 to 63, ..., all dimensions but the last counted through in order) at most 2 rows name the same one
- cont_flag: int32 [32], replicated, may hold values 0 or 1
Outputs:
- attn_out: bfloat16 [32768, 2048], P(('req', 'tp'))
The draws below stay inside these ranges and needn't reach their ends.
Inputs may be any that keep to these rules, and one draw needn't show every extreme that they name: `page_holder`: within the table entries of the requests of one index of req (aligned blocks of 1 request), no holder is named more than 2 times. `cached_len`: A cached length of 4096 occurs in every draw. `page_slot`: page slot k of holder h is row h * 16 + k of kv_pool.
All inputs are finite; a program needn't handle non-finite values.
Results may differ from the reference program's by a relative error of at most 0.02.
Values may be sent and summed in bfloat16 or wider, within the bound.
A program may use at most 128 MiB of HBM per device.

```python
import math
import jax
import jax.numpy as jnp
import numpy as np
from jax import lax

D = 2048
HEADS = 16
HD = 128
NEW = 1024
R_DEV = 1
PAGE = 128
MAXP = 32
POOL_DEV = 16
REQS = 32
TOKENS = 32768
CACHE = 4096
POOL = 512
CAP = 2
N_REQ = 32
N_TP = 8


def draw_kv_pool(key, part):
    full_shape = (POOL, 2, PAGE, HEADS * HD)
    key_base = jax.random.fold_in(jax.random.fold_in(key, 11), 0)
    scales = jnp.array([1.5, 1.0], jnp.float32).reshape(1, 2, 1, 1)
    base_draw = jnp.clip(jax.random.normal(key_base, full_shape, jnp.float32), -6.0, 6.0) * scales
    return base_draw.astype(jnp.bfloat16)


def draw_cached_len(key, part):
    key_lengths, key_longest = jax.random.split(jax.random.fold_in(key, 23))
    lengths = jax.random.randint(key_lengths, (REQS,), 7 * CACHE // 8 + 1, CACHE + 1)
    longest = jax.random.randint(key_longest, (), 0, REQS)
    return jnp.where(jnp.arange(REQS) == longest, CACHE, lengths).astype(jnp.int32)


def set_ends(values, key, least, largest):
    longest = values.shape.index(max(values.shape))
    spots = []
    for shift in (0, 1):
        where = [jax.random.randint(jax.random.fold_in(key, axis), (), 0, length) for axis, length in enumerate(values.shape)]
        where[longest] = (where[longest] + shift) % values.shape[longest]
        spots.append(tuple(where))
    return values.at[spots[0]].set(least).at[spots[1]].set(largest)


def block_scale(stream_key, shape, cuts, least, largest):
    factor_of = 1.0
    for dim, blocks in cuts:
        heights = jax.random.uniform(jax.random.fold_in(jax.random.fold_in(stream_key, 6), dim), (blocks,), jnp.float32, least / len(cuts), largest / len(cuts))
        factor_of = factor_of * jnp.repeat(jnp.exp(heights), shape[dim] // blocks).reshape((-1,) + (1,) * (len(shape) - 1 - dim))
    return factor_of


def shared_out(own_key, own, number, rows, count, top, reach, skew):
    order = jax.random.permutation(own_key, count)
    packed, common = portions_of(count, rows * top, reach, skew, True), portions_of(count, rows * top, reach, skew, False)
    places = jnp.arange(count)

    def named(sizes, offset_by):
        used = int((sizes > 0).sum())
        fixed = max(1, used // 4)
        shifted = fixed + (places - fixed + offset_by * (used - fixed)) % max(1, count - fixed)
        return jnp.zeros((count,), jnp.int32).at[order[jnp.where(places < fixed, places, shifted)]].set(jnp.asarray(sizes, jnp.int32))

    sizes = jnp.where(number % 4 == 0, named(packed, number // 4), named(common, number - number // 4 - 1))
    mixed = jax.random.permutation(jax.random.fold_in(own, 3), count)
    source_of, receiver = mixed[0:count // 2 * 2:2], mixed[1:count // 2 * 2:2]
    slack = jnp.minimum(sizes[source_of] - 1, reach - sizes[receiver]) // 2
    slack = jnp.where((source_of == order[0]) | (receiver == order[0]) | (sizes[receiver] == 0), 0, jnp.maximum(slack, 0))
    shifted = jax.random.randint(jax.random.fold_in(own, 4), (count // 2,), 0, 1 << 20) % (slack + 1)
    sizes = sizes.at[source_of].add(-shifted).at[receiver].add(shifted)
    members = jnp.searchsorted(jnp.cumsum(sizes), jnp.arange(rows * top), side="right").astype(jnp.int32)
    table = members.reshape(top, rows).T
    table = table[jax.random.permutation(jax.random.fold_in(own, 1), rows)]
    offset_by = jax.random.randint(jax.random.fold_in(own, 2), (rows, 1), 0, top)
    return jnp.take_along_axis(table, (jnp.arange(top)[None, :] + offset_by) % top, axis=1)


def portions_of(amount, total, bound, slope, full):
    weights = [(1 << 20) // math.isqrt(grade ** slope) + 1 for grade in range(1, amount + 1)]
    largest = bound if full else min(bound, max(-(-total // amount), total * weights[0] // sum(weights)))
    least = 1 if total - largest >= amount - 1 else 0
    given, rest = [largest] + [least] * (amount - 1), total - largest - least * (amount - 1)
    while rest > 0:
        movable = [i for i in range(1, amount) if given[i] < largest] or [i for i in range(1, amount) if given[i] < bound]
        whole, budget = sum([weights[i] for i in movable]), rest
        for i in movable:
            more = min(bound - given[i], max(1, budget * weights[i] // whole), rest)
            given[i] = given[i] + more
            rest = rest - more
    return np.array(given)


def bell_draw(stream_key, shape, scale, most, cuts=(), kind=jnp.bfloat16):
    entries = jax.random.normal(stream_key, shape, jnp.float32) * scale
    if len(cuts) > 0:
        entries = block_scale(stream_key, shape, cuts, -0.22, 0.18) * entries
    return jnp.clip(entries, min=-most, max=most).astype(kind)


def setup_inputs(seed: int = 0) -> dict:
    seeds = jax.random.split(jax.random.key(seed), 9)
    hidden_in = bell_draw(seeds[0], (TOKENS, D), 1.0, 6.0, ((0, 32),))
    qkv_weight = bell_draw(seeds[1], (D, 3, HEADS * HD), D ** -0.5, 0.125, ((2, 8),))
    out_weight = bell_draw(seeds[2], (HEADS * HD, D), (HD // 8) ** -0.5, 1.5, ((0, 8),))
    kv_pool = draw_kv_pool(jax.random.fold_in(seeds[8], 71), 0)
    cached_len = draw_cached_len(jax.random.fold_in(seeds[8], 71), 0)
    page_slot = set_ends(jax.random.randint(seeds[5], (REQS, MAXP), 0, POOL_DEV), jax.random.fold_in(seeds[5], 1), 0, POOL_DEV - 1).astype(jnp.int32)
    page_holder_keys = jax.random.split(jax.random.fold_in(seeds[6], 1), REQS * MAXP // (R_DEV * MAXP))
    page_holder_turns = jax.random.permutation(jax.random.fold_in(seeds[6], 3), REQS * MAXP // (R_DEV * MAXP))
    page_holder = jax.vmap(lambda own, number: shared_out(jax.random.fold_in(seeds[6], 2), own, number, R_DEV * MAXP, N_REQ, 1, CAP, 0))(page_holder_keys, page_holder_turns).reshape((REQS, MAXP, 1))
    cont_flag = set_ends((jax.random.randint(seeds[7], (REQS,), 0, 8) < 7).astype(jnp.int32), jax.random.fold_in(seeds[7], 1), 0, 1)
    return {"hidden_in": hidden_in, "qkv_weight": qkv_weight, "out_weight": out_weight, "kv_pool": kv_pool, "cached_len": cached_len, "page_slot": page_slot, "page_holder": page_holder, "cont_flag": cont_flag}


def rotate(feature, position):
    half_width = feature.shape[-1] // 2
    indices = jnp.arange(half_width).astype(jnp.float32)
    inverse = jnp.exp(indices * (-2.0 / feature.shape[-1]) * jnp.log(jnp.float32(10000.0)))
    angles = position[:, None, None] * inverse[None, None, :]
    cosine = jnp.cos(angles)
    sine_part = jnp.sin(angles)
    first_half = feature[..., :half_width]
    second_half = feature[..., half_width:]
    return jnp.concatenate([first_half * cosine - second_half * sine_part, second_half * cosine + first_half * sine_part], axis=-1)

def settle(value):
    return lax.optimization_barrier(value.astype(jnp.bfloat16))

def reference(hidden_in, qkv_weight, out_weight, kv_pool, cached_len, page_slot, page_holder, cont_flag):
    weight_wide = qkv_weight.astype(jnp.float32)
    group_width = HEADS * HD // N_TP
    out_groups = out_weight.astype(jnp.float32).reshape(N_TP, group_width, D)
    inputs_all = hidden_in.reshape(REQS, NEW, D)
    holders_all = page_holder[:, :, 0]

    def one_request(request_item):
        tokens_one, length_one, flag_one, slots_one, holders_one = request_item
        token_rows = tokens_one.astype(jnp.float32)
        centre = lax.optimization_barrier(jnp.mean(token_rows, axis=-1, keepdims=True))
        centred = token_rows - centre
        spread = lax.optimization_barrier(jnp.mean(centred * centred, axis=-1, keepdims=True))
        normed = settle(centred * lax.rsqrt(spread + 1e-05))
        united_qkv = jnp.einsum('td,dcf->tcf', normed.astype(jnp.float32), weight_wide)
        live_len = length_one * flag_one
        positions = (live_len + jnp.arange(NEW)).astype(jnp.float32)
        query_rot = settle(rotate(united_qkv[:, 0].reshape(NEW, HEADS, HD), positions))
        new_key = settle(rotate(united_qkv[:, 1].reshape(NEW, HEADS, HD), positions))
        new_value = settle(united_qkv[:, 2].reshape(NEW, HEADS, HD))
        page_rows = kv_pool[holders_one * POOL_DEV + slots_one]
        cache_key = page_rows[:, 0].reshape(CACHE, HEADS, HD)
        cache_value = page_rows[:, 1].reshape(CACHE, HEADS, HD)
        keys_all = jnp.concatenate([cache_key, new_key], axis=0)
        values_all = jnp.concatenate([cache_value, new_value], axis=0)
        scores = jnp.einsum('thd,khd->htk', query_rot.astype(jnp.float32), keys_all.astype(jnp.float32)) * HD ** (-0.5)
        key_pos = jnp.arange(CACHE + NEW)
        query_pos = jnp.arange(NEW)
        allowed = jnp.where(key_pos[None, :] < CACHE, key_pos[None, :] < live_len, key_pos[None, :] - CACHE <= query_pos[:, None])
        scores = jnp.where(allowed[None], scores, -1e+30)
        row_top = lax.optimization_barrier(jnp.max(scores, axis=-1, keepdims=True))
        weights = jnp.where(allowed[None], jnp.exp(scores - row_top), 0.0)
        row_total = lax.optimization_barrier(jnp.sum(weights, axis=-1))
        summed = jnp.einsum('htk,khd->htd', settle(weights).astype(jnp.float32), values_all.astype(jnp.float32))
        attended = settle((summed / row_total[:, :, None]).transpose(1, 0, 2).reshape(NEW, HEADS * HD))
        grouped = attended.astype(jnp.float32).reshape(NEW, N_TP, group_width)
        partial_sums = settle(jnp.einsum('tgf,gfd->gtd', grouped, out_groups))
        return lax.optimization_barrier(jnp.sum(partial_sums.astype(jnp.float32), axis=0)).astype(jnp.bfloat16)
    result = lax.map(one_request, (inputs_all, cached_len, cont_flag, page_slot, holders_all))
    return result.reshape(TOKENS, D)
```

```python
import jax
import jax.numpy as jnp
from jax import lax
from jax.sharding import PartitionSpec as P

HD = 128
NEW = 1024
PAGE = 128
MAXP = 32


def rotate(feature, position):
    half_width = feature.shape[-1] // 2
    indices = jnp.arange(half_width).astype(jnp.float32)
    inverse = jnp.exp(indices * (-2.0 / feature.shape[-1]) * jnp.log(jnp.float32(10000.0)))
    angles = position[:, None, None] * inverse[None, None, :]
    cosine = jnp.cos(angles)
    sine_part = jnp.sin(angles)
    first_half = feature[..., :half_width]
    second_half = feature[..., half_width:]
    return jnp.concatenate(
        [
            first_half * cosine - second_half * sine_part,
            second_half * cosine + first_half * sine_part,
        ],
        axis=-1,
    )


def attend_block(query_part, keys_part, values_part, allowed):
    scores = jnp.einsum(
        "qd,kd->qk", query_part, keys_part, preferred_element_type=jnp.float32
    ) * HD ** (-0.5)
    scores = jnp.where(allowed, scores, -1e30)
    row_top = jnp.max(scores, axis=-1)
    weights = jnp.where(allowed, jnp.exp(scores - row_top[:, None]), 0.0)
    row_total = jnp.sum(weights, axis=-1)
    summed = jnp.einsum(
        "qk,kd->qd", weights.astype(jnp.bfloat16), values_part, preferred_element_type=jnp.float32
    )
    return (summed, row_top, row_total)


def body(hidden_in, qkv_weight, out_weight, kv_pool, cached_len, page_slot, page_holder, cont_flag):
    req_count = lax.axis_size("req")
    tp_count = lax.axis_size("tp")
    req_index = lax.axis_index("req")
    local_reqs = hidden_in.shape[0] // NEW
    local_width = qkv_weight.shape[2]
    local_heads = local_width // HD
    cache_span = MAXP * PAGE
    holder_rows = page_holder[:, :, 0]
    all_rows = holder_rows.shape[0]
    same_holder_all = holder_rows[:, :, None] == holder_rows[:, None, :]
    entry_ids = jnp.arange(holder_rows.shape[1])
    earlier_all = entry_ids[None, None, :] < entry_ids[None, :, None]
    rank_all = jnp.sum((same_holder_all & earlier_all).astype(jnp.int32), axis=2)
    first_hit = (holder_rows == req_index) & (rank_all == 0)
    send_slots = jnp.sum(jnp.where(first_hit, page_slot, 0), axis=1)
    outgoing = kv_pool[send_slots]
    spill_flat = (rank_all > 0).reshape(-1)
    spill_pos = jnp.cumsum(spill_flat.astype(jnp.int32)) - 1
    spill_count = jnp.sum(spill_flat.astype(jnp.int32))
    holders_flat = holder_rows.reshape(-1)
    slots_flat = page_slot.reshape(-1)
    lengths = lax.dynamic_slice_in_dim(cached_len, req_index * local_reqs, local_reqs)
    flags = lax.dynamic_slice_in_dim(cont_flag, req_index * local_reqs, local_reqs)
    live_len = lengths * flags
    token_rows = hidden_in.astype(jnp.float32)
    centre = jnp.mean(token_rows, axis=-1, keepdims=True)
    centred = token_rows - centre
    spread = jnp.mean(centred * centred, axis=-1, keepdims=True)
    normed = (centred * lax.rsqrt(spread + 1e-05)).astype(jnp.bfloat16)
    united_qkv = jnp.einsum("td,dcf->tcf", normed, qkv_weight, preferred_element_type=jnp.float32)
    positions = (live_len[:, None] + jnp.arange(NEW)[None, :]).astype(jnp.float32).reshape(-1)
    query_rot = rotate(united_qkv[:, 0].reshape(-1, local_heads, HD), positions).astype(
        jnp.bfloat16
    )
    new_key = rotate(united_qkv[:, 1].reshape(-1, local_heads, HD), positions).astype(jnp.bfloat16)
    new_value = united_qkv[:, 2].reshape(-1, local_heads, HD).astype(jnp.bfloat16)
    row_count = local_reqs * NEW
    block_rows = min(512, NEW)
    req_blocks = NEW // block_rows
    row_blocks = row_count // block_rows
    work_items = local_heads * row_blocks
    query_heads = query_rot.transpose(1, 0, 2)
    new_places = jnp.arange(NEW)[None, :]

    def block_place(index):
        head = index // row_blocks
        block = index % row_blocks
        owner = block // req_blocks
        query_pos = block % req_blocks * block_rows + jnp.arange(block_rows)
        query_part = lax.dynamic_slice(
            query_heads, (head, block * block_rows, 0), (1, block_rows, HD)
        )[0]
        return (head, owner, query_pos, query_part)

    incoming = lax.all_to_all(outgoing, "req", split_axis=0, concat_axis=0, tiled=True)
    spill_chunk = 8

    def spill_pages(chunk):
        wanted = chunk * spill_chunk + jnp.arange(spill_chunk)
        match = spill_flat[None, :] & (spill_pos[None, :] == wanted[:, None])
        owner = jnp.sum(jnp.where(match, holders_flat[None, :], 0), axis=1)
        slot = jnp.sum(jnp.where(match, slots_flat[None, :], 0), axis=1)
        mine = jnp.any(match, axis=1) & (owner == req_index)
        contrib = jnp.where(mine[:, None, None, None], kv_pool[slot], jnp.zeros((), kv_pool.dtype))
        return lax.psum(contrib, "req")

    own_holders = lax.dynamic_index_in_dim(holder_rows, req_index, 0, keepdims=False)
    own_rank = lax.dynamic_index_in_dim(rank_all, req_index, 0, keepdims=False)
    own_pos = lax.dynamic_index_in_dim(spill_pos.reshape(all_rows, -1), req_index, 0, keepdims=False)
    first_spill = spill_pages(0)
    source = jnp.concatenate([incoming, first_spill], axis=0)
    pick = jnp.where(own_rank == 0, own_holders, req_count + jnp.clip(own_pos, 0, spill_chunk - 1))
    fetched = source[pick]

    def more_cond(carry):
        chunk, _ = carry
        return chunk * spill_chunk < spill_count

    def more_body(carry):
        chunk, pages = carry
        got = spill_pages(chunk)
        local = own_pos - chunk * spill_chunk
        hit = (own_rank > 0) & (local >= 0) & (local < spill_chunk)
        pages = jnp.where(hit[:, None, None, None], got[jnp.clip(local, 0, spill_chunk - 1)], pages)
        return (chunk + 1, pages)

    _, fetched = lax.while_loop(more_cond, more_body, (jnp.int32(1), fetched))
    fetched = fetched.reshape(local_reqs, MAXP, 2, PAGE, local_width)
    cache_key = fetched[:, :, 0].reshape(local_reqs, cache_span, local_heads, HD)
    cache_value = fetched[:, :, 1].reshape(local_reqs, cache_span, local_heads, HD)
    keys_all = jnp.concatenate(
        [cache_key, new_key.reshape(local_reqs, NEW, local_heads, HD)], axis=1
    )
    values_all = jnp.concatenate(
        [cache_value, new_value.reshape(local_reqs, NEW, local_heads, HD)], axis=1
    )

    def joined_block(index):
        head, owner, query_pos, query_part = block_place(index)
        keys_part = lax.dynamic_slice(
            keys_all, (owner, 0, head, 0), (1, cache_span + NEW, 1, HD)
        ).reshape(cache_span + NEW, HD)
        values_part = lax.dynamic_slice(
            values_all, (owner, 0, head, 0), (1, cache_span + NEW, 1, HD)
        ).reshape(cache_span + NEW, HD)
        live_one = lax.dynamic_index_in_dim(live_len, owner, 0, keepdims=False)
        cache_ok = jnp.broadcast_to(
            jnp.arange(cache_span)[None, :] < live_one, (block_rows, cache_span)
        )
        allowed = jnp.concatenate([cache_ok, new_places <= query_pos[:, None]], axis=1)
        summed, row_top, row_total = attend_block(query_part, keys_part, values_part, allowed)
        return (summed / row_total[:, None]).astype(jnp.bfloat16)

    blocks_out = lax.map(joined_block, jnp.arange(work_items))
    attended = (
        blocks_out.reshape(local_heads, row_count, HD)
        .transpose(1, 0, 2)
        .reshape(row_count, local_width)
    )
    head_term = jnp.dot(attended, out_weight, preferred_element_type=jnp.float32)
    return lax.psum_scatter(head_term.astype(jnp.bfloat16), "tp", scatter_dimension=0, tiled=True)


def solution(mesh):
    in_specs = (
        P("req", None),
        P(None, None, "tp"),
        P("tp", None),
        P("req", None, None, "tp"),
        P(),
        P(),
        P(),
        P(),
    )
    out_specs = P(("req", "tp"), None)
    return jax.shard_map(body, mesh=mesh, in_specs=in_specs, out_specs=out_specs, check_vma=False)
```

```python
import functools

import jax
import jax.numpy as jnp
from jax import lax
from jax.experimental import pallas as pl
from jax.experimental.pallas import tpu as pltpu
from jax.sharding import PartitionSpec as P

HD = 128
NEW = 1024
PAGE = 128
MAXP = 32
BLOCK_Q = 256


def rotate(feature, position):
    half_width = feature.shape[-1] // 2
    indices = jnp.arange(half_width).astype(jnp.float32)
    inverse = jnp.exp(indices * (-2.0 / feature.shape[-1]) * jnp.log(jnp.float32(10000.0)))
    angles = position[:, None, None] * inverse[None, None, :]
    cosine = jnp.cos(angles)
    sine_part = jnp.sin(angles)
    first_half = feature[..., :half_width]
    second_half = feature[..., half_width:]
    return jnp.concatenate(
        [
            first_half * cosine - second_half * sine_part,
            second_half * cosine + first_half * sine_part,
        ],
        axis=-1,
    )


def attend_kernel(live_ref, q_ref, ck_ref, cv_ref, nk_ref, nv_ref, out_ref):
    block = pl.program_id(1)
    live = live_ref[0]
    cache_span = ck_ref.shape[0] * ck_ref.shape[2]
    query = q_ref[...]
    cache_key = ck_ref[...].reshape(cache_span, HD)
    cache_value = cv_ref[...].reshape(cache_span, HD)
    contract = (((1,), (1,)), ((), ()))
    scale = HD ** (-0.5)
    cache_scores = lax.dot_general(
        query, cache_key, contract, preferred_element_type=jnp.float32
    ) * scale
    new_scores = lax.dot_general(
        query, nk_ref[...], contract, preferred_element_type=jnp.float32
    ) * scale
    cache_ok = lax.broadcasted_iota(jnp.int32, cache_scores.shape, 1) < live
    query_pos = block * BLOCK_Q + lax.broadcasted_iota(jnp.int32, new_scores.shape, 0)
    new_ok = lax.broadcasted_iota(jnp.int32, new_scores.shape, 1) <= query_pos
    cache_scores = jnp.where(cache_ok, cache_scores, -1e30)
    new_scores = jnp.where(new_ok, new_scores, -1e30)
    row_top = jnp.maximum(
        jnp.max(cache_scores, axis=1, keepdims=True), jnp.max(new_scores, axis=1, keepdims=True)
    )
    cache_weights = jnp.where(cache_ok, jnp.exp(cache_scores - row_top), 0.0)
    new_weights = jnp.where(new_ok, jnp.exp(new_scores - row_top), 0.0)
    row_total = jnp.sum(cache_weights, axis=1, keepdims=True) + jnp.sum(
        new_weights, axis=1, keepdims=True
    )
    summed = jnp.dot(
        cache_weights.astype(jnp.bfloat16), cache_value, preferred_element_type=jnp.float32
    ) + jnp.dot(new_weights.astype(jnp.bfloat16), nv_ref[...], preferred_element_type=jnp.float32)
    out_ref[...] = (summed / row_total).astype(out_ref.dtype)


def attend(live, query, pages, new_key, new_value):
    rows, width = query.shape
    heads = width // HD
    pages_n = pages.shape[0]
    grid_spec = pltpu.PrefetchScalarGridSpec(
        num_scalar_prefetch=1,
        grid=(heads, rows // BLOCK_Q),
        in_specs=[
            pl.BlockSpec((BLOCK_Q, HD), lambda h, b, live: (b, h)),
            pl.BlockSpec((pages_n, None, PAGE, HD), lambda h, b, live: (0, 0, 0, h)),
            pl.BlockSpec((pages_n, None, PAGE, HD), lambda h, b, live: (0, 1, 0, h)),
            pl.BlockSpec((rows, HD), lambda h, b, live: (0, h)),
            pl.BlockSpec((rows, HD), lambda h, b, live: (0, h)),
        ],
        out_specs=pl.BlockSpec((BLOCK_Q, HD), lambda h, b, live: (b, h)),
    )
    keys_n = pages_n * PAGE + rows
    return pl.pallas_call(
        attend_kernel,
        grid_spec=grid_spec,
        out_shape=jax.ShapeDtypeStruct((rows, width), jnp.bfloat16),
        compiler_params=pltpu.CompilerParams(vmem_limit_bytes=48 * 1024 * 1024),
        cost_estimate=pl.CostEstimate(
            flops=4 * rows * keys_n * width,
            transcendentals=rows * keys_n * heads,
            bytes_accessed=2 * (2 * keys_n * width + 2 * rows * width),
        ),
    )(live, query, pages, pages, new_key, new_value)


def body(hidden_in, qkv_weight, out_weight, kv_pool, cached_len, page_slot, page_holder, cont_flag):
    req_count = lax.axis_size("req")
    req_index = lax.axis_index("req")
    local_reqs = hidden_in.shape[0] // NEW
    local_width = qkv_weight.shape[2]
    local_heads = local_width // HD
    table_block = local_reqs * MAXP
    capacity = max(2, 2 * table_block // req_count)
    holder_rows = page_holder[:, :, 0]
    held_here = holder_rows == req_index
    ranking = jnp.cumsum(held_here.astype(jnp.int32), axis=1) - 1
    picked = held_here[:, :, None] & (ranking[:, :, None] == jnp.arange(capacity)[None, None, :])
    send_slots = jnp.sum(jnp.where(picked, page_slot[:, :, None], 0), axis=1)
    outgoing = kv_pool[send_slots]
    incoming = lax.all_to_all(outgoing, "req", split_axis=0, concat_axis=0, tiled=True)
    lengths = lax.dynamic_slice_in_dim(cached_len, req_index * local_reqs, local_reqs)
    flags = lax.dynamic_slice_in_dim(cont_flag, req_index * local_reqs, local_reqs)
    live_len = lengths * flags
    token_rows = hidden_in.astype(jnp.float32)
    centre = jnp.mean(token_rows, axis=-1, keepdims=True)
    centred = token_rows - centre
    spread = jnp.mean(centred * centred, axis=-1, keepdims=True)
    normed = (centred * lax.rsqrt(spread + 1e-05)).astype(jnp.bfloat16)
    united_qkv = jnp.einsum("td,dcf->tcf", normed, qkv_weight, preferred_element_type=jnp.float32)
    positions = (live_len[:, None] + jnp.arange(NEW)[None, :]).astype(jnp.float32).reshape(-1)
    query_rot = rotate(united_qkv[:, 0].reshape(-1, local_heads, HD), positions).astype(
        jnp.bfloat16
    ).reshape(-1, local_width)
    new_key = rotate(united_qkv[:, 1].reshape(-1, local_heads, HD), positions).astype(
        jnp.bfloat16
    ).reshape(-1, local_width)
    new_value = united_qkv[:, 2].astype(jnp.bfloat16)
    own_holders = lax.dynamic_index_in_dim(holder_rows, req_index, 0, keepdims=False)
    same_holder = own_holders[:, None] == own_holders[None, :]
    earlier = jnp.arange(table_block)[None, :] < jnp.arange(table_block)[:, None]
    own_rank = jnp.sum((same_holder & earlier).astype(jnp.int32), axis=1)
    fetched = incoming.reshape(req_count * capacity, 2, PAGE, local_width)[
        own_holders * capacity + own_rank
    ]
    attended = attend(live_len[:1], query_rot, fetched, new_key, new_value)
    head_term = jnp.dot(attended, out_weight, preferred_element_type=jnp.float32)
    return lax.psum_scatter(head_term.astype(jnp.bfloat16), "tp", scatter_dimension=0, tiled=True)


def solution(mesh):
    in_specs = (
        P("req", None),
        P(None, None, "tp"),
        P("tp", None),
        P("req", None, None, "tp"),
        P(),
        P(),
        P(),
        P(),
    )
    out_specs = P(("req", "tp"), None)
    return jax.shard_map(body, mesh=mesh, in_specs=in_specs, out_specs=out_specs, check_vma=False)
```

```python
import functools

import jax
import jax.numpy as jnp
from jax import lax
from jax.experimental import pallas as pl
from jax.experimental.pallas import tpu as pltpu
from jax.sharding import PartitionSpec as P

HD = 128
NEW = 1024
PAGE = 128
MAXP = 32
BLOCK_Q = 256
RELAY_A = 8
RELAY_B = 1


def rotate(feature, position):
    half_width = feature.shape[-1] // 2
    indices = jnp.arange(half_width).astype(jnp.float32)
    inverse = jnp.exp(indices * (-2.0 / feature.shape[-1]) * jnp.log(jnp.float32(10000.0)))
    angles = position[:, None, None] * inverse[None, None, :]
    cosine = jnp.cos(angles)
    sine_part = jnp.sin(angles)
    first_half = feature[..., :half_width]
    second_half = feature[..., half_width:]
    return jnp.concatenate(
        [
            first_half * cosine - second_half * sine_part,
            second_half * cosine + first_half * sine_part,
        ],
        axis=-1,
    )


def attend_kernel(live_ref, q_ref, ck_ref, cv_ref, nk_ref, nv_ref, out_ref):
    block = pl.program_id(1)
    live = live_ref[0]
    cache_span = ck_ref.shape[0] * ck_ref.shape[2]
    query = q_ref[...]
    cache_key = ck_ref[...].reshape(cache_span, HD)
    cache_value = cv_ref[...].reshape(cache_span, HD)
    contract = (((1,), (1,)), ((), ()))
    scale = HD ** (-0.5)
    cache_scores = lax.dot_general(
        query, cache_key, contract, preferred_element_type=jnp.float32
    ) * scale
    new_scores = lax.dot_general(
        query, nk_ref[...], contract, preferred_element_type=jnp.float32
    ) * scale
    cache_ok = lax.broadcasted_iota(jnp.int32, cache_scores.shape, 1) < live
    query_pos = block * BLOCK_Q + lax.broadcasted_iota(jnp.int32, new_scores.shape, 0)
    new_ok = lax.broadcasted_iota(jnp.int32, new_scores.shape, 1) <= query_pos
    cache_scores = jnp.where(cache_ok, cache_scores, -1e30)
    new_scores = jnp.where(new_ok, new_scores, -1e30)
    row_top = jnp.maximum(
        jnp.max(cache_scores, axis=1, keepdims=True), jnp.max(new_scores, axis=1, keepdims=True)
    )
    cache_weights = jnp.where(cache_ok, jnp.exp(cache_scores - row_top), 0.0)
    new_weights = jnp.where(new_ok, jnp.exp(new_scores - row_top), 0.0)
    row_total = jnp.sum(cache_weights, axis=1, keepdims=True) + jnp.sum(
        new_weights, axis=1, keepdims=True
    )
    summed = jnp.dot(
        cache_weights.astype(jnp.bfloat16), cache_value, preferred_element_type=jnp.float32
    ) + jnp.dot(new_weights.astype(jnp.bfloat16), nv_ref[...], preferred_element_type=jnp.float32)
    out_ref[...] = (summed / row_total).astype(out_ref.dtype)


def attend(live, query, pages, new_key, new_value):
    rows, width = query.shape
    heads = width // HD
    pages_n = pages.shape[0]
    grid_spec = pltpu.PrefetchScalarGridSpec(
        num_scalar_prefetch=1,
        grid=(heads, rows // BLOCK_Q),
        in_specs=[
            pl.BlockSpec((BLOCK_Q, HD), lambda h, b, live: (b, h)),
            pl.BlockSpec((pages_n, None, PAGE, HD), lambda h, b, live: (0, 0, 0, h)),
            pl.BlockSpec((pages_n, None, PAGE, HD), lambda h, b, live: (0, 1, 0, h)),
            pl.BlockSpec((rows, HD), lambda h, b, live: (0, h)),
            pl.BlockSpec((rows, HD), lambda h, b, live: (0, h)),
        ],
        out_specs=pl.BlockSpec((BLOCK_Q, HD), lambda h, b, live: (b, h)),
    )
    keys_n = pages_n * PAGE + rows
    return pl.pallas_call(
        attend_kernel,
        grid_spec=grid_spec,
        out_shape=jax.ShapeDtypeStruct((rows, width), jnp.bfloat16),
        compiler_params=pltpu.CompilerParams(vmem_limit_bytes=48 * 1024 * 1024),
        cost_estimate=pl.CostEstimate(
            flops=4 * rows * keys_n * width,
            transcendentals=rows * keys_n * heads,
            bytes_accessed=2 * (2 * keys_n * width + 2 * rows * width),
        ),
    )(live, query, pages, pages, new_key, new_value)


def project(hidden_in, qkv_weight, live_len, local_heads, local_width):
    token_rows = hidden_in.astype(jnp.float32)
    centre = jnp.mean(token_rows, axis=-1, keepdims=True)
    centred = token_rows - centre
    spread = jnp.mean(centred * centred, axis=-1, keepdims=True)
    normed = (centred * lax.rsqrt(spread + 1e-05)).astype(jnp.bfloat16)
    united_qkv = jnp.einsum("td,dcf->tcf", normed, qkv_weight, preferred_element_type=jnp.float32)
    positions = (live_len[:, None] + jnp.arange(NEW)[None, :]).astype(jnp.float32).reshape(-1)
    query_rot = rotate(united_qkv[:, 0].reshape(-1, local_heads, HD), positions).astype(
        jnp.bfloat16
    ).reshape(-1, local_width)
    new_key = rotate(united_qkv[:, 1].reshape(-1, local_heads, HD), positions).astype(
        jnp.bfloat16
    ).reshape(-1, local_width)
    new_value = united_qkv[:, 2].astype(jnp.bfloat16)
    return query_rot, new_key, new_value


def exchange_wide(kv_pool, page_slot, holder_rows, rank_all, req_index, req_count):
    capacity = 2
    held_here = holder_rows == req_index
    ranking = jnp.cumsum(held_here.astype(jnp.int32), axis=1) - 1
    picked = held_here[:, :, None] & (ranking[:, :, None] == jnp.arange(capacity)[None, None, :])
    send_slots = jnp.sum(jnp.where(picked, page_slot[:, :, None], 0), axis=1)
    incoming = lax.all_to_all(kv_pool[send_slots], "req", split_axis=0, concat_axis=0, tiled=True)
    own_holders = holder_rows[req_index]
    own_rank = rank_all[req_index]
    return incoming.reshape((req_count * capacity,) + kv_pool.shape[1:])[
        own_holders * capacity + own_rank
    ]


def exchange_relay(kv_pool, page_slot, holder_rows, rank_all, req_index, req_count):
    rows, entries = holder_rows.shape
    spill = rank_all > 0
    frag = PAGE // req_count
    spill_flat = spill.reshape(-1)
    holders_flat = holder_rows.reshape(-1)
    slots_flat = page_slot.reshape(-1)
    by_holder = (holders_flat[:, None] == jnp.arange(req_count)[None, :]) & spill_flat[:, None]
    by_holder = by_holder.astype(jnp.int32)
    holder_order = jnp.sum((jnp.cumsum(by_holder, axis=0) - by_holder) * by_holder, axis=1)
    spill_i = spill.astype(jnp.int32)
    req_order = jnp.cumsum(spill_i, axis=1) - spill_i
    wanted = jnp.arange(RELAY_A)
    match_a = (
        spill_flat[None, :]
        & (holders_flat[None, :] == req_index)
        & (holder_order[None, :] == wanted[:, None])
    )
    slot_a = jnp.sum(jnp.where(match_a, slots_flat[None, :], 0), axis=1)
    pages_a = kv_pool[slot_a]
    pieces = pages_a.reshape(RELAY_A, 2, req_count, frag, -1).transpose(2, 0, 1, 3, 4)
    relayed = lax.all_to_all(pieces, "req", split_axis=0, concat_axis=0, tiled=True)
    relayed = relayed.reshape((req_count * RELAY_A, 2, frag, relayed.shape[-1]))
    match_b = spill[:, None, :] & (req_order[:, None, :] == jnp.arange(RELAY_B)[None, :, None])
    src_holder = jnp.sum(jnp.where(match_b, holder_rows[:, None, :], 0), axis=2)
    src_index = jnp.sum(
        jnp.where(match_b, holder_order.reshape(rows, entries)[:, None, :], 0), axis=2
    )
    extra = relayed[src_holder * RELAY_A + jnp.clip(src_index, 0, RELAY_A - 1)]
    extra = extra.transpose(0, 2, 1, 3, 4).reshape(rows, 2, RELAY_B * frag, -1)
    first_hit = (holder_rows == req_index) & (rank_all == 0)
    send_slots = jnp.sum(jnp.where(first_hit, page_slot, 0), axis=1)
    outgoing = jnp.concatenate([kv_pool[send_slots], extra], axis=2)
    incoming = lax.all_to_all(outgoing, "req", split_axis=0, concat_axis=0, tiled=True)
    first_pages = incoming[:, :, :PAGE]
    spill_pages = (
        incoming[:, :, PAGE:]
        .reshape(req_count, 2, RELAY_B, frag, -1)
        .transpose(2, 1, 0, 3, 4)
        .reshape(RELAY_B, 2, PAGE, -1)
    )
    source = jnp.concatenate([first_pages, spill_pages], axis=0)
    own_holders = holder_rows[req_index]
    pick = jnp.where(
        rank_all[req_index] == 0,
        own_holders,
        req_count + jnp.clip(req_order[req_index], 0, RELAY_B - 1),
    )
    return source[pick]


def body(hidden_in, qkv_weight, out_weight, kv_pool, cached_len, page_slot, page_holder, cont_flag):
    req_count = lax.axis_size("req")
    req_index = lax.axis_index("req")
    local_width = qkv_weight.shape[2]
    local_heads = local_width // HD
    holder_rows = page_holder[:, :, 0]
    entries = holder_rows.shape[1]
    same_holder = holder_rows[:, :, None] == holder_rows[:, None, :]
    earlier = jnp.arange(entries)[None, None, :] < jnp.arange(entries)[None, :, None]
    rank_all = jnp.sum((same_holder & earlier).astype(jnp.int32), axis=2)
    spill = (rank_all > 0).astype(jnp.int32)
    relay_fits = (jnp.max(jnp.sum(spill, axis=1)) <= RELAY_B) & (
        jnp.max(jnp.sum(spill[:, :, None] * (holder_rows[:, :, None] == jnp.arange(req_count)), axis=(0, 1)))
        <= RELAY_A
    )
    lengths = lax.dynamic_slice_in_dim(cached_len, req_index, 1)
    flags = lax.dynamic_slice_in_dim(cont_flag, req_index, 1)
    live_len = lengths * flags
    operands = (hidden_in, qkv_weight, kv_pool, page_slot, holder_rows, rank_all, live_len)

    def branch(exchange):
        def run(ops):
            hidden, weight, pool, slots, holders, ranks, live = ops
            fetched = exchange(pool, slots, holders, ranks, req_index, req_count)
            query_rot, new_key, new_value = project(hidden, weight, live, local_heads, local_width)
            return fetched, query_rot, new_key, new_value

        return run

    fetched, query_rot, new_key, new_value = lax.cond(
        relay_fits, branch(exchange_relay), branch(exchange_wide), operands
    )
    attended = attend(live_len, query_rot, fetched, new_key, new_value)
    head_term = jnp.dot(attended, out_weight, preferred_element_type=jnp.float32)
    return lax.psum_scatter(head_term.astype(jnp.bfloat16), "tp", scatter_dimension=0, tiled=True)


def solution(mesh):
    in_specs = (
        P("req", None),
        P(None, None, "tp"),
        P("tp", None),
        P("req", None, None, "tp"),
        P(),
        P(),
        P(),
        P(),
    )
    out_specs = P(("req", "tp"), None)
    return jax.shard_map(body, mesh=mesh, in_specs=in_specs, out_specs=out_specs, check_vma=False)
```

```python
import functools

import jax
import jax.numpy as jnp
from jax import lax
from jax.experimental import pallas as pl
from jax.experimental.pallas import tpu as pltpu
from jax.sharding import PartitionSpec as P

HD = 128
NEW = 1024
PAGE = 128
MAXP = 32
BLOCK_Q = 256
RELAY_A = 8
RELAY_B = 1


def rotate(feature, position):
    half_width = feature.shape[-1] // 2
    indices = jnp.arange(half_width).astype(jnp.float32)
    inverse = jnp.exp(indices * (-2.0 / feature.shape[-1]) * jnp.log(jnp.float32(10000.0)))
    angles = position[:, None, None] * inverse[None, None, :]
    cosine = jnp.cos(angles)
    sine_part = jnp.sin(angles)
    first_half = feature[..., :half_width]
    second_half = feature[..., half_width:]
    return jnp.concatenate(
        [
            first_half * cosine - second_half * sine_part,
            second_half * cosine + first_half * sine_part,
        ],
        axis=-1,
    )


def attend_kernel(
    live_ref, kpm_ref, kpe_ref, q_ref, mk_ref, mv_ref, ek_ref, ev_ref, nk_ref, nv_ref, out_ref
):
    block = pl.program_id(1)
    live = live_ref[0]
    main_span = mk_ref.shape[0] * mk_ref.shape[1]
    extra_span = ek_ref.shape[0] * ek_ref.shape[1]
    query = q_ref[...]
    contract = (((1,), (1,)), ((), ()))
    scale = HD ** (-0.5)

    def scores(keys):
        return lax.dot_general(query, keys, contract, preferred_element_type=jnp.float32) * scale

    main_scores = scores(mk_ref[...].reshape(main_span, HD))
    extra_scores = scores(ek_ref[...].reshape(extra_span, HD))
    new_scores = scores(nk_ref[...])
    main_ok = kpm_ref[...] < live
    extra_ok = kpe_ref[...] < live
    query_pos = block * BLOCK_Q + lax.broadcasted_iota(jnp.int32, new_scores.shape, 0)
    new_ok = lax.broadcasted_iota(jnp.int32, new_scores.shape, 1) <= query_pos
    main_scores = jnp.where(main_ok, main_scores, -1e30)
    extra_scores = jnp.where(extra_ok, extra_scores, -1e30)
    new_scores = jnp.where(new_ok, new_scores, -1e30)
    row_top = jnp.maximum(
        jnp.maximum(
            jnp.max(main_scores, axis=1, keepdims=True),
            jnp.max(extra_scores, axis=1, keepdims=True),
        ),
        jnp.max(new_scores, axis=1, keepdims=True),
    )
    main_w = jnp.where(main_ok, jnp.exp(main_scores - row_top), 0.0)
    extra_w = jnp.where(extra_ok, jnp.exp(extra_scores - row_top), 0.0)
    new_w = jnp.where(new_ok, jnp.exp(new_scores - row_top), 0.0)
    row_total = (
        jnp.sum(main_w, axis=1, keepdims=True)
        + jnp.sum(extra_w, axis=1, keepdims=True)
        + jnp.sum(new_w, axis=1, keepdims=True)
    )

    def weighted(weights, values):
        return jnp.dot(weights.astype(jnp.bfloat16), values, preferred_element_type=jnp.float32)

    summed = (
        weighted(main_w, mv_ref[...].reshape(main_span, HD))
        + weighted(extra_w, ev_ref[...].reshape(extra_span, HD))
        + weighted(new_w, nv_ref[...])
    )
    out_ref[...] = (summed / row_total).astype(out_ref.dtype)


def attend(live, query, main_pages, main_pos, extra_pages, extra_pos, new_key, new_value):
    rows, width = query.shape
    heads = width // HD
    main_n = main_pages.shape[0]
    extra_n = extra_pages.shape[0]
    grid_spec = pltpu.PrefetchScalarGridSpec(
        num_scalar_prefetch=1,
        grid=(heads, rows // BLOCK_Q),
        in_specs=[
            pl.BlockSpec((1, main_n * PAGE), lambda h, b, live: (0, 0)),
            pl.BlockSpec((1, extra_n * PAGE), lambda h, b, live: (0, 0)),
            pl.BlockSpec((BLOCK_Q, HD), lambda h, b, live: (b, h)),
            pl.BlockSpec((main_n, None, PAGE, HD), lambda h, b, live: (0, 0, 0, h)),
            pl.BlockSpec((main_n, None, PAGE, HD), lambda h, b, live: (0, 1, 0, h)),
            pl.BlockSpec((extra_n, None, PAGE, HD), lambda h, b, live: (0, 0, 0, h)),
            pl.BlockSpec((extra_n, None, PAGE, HD), lambda h, b, live: (0, 1, 0, h)),
            pl.BlockSpec((rows, HD), lambda h, b, live: (0, h)),
            pl.BlockSpec((rows, HD), lambda h, b, live: (0, h)),
        ],
        out_specs=pl.BlockSpec((BLOCK_Q, HD), lambda h, b, live: (b, h)),
    )
    keys_n = (main_n + extra_n) * PAGE + rows
    return pl.pallas_call(
        attend_kernel,
        grid_spec=grid_spec,
        out_shape=jax.ShapeDtypeStruct((rows, width), jnp.bfloat16),
        compiler_params=pltpu.CompilerParams(vmem_limit_bytes=56 * 1024 * 1024),
        cost_estimate=pl.CostEstimate(
            flops=4 * rows * keys_n * width,
            transcendentals=rows * keys_n * heads,
            bytes_accessed=2 * (2 * keys_n * width + 2 * rows * width),
        ),
    )(
        live,
        main_pos.reshape(1, -1),
        extra_pos.reshape(1, -1),
        query,
        main_pages,
        main_pages,
        extra_pages,
        extra_pages,
        new_key,
        new_value,
    )


def key_positions(entry_of_slot):
    tokens = jnp.arange(PAGE)[None, :]
    return jnp.where(entry_of_slot[:, None] >= 0, entry_of_slot[:, None] * PAGE + tokens, 1 << 30)


def project(hidden_in, qkv_weight, live_len, local_heads, local_width):
    token_rows = hidden_in.astype(jnp.float32)
    centre = jnp.mean(token_rows, axis=-1, keepdims=True)
    centred = token_rows - centre
    spread = jnp.mean(centred * centred, axis=-1, keepdims=True)
    normed = (centred * lax.rsqrt(spread + 1e-05)).astype(jnp.bfloat16)
    united_qkv = jnp.einsum("td,dcf->tcf", normed, qkv_weight, preferred_element_type=jnp.float32)
    positions = (live_len[:, None] + jnp.arange(NEW)[None, :]).astype(jnp.float32).reshape(-1)
    query_rot = rotate(united_qkv[:, 0].reshape(-1, local_heads, HD), positions).astype(
        jnp.bfloat16
    ).reshape(-1, local_width)
    new_key = rotate(united_qkv[:, 1].reshape(-1, local_heads, HD), positions).astype(
        jnp.bfloat16
    ).reshape(-1, local_width)
    new_value = united_qkv[:, 2].astype(jnp.bfloat16)
    return query_rot, new_key, new_value


def exchange_wide(kv_pool, page_slot, holder_rows, rank_all, req_index, req_count):
    capacity = 2
    held_here = holder_rows == req_index
    ranking = jnp.cumsum(held_here.astype(jnp.int32), axis=1) - 1
    picked = held_here[:, :, None] & (ranking[:, :, None] == jnp.arange(capacity)[None, None, :])
    send_slots = jnp.sum(jnp.where(picked, page_slot[:, :, None], 0), axis=1)
    incoming = lax.all_to_all(kv_pool[send_slots], "req", split_axis=0, concat_axis=0, tiled=True)
    incoming = incoming.reshape((req_count * capacity,) + kv_pool.shape[1:])
    own_holders = holder_rows[req_index]
    own_rank = rank_all[req_index]
    slot_of_entry = own_holders * capacity + own_rank
    hit = slot_of_entry[None, :] == jnp.arange(req_count * capacity)[:, None]
    entry_of_slot = jnp.max(jnp.where(hit, jnp.arange(hit.shape[1])[None, :], -1), axis=1)
    main_pos = key_positions(entry_of_slot)
    extra_pages = incoming[:1]
    extra_pos = key_positions(jnp.full((1,), -1, jnp.int32))
    return incoming, main_pos, extra_pages, extra_pos


def exchange_relay(kv_pool, page_slot, holder_rows, rank_all, req_index, req_count):
    rows, entries = holder_rows.shape
    spill = rank_all > 0
    frag = PAGE // req_count
    width = kv_pool.shape[-1]
    spill_flat = spill.reshape(-1)
    holders_flat = holder_rows.reshape(-1)
    slots_flat = page_slot.reshape(-1)
    spill_i = spill.astype(jnp.int32)
    named = (holder_rows[:, :, None] == jnp.arange(req_count)[None, None, :]).astype(jnp.int32)
    row_spills = jnp.sum(spill_i[:, :, None] * named, axis=1)
    before = jnp.cumsum(row_spills, axis=0) - row_spills
    holder_order = jnp.sum(named * before[:, None, :], axis=2).reshape(-1)
    req_order = jnp.cumsum(spill_i, axis=1) - spill_i
    first_hit = (holder_rows == req_index) & (rank_all == 0)
    send_slots = jnp.sum(jnp.where(first_hit, page_slot, 0), axis=1)
    wanted = jnp.arange(RELAY_A)
    match_a = (
        spill_flat[None, :]
        & (holders_flat[None, :] == req_index)
        & (holder_order[None, :] == wanted[:, None])
    )
    slot_a = jnp.sum(jnp.where(match_a, slots_flat[None, :], 0), axis=1)
    pieces = (
        kv_pool[slot_a]
        .reshape(RELAY_A, 2, req_count, frag, width)
        .transpose(2, 1, 0, 3, 4)
        .reshape(req_count, 2, RELAY_A * frag, width)
    )
    outgoing = jnp.concatenate([kv_pool[send_slots], pieces], axis=2)
    incoming = lax.all_to_all(outgoing, "req", split_axis=0, concat_axis=0, tiled=True)
    relayed = (
        incoming[:, :, PAGE:]
        .reshape(req_count, 2, RELAY_A, frag, width)
        .transpose(0, 2, 1, 3, 4)
        .reshape(req_count * RELAY_A, 2, frag, width)
    )
    match_b = spill[:, None, :] & (req_order[:, None, :] == jnp.arange(RELAY_B)[None, :, None])
    src_holder = jnp.sum(jnp.where(match_b, holder_rows[:, None, :], 0), axis=2)
    src_index = jnp.sum(
        jnp.where(match_b, holder_order.reshape(rows, entries)[:, None, :], 0), axis=2
    )
    extra = relayed[src_holder * RELAY_A + jnp.clip(src_index, 0, RELAY_A - 1)]
    extra = extra.transpose(0, 2, 1, 3, 4).reshape(rows, 2, RELAY_B * frag, width)
    returned = lax.all_to_all(extra, "req", split_axis=0, concat_axis=0, tiled=True)
    extra_pages = (
        returned.reshape(req_count, 2, RELAY_B, frag, width)
        .transpose(2, 1, 0, 3, 4)
        .reshape(RELAY_B, 2, PAGE, width)
    )
    own_holders = holder_rows[req_index]
    own_first = rank_all[req_index] == 0
    entry_ids = jnp.arange(entries)
    main_hit = own_first[None, :] & (own_holders[None, :] == jnp.arange(req_count)[:, None])
    main_pos = key_positions(jnp.max(jnp.where(main_hit, entry_ids[None, :], -1), axis=1))
    extra_hit = (~own_first)[None, :] & (
        req_order[req_index][None, :] == jnp.arange(RELAY_B)[:, None]
    )
    extra_pos = key_positions(jnp.max(jnp.where(extra_hit, entry_ids[None, :], -1), axis=1))
    return incoming, main_pos, extra_pages, extra_pos


def body(hidden_in, qkv_weight, out_weight, kv_pool, cached_len, page_slot, page_holder, cont_flag):
    req_count = lax.axis_size("req")
    req_index = lax.axis_index("req")
    local_width = qkv_weight.shape[2]
    local_heads = local_width // HD
    holder_rows = page_holder[:, :, 0]
    entries = holder_rows.shape[1]
    same_holder = holder_rows[:, :, None] == holder_rows[:, None, :]
    earlier = jnp.arange(entries)[None, None, :] < jnp.arange(entries)[None, :, None]
    rank_all = jnp.sum((same_holder & earlier).astype(jnp.int32), axis=2)
    spill = (rank_all > 0).astype(jnp.int32)
    relay_fits = (jnp.max(jnp.sum(spill, axis=1)) <= RELAY_B) & (
        jnp.max(jnp.sum(spill[:, :, None] * (holder_rows[:, :, None] == jnp.arange(req_count)), axis=(0, 1)))
        <= RELAY_A
    )
    lengths = lax.dynamic_slice_in_dim(cached_len, req_index, 1)
    flags = lax.dynamic_slice_in_dim(cont_flag, req_index, 1)
    live_len = lengths * flags
    operands = (hidden_in, qkv_weight, kv_pool, page_slot, holder_rows, rank_all, live_len)

    def branch(exchange):
        def run(ops):
            hidden, weight, pool, slots, holders, ranks, live = ops
            main_pages, main_pos, extra_pages, extra_pos = exchange(
                pool, slots, holders, ranks, req_index, req_count
            )
            query_rot, new_key, new_value = project(hidden, weight, live, local_heads, local_width)
            return attend(
                live, query_rot, main_pages, main_pos, extra_pages, extra_pos, new_key, new_value
            )

        return run

    attended = lax.cond(relay_fits, branch(exchange_relay), branch(exchange_wide), operands)
    head_term = jnp.dot(attended, out_weight, preferred_element_type=jnp.float32)
    return lax.psum_scatter(head_term.astype(jnp.bfloat16), "tp", scatter_dimension=0, tiled=True)


def solution(mesh):
    in_specs = (
        P("req", None),
        P(None, None, "tp"),
        P("tp", None),
        P("req", None, None, "tp"),
        P(),
        P(),
        P(),
        P(),
    )
    out_specs = P(("req", "tp"), None)
    return jax.shard_map(body, mesh=mesh, in_specs=in_specs, out_specs=out_specs, check_vma=False)
```

```python
import functools

import jax
import jax.numpy as jnp
from jax import lax
from jax.experimental import pallas as pl
from jax.experimental.pallas import tpu as pltpu
from jax.sharding import PartitionSpec as P

HD = 128
NEW = 1024
PAGE = 128
MAXP = 32
BLOCK_Q = 256
MESH = pl.DeviceIdType.MESH
RELAY_A = 8
RELAY_B = 1


def rotate(feature, position):
    half_width = feature.shape[-1] // 2
    indices = jnp.arange(half_width).astype(jnp.float32)
    inverse = jnp.exp(indices * (-2.0 / feature.shape[-1]) * jnp.log(jnp.float32(10000.0)))
    angles = position[:, None, None] * inverse[None, None, :]
    cosine = jnp.cos(angles)
    sine_part = jnp.sin(angles)
    first_half = feature[..., :half_width]
    second_half = feature[..., half_width:]
    return jnp.concatenate(
        [
            first_half * cosine - second_half * sine_part,
            second_half * cosine + first_half * sine_part,
        ],
        axis=-1,
    )


def attend_kernel(
    live_ref, kpm_ref, kpe_ref, q_ref, mk_ref, mv_ref, ek_ref, ev_ref, nk_ref, nv_ref, out_ref
):
    block = pl.program_id(1)
    live = live_ref[0]
    main_span = mk_ref.shape[0] * mk_ref.shape[1]
    extra_span = ek_ref.shape[0] * ek_ref.shape[1]
    query = q_ref[...]
    contract = (((1,), (1,)), ((), ()))
    scale = HD ** (-0.5)

    def scores(keys):
        return lax.dot_general(query, keys, contract, preferred_element_type=jnp.float32) * scale

    main_scores = scores(mk_ref[...].reshape(main_span, HD))
    extra_scores = scores(ek_ref[...].reshape(extra_span, HD))
    new_scores = scores(nk_ref[...])
    main_ok = kpm_ref[...] < live
    extra_ok = kpe_ref[...] < live
    query_pos = block * BLOCK_Q + lax.broadcasted_iota(jnp.int32, new_scores.shape, 0)
    new_ok = lax.broadcasted_iota(jnp.int32, new_scores.shape, 1) <= query_pos
    main_scores = jnp.where(main_ok, main_scores, -1e30)
    extra_scores = jnp.where(extra_ok, extra_scores, -1e30)
    new_scores = jnp.where(new_ok, new_scores, -1e30)
    row_top = jnp.maximum(
        jnp.maximum(
            jnp.max(main_scores, axis=1, keepdims=True),
            jnp.max(extra_scores, axis=1, keepdims=True),
        ),
        jnp.max(new_scores, axis=1, keepdims=True),
    )
    main_w = jnp.exp(main_scores - row_top)
    extra_w = jnp.exp(extra_scores - row_top)
    new_w = jnp.exp(new_scores - row_top)
    row_total = (
        jnp.sum(main_w, axis=1, keepdims=True)
        + jnp.sum(extra_w, axis=1, keepdims=True)
        + jnp.sum(new_w, axis=1, keepdims=True)
    )

    def weighted(weights, values):
        return jnp.dot(weights.astype(jnp.bfloat16), values, preferred_element_type=jnp.float32)

    summed = (
        weighted(main_w, mv_ref[...].reshape(main_span, HD))
        + weighted(extra_w, ev_ref[...].reshape(extra_span, HD))
        + weighted(new_w, nv_ref[...])
    )
    out_ref[...] = (summed / row_total).astype(out_ref.dtype)


def attend(live, query, main_pages, main_pos, extra_pages, extra_pos, new_key, new_value):
    rows, width = query.shape
    heads = width // HD
    main_n = main_pages.shape[0]
    extra_n = extra_pages.shape[0]
    grid_spec = pltpu.PrefetchScalarGridSpec(
        num_scalar_prefetch=1,
        grid=(heads, rows // BLOCK_Q),
        in_specs=[
            pl.BlockSpec((1, main_n * PAGE), lambda h, b, live: (0, 0)),
            pl.BlockSpec((1, extra_n * PAGE), lambda h, b, live: (0, 0)),
            pl.BlockSpec((BLOCK_Q, HD), lambda h, b, live: (b, h)),
            pl.BlockSpec((main_n, None, PAGE, HD), lambda h, b, live: (0, 0, 0, h)),
            pl.BlockSpec((main_n, None, PAGE, HD), lambda h, b, live: (0, 1, 0, h)),
            pl.BlockSpec((extra_n, None, PAGE, HD), lambda h, b, live: (0, 0, 0, h)),
            pl.BlockSpec((extra_n, None, PAGE, HD), lambda h, b, live: (0, 1, 0, h)),
            pl.BlockSpec((rows, HD), lambda h, b, live: (0, h)),
            pl.BlockSpec((rows, HD), lambda h, b, live: (0, h)),
        ],
        out_specs=pl.BlockSpec((BLOCK_Q, HD), lambda h, b, live: (b, h)),
    )
    keys_n = (main_n + extra_n) * PAGE + rows
    return pl.pallas_call(
        attend_kernel,
        grid_spec=grid_spec,
        out_shape=jax.ShapeDtypeStruct((rows, width), jnp.bfloat16),
        compiler_params=pltpu.CompilerParams(vmem_limit_bytes=56 * 1024 * 1024),
        cost_estimate=pl.CostEstimate(
            flops=4 * rows * keys_n * width,
            transcendentals=rows * keys_n * heads,
            bytes_accessed=2 * (2 * keys_n * width + 2 * rows * width),
        ),
    )(
        live,
        main_pos.reshape(1, -1),
        extra_pos.reshape(1, -1),
        query,
        main_pages,
        main_pages,
        extra_pages,
        extra_pages,
        new_key,
        new_value,
    )


def swap_kernel(send_ref, recv_ref, send_sems, recv_sems):
    count = send_ref.shape[0]
    me = lax.axis_index("req")
    tp_me = lax.axis_index("tp")
    barrier = pltpu.get_barrier_semaphore()

    def others(fn):
        def step(peer, carry):
            @pl.when(peer != me)
            def _():
                fn(peer)

            return carry

        lax.fori_loop(0, count, step, 0)

    def greet(peer):
        pl.semaphore_signal(barrier, inc=1, device_id=(peer, tp_me), device_id_type=MESH)

    others(greet)
    pl.semaphore_wait(barrier, count - 1)

    def outgoing(peer):
        return pltpu.make_async_remote_copy(
            src_ref=send_ref.at[peer],
            dst_ref=recv_ref.at[me],
            send_sem=send_sems.at[peer],
            recv_sem=recv_sems.at[me],
            device_id=(peer, tp_me),
            device_id_type=MESH,
        )

    def arriving(peer):
        return pltpu.make_async_remote_copy(
            src_ref=send_ref.at[peer],
            dst_ref=recv_ref.at[peer],
            send_sem=send_sems.at[peer],
            recv_sem=recv_sems.at[peer],
            device_id=(peer, tp_me),
            device_id_type=MESH,
        )

    others(lambda peer: outgoing(peer).start())
    recv_ref[pl.ds(me, 1)] = send_ref[pl.ds(me, 1)]
    others(lambda peer: outgoing(peer).wait_send())
    others(lambda peer: arriving(peer).wait_recv())


def swap_pieces(pieces):
    count = pieces.shape[0]
    return pl.pallas_call(
        swap_kernel,
        out_shape=jax.ShapeDtypeStruct(pieces.shape, pieces.dtype),
        in_specs=[pl.BlockSpec(memory_space=pltpu.VMEM)],
        out_specs=pl.BlockSpec(memory_space=pltpu.VMEM),
        scratch_shapes=[pltpu.SemaphoreType.DMA((count,)), pltpu.SemaphoreType.DMA((count,))],
        compiler_params=pltpu.CompilerParams(collective_id=0, has_side_effects=True),
    )(pieces)


def key_positions(entry_of_slot):
    tokens = jnp.arange(PAGE)[None, :]
    return jnp.where(entry_of_slot[:, None] >= 0, entry_of_slot[:, None] * PAGE + tokens, 1 << 30)


def project(hidden_in, qkv_weight, live_len, local_heads, local_width):
    token_rows = hidden_in.astype(jnp.float32)
    centre = jnp.mean(token_rows, axis=-1, keepdims=True)
    centred = token_rows - centre
    spread = jnp.mean(centred * centred, axis=-1, keepdims=True)
    normed = (centred * lax.rsqrt(spread + 1e-05)).astype(jnp.bfloat16)
    united_qkv = jnp.einsum("td,dcf->tcf", normed, qkv_weight, preferred_element_type=jnp.float32)
    positions = (live_len[:, None] + jnp.arange(NEW)[None, :]).astype(jnp.float32).reshape(-1)
    query_rot = rotate(united_qkv[:, 0].reshape(-1, local_heads, HD), positions).astype(
        jnp.bfloat16
    ).reshape(-1, local_width)
    new_key = rotate(united_qkv[:, 1].reshape(-1, local_heads, HD), positions).astype(
        jnp.bfloat16
    ).reshape(-1, local_width)
    new_value = united_qkv[:, 2].astype(jnp.bfloat16)
    return query_rot, new_key, new_value


def exchange_wide(kv_pool, page_slot, holder_rows, rank_all, req_index, req_count):
    capacity = 2
    held_here = holder_rows == req_index
    ranking = jnp.cumsum(held_here.astype(jnp.int32), axis=1) - 1
    picked = held_here[:, :, None] & (ranking[:, :, None] == jnp.arange(capacity)[None, None, :])
    send_slots = jnp.sum(jnp.where(picked, page_slot[:, :, None], 0), axis=1)
    incoming = lax.all_to_all(kv_pool[send_slots], "req", split_axis=0, concat_axis=0, tiled=True)
    incoming = incoming.reshape((req_count * capacity,) + kv_pool.shape[1:])
    own_holders = holder_rows[req_index]
    own_rank = rank_all[req_index]
    slot_of_entry = own_holders * capacity + own_rank
    hit = slot_of_entry[None, :] == jnp.arange(req_count * capacity)[:, None]
    entry_of_slot = jnp.max(jnp.where(hit, jnp.arange(hit.shape[1])[None, :], -1), axis=1)
    main_pos = key_positions(entry_of_slot)
    extra_pages = incoming[:1]
    extra_pos = key_positions(jnp.full((1,), -1, jnp.int32))
    return incoming, main_pos, extra_pages, extra_pos


def exchange_relay(kv_pool, page_slot, holder_rows, rank_all, req_index, req_count):
    rows, entries = holder_rows.shape
    spill = rank_all > 0
    frag = PAGE // req_count
    width = kv_pool.shape[-1]
    spill_flat = spill.reshape(-1)
    holders_flat = holder_rows.reshape(-1)
    slots_flat = page_slot.reshape(-1)
    spill_i = spill.astype(jnp.int32)
    named = (holder_rows[:, :, None] == jnp.arange(req_count)[None, None, :]).astype(jnp.int32)
    row_spills = jnp.sum(spill_i[:, :, None] * named, axis=1)
    before = jnp.cumsum(row_spills, axis=0) - row_spills
    holder_order = jnp.sum(named * before[:, None, :], axis=2).reshape(-1)
    req_order = jnp.cumsum(spill_i, axis=1) - spill_i
    first_hit = (holder_rows == req_index) & (rank_all == 0)
    send_slots = jnp.sum(jnp.where(first_hit, page_slot, 0), axis=1)
    wanted = jnp.arange(RELAY_A)
    match_a = (
        spill_flat[None, :]
        & (holders_flat[None, :] == req_index)
        & (holder_order[None, :] == wanted[:, None])
    )
    slot_a = jnp.sum(jnp.where(match_a, slots_flat[None, :], 0), axis=1)
    pieces = (
        kv_pool[slot_a]
        .reshape(RELAY_A, 2, req_count, frag, width)
        .transpose(2, 1, 0, 3, 4)
        .reshape(req_count, 2, RELAY_A * frag, width)
    )
    outgoing = jnp.concatenate([kv_pool[send_slots], pieces], axis=2)
    incoming = lax.all_to_all(outgoing, "req", split_axis=0, concat_axis=0, tiled=True)
    relayed = (
        incoming[:, :, PAGE:]
        .reshape(req_count, 2, RELAY_A, frag, width)
        .transpose(0, 2, 1, 3, 4)
        .reshape(req_count * RELAY_A, 2, frag, width)
    )
    match_b = spill[:, None, :] & (req_order[:, None, :] == jnp.arange(RELAY_B)[None, :, None])
    src_holder = jnp.sum(jnp.where(match_b, holder_rows[:, None, :], 0), axis=2)
    src_index = jnp.sum(
        jnp.where(match_b, holder_order.reshape(rows, entries)[:, None, :], 0), axis=2
    )
    extra = relayed[src_holder * RELAY_A + jnp.clip(src_index, 0, RELAY_A - 1)]
    extra = extra.transpose(0, 2, 1, 3, 4).reshape(rows, 2, RELAY_B * frag, width)
    returned = swap_pieces(extra)
    extra_pages = (
        returned.reshape(req_count, 2, RELAY_B, frag, width)
        .transpose(2, 1, 0, 3, 4)
        .reshape(RELAY_B, 2, PAGE, width)
    )
    own_holders = holder_rows[req_index]
    own_first = rank_all[req_index] == 0
    entry_ids = jnp.arange(entries)
    main_hit = own_first[None, :] & (own_holders[None, :] == jnp.arange(req_count)[:, None])
    main_pos = key_positions(jnp.max(jnp.where(main_hit, entry_ids[None, :], -1), axis=1))
    extra_hit = (~own_first)[None, :] & (
        req_order[req_index][None, :] == jnp.arange(RELAY_B)[:, None]
    )
    extra_pos = key_positions(jnp.max(jnp.where(extra_hit, entry_ids[None, :], -1), axis=1))
    return incoming, main_pos, extra_pages, extra_pos


def body(hidden_in, qkv_weight, out_weight, kv_pool, cached_len, page_slot, page_holder, cont_flag):
    req_count = lax.axis_size("req")
    req_index = lax.axis_index("req")
    local_width = qkv_weight.shape[2]
    local_heads = local_width // HD
    holder_rows = page_holder[:, :, 0]
    entries = holder_rows.shape[1]
    same_holder = holder_rows[:, :, None] == holder_rows[:, None, :]
    earlier = jnp.arange(entries)[None, None, :] < jnp.arange(entries)[None, :, None]
    rank_all = jnp.sum((same_holder & earlier).astype(jnp.int32), axis=2)
    spill = (rank_all > 0).astype(jnp.int32)
    relay_fits = (jnp.max(jnp.sum(spill, axis=1)) <= RELAY_B) & (
        jnp.max(jnp.sum(spill[:, :, None] * (holder_rows[:, :, None] == jnp.arange(req_count)), axis=(0, 1)))
        <= RELAY_A
    )
    lengths = lax.dynamic_slice_in_dim(cached_len, req_index, 1)
    flags = lax.dynamic_slice_in_dim(cont_flag, req_index, 1)
    live_len = lengths * flags
    operands = (hidden_in, qkv_weight, kv_pool, page_slot, holder_rows, rank_all, live_len)

    def branch(exchange):
        def run(ops):
            hidden, weight, pool, slots, holders, ranks, live = ops
            main_pages, main_pos, extra_pages, extra_pos = exchange(
                pool, slots, holders, ranks, req_index, req_count
            )
            query_rot, new_key, new_value = project(hidden, weight, live, local_heads, local_width)
            return attend(
                live, query_rot, main_pages, main_pos, extra_pages, extra_pos, new_key, new_value
            )

        return run

    attended = lax.cond(relay_fits, branch(exchange_relay), branch(exchange_wide), operands)
    head_term = jnp.dot(attended, out_weight, preferred_element_type=jnp.float32)
    return lax.psum_scatter(head_term.astype(jnp.bfloat16), "tp", scatter_dimension=0, tiled=True)


def solution(mesh):
    in_specs = (
        P("req", None),
        P(None, None, "tp"),
        P("tp", None),
        P("req", None, None, "tp"),
        P(),
        P(),
        P(),
        P(),
    )
    out_specs = P(("req", "tp"), None)
    return jax.shard_map(body, mesh=mesh, in_specs=in_specs, out_specs=out_specs, check_vma=False)
```

```python
import functools

import jax
import jax.numpy as jnp
from jax import lax
from jax.experimental import pallas as pl
from jax.experimental.pallas import tpu as pltpu
from jax.sharding import PartitionSpec as P

HD = 128
NEW = 1024
PAGE = 128
MAXP = 32
BLOCK_Q = 256
CHUNKS = 4
MESH = pl.DeviceIdType.MESH
RELAY_A = 8
RELAY_B = 1


def rotate(feature, position):
    half_width = feature.shape[-1] // 2
    indices = jnp.arange(half_width).astype(jnp.float32)
    inverse = jnp.exp(indices * (-2.0 / feature.shape[-1]) * jnp.log(jnp.float32(10000.0)))
    angles = position[:, None, None] * inverse[None, None, :]
    cosine = jnp.cos(angles)
    sine_part = jnp.sin(angles)
    first_half = feature[..., :half_width]
    second_half = feature[..., half_width:]
    return jnp.concatenate(
        [
            first_half * cosine - second_half * sine_part,
            second_half * cosine + first_half * sine_part,
        ],
        axis=-1,
    )


def attend_kernel(
    live_ref, qp_ref, kpm_ref, kpe_ref, q_ref, mk_ref, mv_ref, ek_ref, ev_ref, nk_ref, nv_ref, out_ref
):
    live = live_ref[0]
    main_span = mk_ref.shape[0] * mk_ref.shape[1]
    extra_span = ek_ref.shape[0] * ek_ref.shape[1]
    query = q_ref[...]
    contract = (((1,), (1,)), ((), ()))
    scale = HD ** (-0.5)

    def scores(keys):
        return lax.dot_general(query, keys, contract, preferred_element_type=jnp.float32) * scale

    main_scores = scores(mk_ref[...].reshape(main_span, HD))
    extra_scores = scores(ek_ref[...].reshape(extra_span, HD))
    new_scores = scores(nk_ref[...])
    main_ok = kpm_ref[...] < live
    extra_ok = kpe_ref[...] < live
    new_ok = lax.broadcasted_iota(jnp.int32, new_scores.shape, 1) <= qp_ref[...]
    main_scores = jnp.where(main_ok, main_scores, -1e30)
    extra_scores = jnp.where(extra_ok, extra_scores, -1e30)
    new_scores = jnp.where(new_ok, new_scores, -1e30)
    row_top = jnp.maximum(
        jnp.maximum(
            jnp.max(main_scores, axis=1, keepdims=True),
            jnp.max(extra_scores, axis=1, keepdims=True),
        ),
        jnp.max(new_scores, axis=1, keepdims=True),
    )
    main_w = jnp.exp(main_scores - row_top)
    extra_w = jnp.exp(extra_scores - row_top)
    new_w = jnp.exp(new_scores - row_top)
    row_total = (
        jnp.sum(main_w, axis=1, keepdims=True)
        + jnp.sum(extra_w, axis=1, keepdims=True)
        + jnp.sum(new_w, axis=1, keepdims=True)
    )

    def weighted(weights, values):
        return jnp.dot(weights.astype(jnp.bfloat16), values, preferred_element_type=jnp.float32)

    summed = (
        weighted(main_w, mv_ref[...].reshape(main_span, HD))
        + weighted(extra_w, ev_ref[...].reshape(extra_span, HD))
        + weighted(new_w, nv_ref[...])
    )
    out_ref[...] = (summed / row_total).astype(out_ref.dtype)


def attend(live, query_pos, query, main_pages, main_pos, extra_pages, extra_pos, new_key, new_value):
    rows, width = query.shape
    keys_new = new_key.shape[0]
    heads = width // HD
    main_n = main_pages.shape[0]
    extra_n = extra_pages.shape[0]
    grid_spec = pltpu.PrefetchScalarGridSpec(
        num_scalar_prefetch=1,
        grid=(heads, rows // BLOCK_Q),
        in_specs=[
            pl.BlockSpec((BLOCK_Q, 1), lambda h, b, live: (b, 0)),
            pl.BlockSpec((1, main_n * PAGE), lambda h, b, live: (0, 0)),
            pl.BlockSpec((1, extra_n * PAGE), lambda h, b, live: (0, 0)),
            pl.BlockSpec((BLOCK_Q, HD), lambda h, b, live: (b, h)),
            pl.BlockSpec((main_n, None, PAGE, HD), lambda h, b, live: (0, 0, 0, h)),
            pl.BlockSpec((main_n, None, PAGE, HD), lambda h, b, live: (0, 1, 0, h)),
            pl.BlockSpec((extra_n, None, PAGE, HD), lambda h, b, live: (0, 0, 0, h)),
            pl.BlockSpec((extra_n, None, PAGE, HD), lambda h, b, live: (0, 1, 0, h)),
            pl.BlockSpec((keys_new, HD), lambda h, b, live: (0, h)),
            pl.BlockSpec((keys_new, HD), lambda h, b, live: (0, h)),
        ],
        out_specs=pl.BlockSpec((BLOCK_Q, HD), lambda h, b, live: (b, h)),
    )
    keys_n = (main_n + extra_n) * PAGE + keys_new
    return pl.pallas_call(
        attend_kernel,
        grid_spec=grid_spec,
        out_shape=jax.ShapeDtypeStruct((rows, width), jnp.bfloat16),
        compiler_params=pltpu.CompilerParams(vmem_limit_bytes=56 * 1024 * 1024),
        cost_estimate=pl.CostEstimate(
            flops=4 * rows * keys_n * width,
            transcendentals=rows * keys_n * heads,
            bytes_accessed=2 * (2 * keys_n * width + 2 * rows * width),
        ),
    )(
        live,
        query_pos.reshape(-1, 1),
        main_pos.reshape(1, -1),
        extra_pos.reshape(1, -1),
        query,
        main_pages,
        main_pages,
        extra_pages,
        extra_pages,
        new_key,
        new_value,
    )


def swap_kernel(send_ref, recv_ref, send_sems, recv_sems):
    count = send_ref.shape[0]
    me = lax.axis_index("req")
    tp_me = lax.axis_index("tp")
    barrier = pltpu.get_barrier_semaphore()

    def others(fn):
        def step(peer, carry):
            @pl.when(peer != me)
            def _():
                fn(peer)

            return carry

        lax.fori_loop(0, count, step, 0)

    def greet(peer):
        pl.semaphore_signal(barrier, inc=1, device_id=(peer, tp_me), device_id_type=MESH)

    others(greet)
    pl.semaphore_wait(barrier, count - 1)

    def outgoing(peer):
        return pltpu.make_async_remote_copy(
            src_ref=send_ref.at[peer],
            dst_ref=recv_ref.at[me],
            send_sem=send_sems.at[peer],
            recv_sem=recv_sems.at[me],
            device_id=(peer, tp_me),
            device_id_type=MESH,
        )

    def arriving(peer):
        return pltpu.make_async_remote_copy(
            src_ref=send_ref.at[peer],
            dst_ref=recv_ref.at[peer],
            send_sem=send_sems.at[peer],
            recv_sem=recv_sems.at[peer],
            device_id=(peer, tp_me),
            device_id_type=MESH,
        )

    others(lambda peer: outgoing(peer).start())
    recv_ref[pl.ds(me, 1)] = send_ref[pl.ds(me, 1)]
    others(lambda peer: outgoing(peer).wait_send())
    others(lambda peer: arriving(peer).wait_recv())


def swap_pieces(pieces):
    count = pieces.shape[0]
    return pl.pallas_call(
        swap_kernel,
        out_shape=jax.ShapeDtypeStruct(pieces.shape, pieces.dtype),
        in_specs=[pl.BlockSpec(memory_space=pltpu.VMEM)],
        out_specs=pl.BlockSpec(memory_space=pltpu.VMEM),
        scratch_shapes=[pltpu.SemaphoreType.DMA((count,)), pltpu.SemaphoreType.DMA((count,))],
        compiler_params=pltpu.CompilerParams(collective_id=0, has_side_effects=True),
    )(pieces)


def key_positions(entry_of_slot):
    tokens = jnp.arange(PAGE)[None, :]
    return jnp.where(entry_of_slot[:, None] >= 0, entry_of_slot[:, None] * PAGE + tokens, 1 << 30)


def project(hidden_in, qkv_weight, live_len, local_heads, local_width):
    token_rows = hidden_in.astype(jnp.float32)
    centre = jnp.mean(token_rows, axis=-1, keepdims=True)
    centred = token_rows - centre
    spread = jnp.mean(centred * centred, axis=-1, keepdims=True)
    normed = (centred * lax.rsqrt(spread + 1e-05)).astype(jnp.bfloat16)
    united_qkv = jnp.einsum("td,dcf->tcf", normed, qkv_weight, preferred_element_type=jnp.float32)
    positions = (live_len[:, None] + jnp.arange(NEW)[None, :]).astype(jnp.float32).reshape(-1)
    query_rot = rotate(united_qkv[:, 0].reshape(-1, local_heads, HD), positions).astype(
        jnp.bfloat16
    ).reshape(-1, local_width)
    new_key = rotate(united_qkv[:, 1].reshape(-1, local_heads, HD), positions).astype(
        jnp.bfloat16
    ).reshape(-1, local_width)
    new_value = united_qkv[:, 2].astype(jnp.bfloat16)
    return query_rot, new_key, new_value


def exchange_wide(kv_pool, page_slot, holder_rows, rank_all, req_index, req_count):
    capacity = 2
    held_here = holder_rows == req_index
    ranking = jnp.cumsum(held_here.astype(jnp.int32), axis=1) - 1
    picked = held_here[:, :, None] & (ranking[:, :, None] == jnp.arange(capacity)[None, None, :])
    send_slots = jnp.sum(jnp.where(picked, page_slot[:, :, None], 0), axis=1)
    incoming = lax.all_to_all(kv_pool[send_slots], "req", split_axis=0, concat_axis=0, tiled=True)
    incoming = incoming.reshape((req_count * capacity,) + kv_pool.shape[1:])
    own_holders = holder_rows[req_index]
    own_rank = rank_all[req_index]
    slot_of_entry = own_holders * capacity + own_rank
    hit = slot_of_entry[None, :] == jnp.arange(req_count * capacity)[:, None]
    entry_of_slot = jnp.max(jnp.where(hit, jnp.arange(hit.shape[1])[None, :], -1), axis=1)
    main_pos = key_positions(entry_of_slot)
    extra_pages = incoming[:1]
    extra_pos = key_positions(jnp.full((1,), -1, jnp.int32))
    return incoming, main_pos, extra_pages, extra_pos


def exchange_relay(kv_pool, page_slot, holder_rows, rank_all, req_index, req_count):
    rows, entries = holder_rows.shape
    spill = rank_all > 0
    frag = PAGE // req_count
    width = kv_pool.shape[-1]
    spill_flat = spill.reshape(-1)
    holders_flat = holder_rows.reshape(-1)
    slots_flat = page_slot.reshape(-1)
    spill_i = spill.astype(jnp.int32)
    named = (holder_rows[:, :, None] == jnp.arange(req_count)[None, None, :]).astype(jnp.int32)
    row_spills = jnp.sum(spill_i[:, :, None] * named, axis=1)
    before = jnp.cumsum(row_spills, axis=0) - row_spills
    holder_order = jnp.sum(named * before[:, None, :], axis=2).reshape(-1)
    req_order = jnp.cumsum(spill_i, axis=1) - spill_i
    first_hit = (holder_rows == req_index) & (rank_all == 0)
    send_slots = jnp.sum(jnp.where(first_hit, page_slot, 0), axis=1)
    wanted = jnp.arange(RELAY_A)
    match_a = (
        spill_flat[None, :]
        & (holders_flat[None, :] == req_index)
        & (holder_order[None, :] == wanted[:, None])
    )
    slot_a = jnp.sum(jnp.where(match_a, slots_flat[None, :], 0), axis=1)
    pieces = (
        kv_pool[slot_a]
        .reshape(RELAY_A, 2, req_count, frag, width)
        .transpose(2, 1, 0, 3, 4)
        .reshape(req_count, 2, RELAY_A * frag, width)
    )
    outgoing = jnp.concatenate([kv_pool[send_slots], pieces], axis=2)
    incoming = lax.all_to_all(outgoing, "req", split_axis=0, concat_axis=0, tiled=True)
    relayed = (
        incoming[:, :, PAGE:]
        .reshape(req_count, 2, RELAY_A, frag, width)
        .transpose(0, 2, 1, 3, 4)
        .reshape(req_count * RELAY_A, 2, frag, width)
    )
    match_b = spill[:, None, :] & (req_order[:, None, :] == jnp.arange(RELAY_B)[None, :, None])
    src_holder = jnp.sum(jnp.where(match_b, holder_rows[:, None, :], 0), axis=2)
    src_index = jnp.sum(
        jnp.where(match_b, holder_order.reshape(rows, entries)[:, None, :], 0), axis=2
    )
    extra = relayed[src_holder * RELAY_A + jnp.clip(src_index, 0, RELAY_A - 1)]
    extra = extra.transpose(0, 2, 1, 3, 4).reshape(rows, 2, RELAY_B * frag, width)
    returned = swap_pieces(extra)
    extra_pages = (
        returned.reshape(req_count, 2, RELAY_B, frag, width)
        .transpose(2, 1, 0, 3, 4)
        .reshape(RELAY_B, 2, PAGE, width)
    )
    own_holders = holder_rows[req_index]
    own_first = rank_all[req_index] == 0
    entry_ids = jnp.arange(entries)
    main_hit = own_first[None, :] & (own_holders[None, :] == jnp.arange(req_count)[:, None])
    main_pos = key_positions(jnp.max(jnp.where(main_hit, entry_ids[None, :], -1), axis=1))
    extra_hit = (~own_first)[None, :] & (
        req_order[req_index][None, :] == jnp.arange(RELAY_B)[:, None]
    )
    extra_pos = key_positions(jnp.max(jnp.where(extra_hit, entry_ids[None, :], -1), axis=1))
    return incoming, main_pos, extra_pages, extra_pos


def body(hidden_in, qkv_weight, out_weight, kv_pool, cached_len, page_slot, page_holder, cont_flag):
    req_count = lax.axis_size("req")
    req_index = lax.axis_index("req")
    local_width = qkv_weight.shape[2]
    local_heads = local_width // HD
    holder_rows = page_holder[:, :, 0]
    entries = holder_rows.shape[1]
    same_holder = holder_rows[:, :, None] == holder_rows[:, None, :]
    earlier = jnp.arange(entries)[None, None, :] < jnp.arange(entries)[None, :, None]
    rank_all = jnp.sum((same_holder & earlier).astype(jnp.int32), axis=2)
    spill = (rank_all > 0).astype(jnp.int32)
    relay_fits = (jnp.max(jnp.sum(spill, axis=1)) <= RELAY_B) & (
        jnp.max(jnp.sum(spill[:, :, None] * (holder_rows[:, :, None] == jnp.arange(req_count)), axis=(0, 1)))
        <= RELAY_A
    )
    lengths = lax.dynamic_slice_in_dim(cached_len, req_index, 1)
    flags = lax.dynamic_slice_in_dim(cont_flag, req_index, 1)
    live_len = lengths * flags
    tp_count = lax.axis_size("tp")
    operands = (hidden_in, qkv_weight, out_weight, kv_pool, page_slot, holder_rows, rank_all, live_len)

    def finish(attended, weight_out):
        head_term = jnp.dot(attended, weight_out, preferred_element_type=jnp.float32)
        return lax.psum_scatter(
            head_term.astype(jnp.bfloat16), "tp", scatter_dimension=0, tiled=True
        )

    def branch(exchange, chunks):
        def run(ops):
            hidden, weight, weight_out, pool, slots, holders, ranks, live = ops
            main_pages, main_pos, extra_pages, extra_pos = exchange(
                pool, slots, holders, ranks, req_index, req_count
            )
            query_rot, new_key, new_value = project(hidden, weight, live, local_heads, local_width)
            rows = query_rot.shape[0]
            share = rows // tp_count // chunks
            order = (
                jnp.arange(rows).reshape(tp_count, chunks, share).transpose(1, 0, 2).reshape(-1)
            )
            query_perm = query_rot[order]
            step = rows // chunks
            parts = []
            for chunk in range(chunks):
                part = attend(
                    live,
                    order[chunk * step : (chunk + 1) * step],
                    query_perm[chunk * step : (chunk + 1) * step],
                    main_pages,
                    main_pos,
                    extra_pages,
                    extra_pos,
                    new_key,
                    new_value,
                )
                parts.append(finish(part, weight_out))
            return jnp.concatenate(parts, axis=0)

        return run

    return lax.cond(
        relay_fits, branch(exchange_relay, CHUNKS), branch(exchange_wide, 1), operands
    )


def solution(mesh):
    in_specs = (
        P("req", None),
        P(None, None, "tp"),
        P("tp", None),
        P("req", None, None, "tp"),
        P(),
        P(),
        P(),
        P(),
    )
    out_specs = P(("req", "tp"), None)
    return jax.shard_map(body, mesh=mesh, in_specs=in_specs, out_specs=out_specs, check_vma=False)
```

```python
import functools

import jax
import jax.numpy as jnp
from jax import lax
from jax.experimental import pallas as pl
from jax.experimental.pallas import tpu as pltpu
from jax.sharding import PartitionSpec as P

HD = 128
NEW = 1024
PAGE = 128
MAXP = 32
BLOCK_Q = 256
MESH = pl.DeviceIdType.MESH
RELAY_A = 8
RELAY_B = 1


def rotate(feature, position):
    half_width = feature.shape[-1] // 2
    indices = jnp.arange(half_width).astype(jnp.float32)
    inverse = jnp.exp(indices * (-2.0 / feature.shape[-1]) * jnp.log(jnp.float32(10000.0)))
    angles = position[:, None, None] * inverse[None, None, :]
    cosine = jnp.cos(angles)
    sine_part = jnp.sin(angles)
    first_half = feature[..., :half_width]
    second_half = feature[..., half_width:]
    return jnp.concatenate(
        [
            first_half * cosine - second_half * sine_part,
            second_half * cosine + first_half * sine_part,
        ],
        axis=-1,
    )


def attend_kernel(
    live_ref, kpm_ref, kpe_ref, q_ref, mk_ref, mv_ref, ek_ref, ev_ref, nk_ref, nv_ref, out_ref
):
    block = pl.program_id(1)
    live = live_ref[0]
    main_span = mk_ref.shape[0] * mk_ref.shape[1]
    extra_span = ek_ref.shape[0] * ek_ref.shape[1]
    query = q_ref[...]
    contract = (((1,), (1,)), ((), ()))
    scale = HD ** (-0.5)

    def scores(keys):
        return lax.dot_general(query, keys, contract, preferred_element_type=jnp.float32) * scale

    main_scores = scores(mk_ref[...].reshape(main_span, HD))
    extra_scores = scores(ek_ref[...].reshape(extra_span, HD))
    new_scores = scores(nk_ref[...])
    main_ok = kpm_ref[...] < live
    extra_ok = kpe_ref[...] < live
    query_pos = block * BLOCK_Q + lax.broadcasted_iota(jnp.int32, new_scores.shape, 0)
    new_ok = lax.broadcasted_iota(jnp.int32, new_scores.shape, 1) <= query_pos
    main_scores = jnp.where(main_ok, main_scores, -1e30)
    extra_scores = jnp.where(extra_ok, extra_scores, -1e30)
    new_scores = jnp.where(new_ok, new_scores, -1e30)
    row_top = jnp.maximum(
        jnp.maximum(
            jnp.max(main_scores, axis=1, keepdims=True),
            jnp.max(extra_scores, axis=1, keepdims=True),
        ),
        jnp.max(new_scores, axis=1, keepdims=True),
    )
    main_w = jnp.exp(main_scores - row_top)
    extra_w = jnp.exp(extra_scores - row_top)
    new_w = jnp.exp(new_scores - row_top)
    row_total = (
        jnp.sum(main_w, axis=1, keepdims=True)
        + jnp.sum(extra_w, axis=1, keepdims=True)
        + jnp.sum(new_w, axis=1, keepdims=True)
    )

    def weighted(weights, values):
        return jnp.dot(weights.astype(jnp.bfloat16), values, preferred_element_type=jnp.float32)

    summed = (
        weighted(main_w, mv_ref[...].reshape(main_span, HD))
        + weighted(extra_w, ev_ref[...].reshape(extra_span, HD))
        + weighted(new_w, nv_ref[...])
    )
    out_ref[...] = (summed / row_total).astype(out_ref.dtype)


def attend(live, query, main_pages, main_pos, extra_pages, extra_pos, new_key, new_value):
    rows, width = query.shape
    heads = width // HD
    main_n = main_pages.shape[0]
    extra_n = extra_pages.shape[0]
    grid_spec = pltpu.PrefetchScalarGridSpec(
        num_scalar_prefetch=1,
        grid=(heads, rows // BLOCK_Q),
        in_specs=[
            pl.BlockSpec((1, main_n * PAGE), lambda h, b, live: (0, 0)),
            pl.BlockSpec((1, extra_n * PAGE), lambda h, b, live: (0, 0)),
            pl.BlockSpec((BLOCK_Q, HD), lambda h, b, live: (b, h)),
            pl.BlockSpec((main_n, None, PAGE, HD), lambda h, b, live: (0, 0, 0, h)),
            pl.BlockSpec((main_n, None, PAGE, HD), lambda h, b, live: (0, 1, 0, h)),
            pl.BlockSpec((extra_n, None, PAGE, HD), lambda h, b, live: (0, 0, 0, h)),
            pl.BlockSpec((extra_n, None, PAGE, HD), lambda h, b, live: (0, 1, 0, h)),
            pl.BlockSpec((rows, HD), lambda h, b, live: (0, h)),
            pl.BlockSpec((rows, HD), lambda h, b, live: (0, h)),
        ],
        out_specs=pl.BlockSpec((BLOCK_Q, HD), lambda h, b, live: (b, h)),
    )
    keys_n = (main_n + extra_n) * PAGE + rows
    return pl.pallas_call(
        attend_kernel,
        grid_spec=grid_spec,
        out_shape=jax.ShapeDtypeStruct((rows, width), jnp.bfloat16),
        compiler_params=pltpu.CompilerParams(vmem_limit_bytes=56 * 1024 * 1024),
        cost_estimate=pl.CostEstimate(
            flops=4 * rows * keys_n * width,
            transcendentals=rows * keys_n * heads,
            bytes_accessed=2 * (2 * keys_n * width + 2 * rows * width),
        ),
    )(
        live,
        main_pos.reshape(1, -1),
        extra_pos.reshape(1, -1),
        query,
        main_pages,
        main_pages,
        extra_pages,
        extra_pages,
        new_key,
        new_value,
    )


def swap_kernel(send_ref, recv_ref, send_sems, recv_sems):
    count = send_ref.shape[0]
    me = lax.axis_index("req")
    tp_me = lax.axis_index("tp")
    barrier = pltpu.get_barrier_semaphore()

    def others(fn):
        def step(peer, carry):
            @pl.when(peer != me)
            def _():
                fn(peer)

            return carry

        lax.fori_loop(0, count, step, 0)

    def greet(peer):
        pl.semaphore_signal(barrier, inc=1, device_id=(peer, tp_me), device_id_type=MESH)

    others(greet)
    pl.semaphore_wait(barrier, count - 1)

    def outgoing(peer):
        return pltpu.make_async_remote_copy(
            src_ref=send_ref.at[peer],
            dst_ref=recv_ref.at[me],
            send_sem=send_sems.at[peer],
            recv_sem=recv_sems.at[me],
            device_id=(peer, tp_me),
            device_id_type=MESH,
        )

    def arriving(peer):
        return pltpu.make_async_remote_copy(
            src_ref=send_ref.at[peer],
            dst_ref=recv_ref.at[peer],
            send_sem=send_sems.at[peer],
            recv_sem=recv_sems.at[peer],
            device_id=(peer, tp_me),
            device_id_type=MESH,
        )

    others(lambda peer: outgoing(peer).start())
    recv_ref[pl.ds(me, 1)] = send_ref[pl.ds(me, 1)]
    others(lambda peer: outgoing(peer).wait_send())
    others(lambda peer: arriving(peer).wait_recv())


def swap_pieces(pieces):
    count = pieces.shape[0]
    return pl.pallas_call(
        swap_kernel,
        out_shape=jax.ShapeDtypeStruct(pieces.shape, pieces.dtype),
        in_specs=[pl.BlockSpec(memory_space=pltpu.VMEM)],
        out_specs=pl.BlockSpec(memory_space=pltpu.VMEM),
        scratch_shapes=[pltpu.SemaphoreType.DMA((count,)), pltpu.SemaphoreType.DMA((count,))],
        compiler_params=pltpu.CompilerParams(collective_id=0, has_side_effects=True),
    )(pieces)


def key_positions(entry_of_slot):
    tokens = jnp.arange(PAGE)[None, :]
    return jnp.where(entry_of_slot[:, None] >= 0, entry_of_slot[:, None] * PAGE + tokens, 1 << 30)


def project(hidden_in, qkv_weight, live_len, local_heads, local_width):
    token_rows = hidden_in.astype(jnp.float32)
    centre = jnp.mean(token_rows, axis=-1, keepdims=True)
    centred = token_rows - centre
    spread = jnp.mean(centred * centred, axis=-1, keepdims=True)
    normed = (centred * lax.rsqrt(spread + 1e-05)).astype(jnp.bfloat16)
    united_qkv = jnp.einsum("td,dcf->tcf", normed, qkv_weight, preferred_element_type=jnp.float32)
    positions = (live_len[:, None] + jnp.arange(NEW)[None, :]).astype(jnp.float32).reshape(-1)
    query_rot = rotate(united_qkv[:, 0].reshape(-1, local_heads, HD), positions).astype(
        jnp.bfloat16
    ).reshape(-1, local_width)
    new_key = rotate(united_qkv[:, 1].reshape(-1, local_heads, HD), positions).astype(
        jnp.bfloat16
    ).reshape(-1, local_width)
    new_value = united_qkv[:, 2].astype(jnp.bfloat16)
    return query_rot, new_key, new_value


def exchange_wide(kv_pool, page_slot, holder_rows, rank_all, req_index, req_count):
    capacity = 2
    held_here = holder_rows == req_index
    ranking = jnp.cumsum(held_here.astype(jnp.int32), axis=1) - 1
    picked = held_here[:, :, None] & (ranking[:, :, None] == jnp.arange(capacity)[None, None, :])
    send_slots = jnp.sum(jnp.where(picked, page_slot[:, :, None], 0), axis=1)
    incoming = lax.all_to_all(kv_pool[send_slots], "req", split_axis=0, concat_axis=0, tiled=True)
    incoming = incoming.reshape((req_count * capacity,) + kv_pool.shape[1:])
    own_holders = holder_rows[req_index]
    own_rank = rank_all[req_index]
    slot_of_entry = own_holders * capacity + own_rank
    hit = slot_of_entry[None, :] == jnp.arange(req_count * capacity)[:, None]
    entry_of_slot = jnp.max(jnp.where(hit, jnp.arange(hit.shape[1])[None, :], -1), axis=1)
    main_pos = key_positions(entry_of_slot)
    extra_pages = incoming[:1]
    extra_pos = key_positions(jnp.full((1,), -1, jnp.int32))
    return incoming, main_pos, extra_pages, extra_pos


def exchange_relay(kv_pool, page_slot, holder_rows, rank_all, req_index, req_count):
    rows, entries = holder_rows.shape
    spill = rank_all > 0
    frag = PAGE // req_count
    width = kv_pool.shape[-1]
    spill_flat = spill.reshape(-1)
    holders_flat = holder_rows.reshape(-1)
    slots_flat = page_slot.reshape(-1)
    spill_i = spill.astype(jnp.int32)
    named = (holder_rows[:, :, None] == jnp.arange(req_count)[None, None, :]).astype(jnp.int32)
    row_spills = jnp.sum(spill_i[:, :, None] * named, axis=1)
    before = jnp.cumsum(row_spills, axis=0) - row_spills
    holder_order = jnp.sum(named * before[:, None, :], axis=2).reshape(-1)
    req_order = jnp.cumsum(spill_i, axis=1) - spill_i
    first_hit = (holder_rows == req_index) & (rank_all == 0)
    send_slots = jnp.sum(jnp.where(first_hit, page_slot, 0), axis=1)
    wanted = jnp.arange(RELAY_A)
    match_a = (
        spill_flat[None, :]
        & (holders_flat[None, :] == req_index)
        & (holder_order[None, :] == wanted[:, None])
    )
    slot_a = jnp.sum(jnp.where(match_a, slots_flat[None, :], 0), axis=1)
    tokens = jnp.arange(PAGE + RELAY_A * frag)
    relay_part = tokens[None, :] >= PAGE
    piece = jnp.clip(tokens - PAGE, 0, None)
    page_idx = jnp.where(relay_part, slot_a[piece // frag][None, :], send_slots[:, None])
    tok_idx = jnp.where(
        relay_part, jnp.arange(req_count)[:, None] * frag + piece[None, :] % frag, tokens[None, :]
    )
    outgoing = kv_pool[page_idx[:, None, :], jnp.arange(2)[None, :, None], tok_idx[:, None, :]]
    incoming = lax.all_to_all(outgoing, "req", split_axis=0, concat_axis=0, tiled=True)
    relayed = (
        incoming[:, :, PAGE:]
        .reshape(req_count, 2, RELAY_A, frag, width)
        .transpose(0, 2, 1, 3, 4)
        .reshape(req_count * RELAY_A, 2, frag, width)
    )
    match_b = spill[:, None, :] & (req_order[:, None, :] == jnp.arange(RELAY_B)[None, :, None])
    src_holder = jnp.sum(jnp.where(match_b, holder_rows[:, None, :], 0), axis=2)
    src_index = jnp.sum(
        jnp.where(match_b, holder_order.reshape(rows, entries)[:, None, :], 0), axis=2
    )
    extra = relayed[src_holder * RELAY_A + jnp.clip(src_index, 0, RELAY_A - 1)]
    extra = extra.transpose(0, 2, 1, 3, 4).reshape(rows, 2, RELAY_B * frag, width)
    returned = swap_pieces(extra)
    extra_pages = (
        returned.reshape(req_count, 2, RELAY_B, frag, width)
        .transpose(2, 1, 0, 3, 4)
        .reshape(RELAY_B, 2, PAGE, width)
    )
    own_holders = holder_rows[req_index]
    own_first = rank_all[req_index] == 0
    entry_ids = jnp.arange(entries)
    main_hit = own_first[None, :] & (own_holders[None, :] == jnp.arange(req_count)[:, None])
    main_pos = key_positions(jnp.max(jnp.where(main_hit, entry_ids[None, :], -1), axis=1))
    extra_hit = (~own_first)[None, :] & (
        req_order[req_index][None, :] == jnp.arange(RELAY_B)[:, None]
    )
    extra_pos = key_positions(jnp.max(jnp.where(extra_hit, entry_ids[None, :], -1), axis=1))
    return incoming, main_pos, extra_pages, extra_pos


def body(hidden_in, qkv_weight, out_weight, kv_pool, cached_len, page_slot, page_holder, cont_flag):
    req_count = lax.axis_size("req")
    req_index = lax.axis_index("req")
    local_width = qkv_weight.shape[2]
    local_heads = local_width // HD
    holder_rows = page_holder[:, :, 0]
    entries = holder_rows.shape[1]
    same_holder = holder_rows[:, :, None] == holder_rows[:, None, :]
    earlier = jnp.arange(entries)[None, None, :] < jnp.arange(entries)[None, :, None]
    rank_all = jnp.sum((same_holder & earlier).astype(jnp.int32), axis=2)
    spill = (rank_all > 0).astype(jnp.int32)
    relay_fits = (jnp.max(jnp.sum(spill, axis=1)) <= RELAY_B) & (
        jnp.max(jnp.sum(spill[:, :, None] * (holder_rows[:, :, None] == jnp.arange(req_count)), axis=(0, 1)))
        <= RELAY_A
    )
    lengths = lax.dynamic_slice_in_dim(cached_len, req_index, 1)
    flags = lax.dynamic_slice_in_dim(cont_flag, req_index, 1)
    live_len = lengths * flags
    operands = (hidden_in, qkv_weight, kv_pool, page_slot, holder_rows, rank_all, live_len)

    def branch(exchange):
        def run(ops):
            hidden, weight, pool, slots, holders, ranks, live = ops
            main_pages, main_pos, extra_pages, extra_pos = exchange(
                pool, slots, holders, ranks, req_index, req_count
            )
            query_rot, new_key, new_value = project(hidden, weight, live, local_heads, local_width)
            return attend(
                live, query_rot, main_pages, main_pos, extra_pages, extra_pos, new_key, new_value
            )

        return run

    attended = lax.cond(relay_fits, branch(exchange_relay), branch(exchange_wide), operands)
    head_term = jnp.dot(attended, out_weight, preferred_element_type=jnp.float32)
    return lax.psum_scatter(head_term.astype(jnp.bfloat16), "tp", scatter_dimension=0, tiled=True)


def solution(mesh):
    in_specs = (
        P("req", None),
        P(None, None, "tp"),
        P("tp", None),
        P("req", None, None, "tp"),
        P(),
        P(),
        P(),
        P(),
    )
    out_specs = P(("req", "tp"), None)
    return jax.shard_map(body, mesh=mesh, in_specs=in_specs, out_specs=out_specs, check_vma=False)
```

```python
import functools

import jax
import jax.numpy as jnp
from jax import lax
from jax.experimental import pallas as pl
from jax.experimental.pallas import tpu as pltpu
from jax.sharding import PartitionSpec as P

HD = 128
NEW = 1024
PAGE = 128
MAXP = 32
BLOCK_Q = 256
MESH = pl.DeviceIdType.MESH
RELAY_A = 8
RELAY_B = 1


def rotate(feature, position):
    half_width = feature.shape[-1] // 2
    indices = jnp.arange(half_width).astype(jnp.float32)
    inverse = jnp.exp(indices * (-2.0 / feature.shape[-1]) * jnp.log(jnp.float32(10000.0)))
    angles = position[:, None, None] * inverse[None, None, :]
    cosine = jnp.cos(angles)
    sine_part = jnp.sin(angles)
    first_half = feature[..., :half_width]
    second_half = feature[..., half_width:]
    return jnp.concatenate(
        [
            first_half * cosine - second_half * sine_part,
            second_half * cosine + first_half * sine_part,
        ],
        axis=-1,
    )


def attend_kernel(
    live_ref, kpm_ref, kpe_ref, q_ref, mk_ref, mv_ref, ek_ref, ev_ref, nk_ref, nv_ref, out_ref
):
    block = pl.program_id(1)
    live = live_ref[0]
    main_span = mk_ref.shape[0] * mk_ref.shape[1]
    extra_span = ek_ref.shape[0] * ek_ref.shape[1]
    query = q_ref[...]
    contract = (((1,), (1,)), ((), ()))
    scale = HD ** (-0.5)

    def scores(keys):
        return lax.dot_general(query, keys, contract, preferred_element_type=jnp.float32) * scale

    main_scores = scores(mk_ref[...].reshape(main_span, HD))
    extra_scores = scores(ek_ref[...].reshape(extra_span, HD))
    new_scores = scores(nk_ref[...])
    main_ok = kpm_ref[...] < live
    extra_ok = kpe_ref[...] < live
    query_pos = block * BLOCK_Q + lax.broadcasted_iota(jnp.int32, new_scores.shape, 0)
    new_ok = lax.broadcasted_iota(jnp.int32, new_scores.shape, 1) <= query_pos
    main_scores = jnp.where(main_ok, main_scores, -1e30)
    extra_scores = jnp.where(extra_ok, extra_scores, -1e30)
    new_scores = jnp.where(new_ok, new_scores, -1e30)
    row_top = jnp.maximum(
        jnp.maximum(
            jnp.max(main_scores, axis=1, keepdims=True),
            jnp.max(extra_scores, axis=1, keepdims=True),
        ),
        jnp.max(new_scores, axis=1, keepdims=True),
    )
    main_w = jnp.exp(main_scores - row_top)
    extra_w = jnp.exp(extra_scores - row_top)
    new_w = jnp.exp(new_scores - row_top)
    row_total = (
        jnp.sum(main_w, axis=1, keepdims=True)
        + jnp.sum(extra_w, axis=1, keepdims=True)
        + jnp.sum(new_w, axis=1, keepdims=True)
    )

    def weighted(weights, values):
        return jnp.dot(weights.astype(jnp.bfloat16), values, preferred_element_type=jnp.float32)

    summed = (
        weighted(main_w, mv_ref[...].reshape(main_span, HD))
        + weighted(extra_w, ev_ref[...].reshape(extra_span, HD))
        + weighted(new_w, nv_ref[...])
    )
    out_ref[...] = (summed / row_total).astype(out_ref.dtype)


def attend(live, query, main_pages, main_pos, extra_pages, extra_pos, new_key, new_value):
    rows, width = query.shape
    heads = width // HD
    main_n = main_pages.shape[0]
    extra_n = extra_pages.shape[0]
    grid_spec = pltpu.PrefetchScalarGridSpec(
        num_scalar_prefetch=1,
        grid=(heads, rows // BLOCK_Q),
        in_specs=[
            pl.BlockSpec((1, main_n * PAGE), lambda h, b, live: (0, 0)),
            pl.BlockSpec((1, extra_n * PAGE), lambda h, b, live: (0, 0)),
            pl.BlockSpec((BLOCK_Q, HD), lambda h, b, live: (b, h)),
            pl.BlockSpec((main_n, None, PAGE, HD), lambda h, b, live: (0, 0, 0, h)),
            pl.BlockSpec((main_n, None, PAGE, HD), lambda h, b, live: (0, 1, 0, h)),
            pl.BlockSpec((extra_n, None, PAGE, HD), lambda h, b, live: (0, 0, 0, h)),
            pl.BlockSpec((extra_n, None, PAGE, HD), lambda h, b, live: (0, 1, 0, h)),
            pl.BlockSpec((rows, HD), lambda h, b, live: (0, h)),
            pl.BlockSpec((rows, HD), lambda h, b, live: (0, h)),
        ],
        out_specs=pl.BlockSpec((BLOCK_Q, HD), lambda h, b, live: (b, h)),
    )
    keys_n = (main_n + extra_n) * PAGE + rows
    return pl.pallas_call(
        attend_kernel,
        grid_spec=grid_spec,
        out_shape=jax.ShapeDtypeStruct((rows, width), jnp.bfloat16),
        compiler_params=pltpu.CompilerParams(vmem_limit_bytes=56 * 1024 * 1024),
        cost_estimate=pl.CostEstimate(
            flops=4 * rows * keys_n * width,
            transcendentals=rows * keys_n * heads,
            bytes_accessed=2 * (2 * keys_n * width + 2 * rows * width),
        ),
    )(
        live,
        main_pos.reshape(1, -1),
        extra_pos.reshape(1, -1),
        query,
        main_pages,
        main_pages,
        extra_pages,
        extra_pages,
        new_key,
        new_value,
    )


def swap_kernel(send_ref, recv_ref, send_sems, recv_sems):
    count = send_ref.shape[0]
    me = lax.axis_index("req")
    tp_me = lax.axis_index("tp")
    barrier = pltpu.get_barrier_semaphore()

    def others(fn):
        def step(peer, carry):
            @pl.when(peer != me)
            def _():
                fn(peer)

            return carry

        lax.fori_loop(0, count, step, 0)

    def greet(peer):
        pl.semaphore_signal(barrier, inc=1, device_id=(peer, tp_me), device_id_type=MESH)

    others(greet)
    pl.semaphore_wait(barrier, count - 1)

    def outgoing(peer):
        return pltpu.make_async_remote_copy(
            src_ref=send_ref.at[peer],
            dst_ref=recv_ref.at[me],
            send_sem=send_sems.at[peer],
            recv_sem=recv_sems.at[me],
            device_id=(peer, tp_me),
            device_id_type=MESH,
        )

    def arriving(peer):
        return pltpu.make_async_remote_copy(
            src_ref=send_ref.at[peer],
            dst_ref=recv_ref.at[peer],
            send_sem=send_sems.at[peer],
            recv_sem=recv_sems.at[peer],
            device_id=(peer, tp_me),
            device_id_type=MESH,
        )

    others(lambda peer: outgoing(peer).start())
    recv_ref[pl.ds(me, 1)] = send_ref[pl.ds(me, 1)]
    others(lambda peer: outgoing(peer).wait_send())
    others(lambda peer: arriving(peer).wait_recv())


def swap_pieces(pieces):
    count = pieces.shape[0]
    return pl.pallas_call(
        swap_kernel,
        out_shape=jax.ShapeDtypeStruct(pieces.shape, pieces.dtype),
        in_specs=[pl.BlockSpec(memory_space=pltpu.VMEM)],
        out_specs=pl.BlockSpec(memory_space=pltpu.VMEM),
        scratch_shapes=[pltpu.SemaphoreType.DMA((count,)), pltpu.SemaphoreType.DMA((count,))],
        compiler_params=pltpu.CompilerParams(collective_id=0, has_side_effects=True),
    )(pieces)


def key_positions(entry_of_slot):
    tokens = jnp.arange(PAGE)[None, :]
    return jnp.where(entry_of_slot[:, None] >= 0, entry_of_slot[:, None] * PAGE + tokens, 1 << 30)


def project(hidden_in, qkv_weight, live_len, local_heads, local_width):
    token_rows = hidden_in.astype(jnp.float32)
    centre = jnp.mean(token_rows, axis=-1, keepdims=True)
    centred = token_rows - centre
    spread = jnp.mean(centred * centred, axis=-1, keepdims=True)
    normed = (centred * lax.rsqrt(spread + 1e-05)).astype(jnp.bfloat16)
    united_qkv = jnp.einsum("td,dcf->tcf", normed, qkv_weight, preferred_element_type=jnp.float32)
    positions = (live_len[:, None] + jnp.arange(NEW)[None, :]).astype(jnp.float32).reshape(-1)
    query_rot = rotate(united_qkv[:, 0].reshape(-1, local_heads, HD), positions).astype(
        jnp.bfloat16
    ).reshape(-1, local_width)
    new_key = rotate(united_qkv[:, 1].reshape(-1, local_heads, HD), positions).astype(
        jnp.bfloat16
    ).reshape(-1, local_width)
    new_value = united_qkv[:, 2].astype(jnp.bfloat16)
    return query_rot, new_key, new_value


def exchange_wide(kv_pool, page_slot, holder_rows, rank_all, req_index, req_count):
    capacity = 2
    held_here = holder_rows == req_index
    ranking = jnp.cumsum(held_here.astype(jnp.int32), axis=1) - 1
    picked = held_here[:, :, None] & (ranking[:, :, None] == jnp.arange(capacity)[None, None, :])
    send_slots = jnp.sum(jnp.where(picked, page_slot[:, :, None], 0), axis=1)
    incoming = lax.all_to_all(kv_pool[send_slots], "req", split_axis=0, concat_axis=0, tiled=True)
    incoming = incoming.reshape((req_count * capacity,) + kv_pool.shape[1:])
    own_holders = holder_rows[req_index]
    own_rank = rank_all[req_index]
    slot_of_entry = own_holders * capacity + own_rank
    hit = slot_of_entry[None, :] == jnp.arange(req_count * capacity)[:, None]
    entry_of_slot = jnp.max(jnp.where(hit, jnp.arange(hit.shape[1])[None, :], -1), axis=1)
    main_pos = key_positions(entry_of_slot)
    extra_pages = incoming[:1]
    extra_pos = key_positions(jnp.full((1,), -1, jnp.int32))
    return incoming, main_pos, extra_pages, extra_pos


def exchange_relay(kv_pool, page_slot, holder_rows, rank_all, req_index, req_count):
    rows, entries = holder_rows.shape
    spill = rank_all > 0
    frag = PAGE // req_count
    width = kv_pool.shape[-1]
    spill_flat = spill.reshape(-1)
    holders_flat = holder_rows.reshape(-1)
    slots_flat = page_slot.reshape(-1)
    spill_i = spill.astype(jnp.int32)
    named = (holder_rows[:, :, None] == jnp.arange(req_count)[None, None, :]).astype(jnp.int32)
    row_spills = jnp.sum(spill_i[:, :, None] * named, axis=1)
    before = jnp.cumsum(row_spills, axis=0) - row_spills
    holder_order = jnp.sum(named * before[:, None, :], axis=2).reshape(-1)
    req_order = jnp.cumsum(spill_i, axis=1) - spill_i
    first_hit = (holder_rows == req_index) & (rank_all == 0)
    send_slots = jnp.sum(jnp.where(first_hit, page_slot, 0), axis=1)
    wanted = jnp.arange(RELAY_A)
    match_a = (
        spill_flat[None, :]
        & (holders_flat[None, :] == req_index)
        & (holder_order[None, :] == wanted[:, None])
    )
    slot_a = jnp.sum(jnp.where(match_a, slots_flat[None, :], 0), axis=1)
    pieces = (
        kv_pool[slot_a]
        .reshape(RELAY_A, 2, req_count, frag, width)
        .transpose(2, 0, 1, 3, 4)
        .reshape(req_count, RELAY_A * 2 * frag, width)
    )
    relayed = swap_pieces(pieces).reshape(req_count * RELAY_A, 2, frag, width)
    match_b = spill[:, None, :] & (req_order[:, None, :] == jnp.arange(RELAY_B)[None, :, None])
    src_holder = jnp.sum(jnp.where(match_b, holder_rows[:, None, :], 0), axis=2)
    src_index = jnp.sum(
        jnp.where(match_b, holder_order.reshape(rows, entries)[:, None, :], 0), axis=2
    )
    extra = relayed[src_holder * RELAY_A + jnp.clip(src_index, 0, RELAY_A - 1)]
    extra = extra.transpose(0, 2, 1, 3, 4).reshape(rows, 2, RELAY_B * frag, width)
    outgoing = jnp.concatenate([kv_pool[send_slots], extra], axis=2)
    incoming = lax.all_to_all(outgoing, "req", split_axis=0, concat_axis=0, tiled=True)
    extra_pages = (
        incoming[:, :, PAGE:]
        .reshape(req_count, 2, RELAY_B, frag, width)
        .transpose(2, 1, 0, 3, 4)
        .reshape(RELAY_B, 2, PAGE, width)
    )
    own_holders = holder_rows[req_index]
    own_first = rank_all[req_index] == 0
    entry_ids = jnp.arange(entries)
    main_hit = own_first[None, :] & (own_holders[None, :] == jnp.arange(req_count)[:, None])
    main_pos = key_positions(jnp.max(jnp.where(main_hit, entry_ids[None, :], -1), axis=1))
    extra_hit = (~own_first)[None, :] & (
        req_order[req_index][None, :] == jnp.arange(RELAY_B)[:, None]
    )
    extra_pos = key_positions(jnp.max(jnp.where(extra_hit, entry_ids[None, :], -1), axis=1))
    return incoming, main_pos, extra_pages, extra_pos


def body(hidden_in, qkv_weight, out_weight, kv_pool, cached_len, page_slot, page_holder, cont_flag):
    req_count = lax.axis_size("req")
    req_index = lax.axis_index("req")
    local_width = qkv_weight.shape[2]
    local_heads = local_width // HD
    holder_rows = page_holder[:, :, 0]
    entries = holder_rows.shape[1]
    same_holder = holder_rows[:, :, None] == holder_rows[:, None, :]
    earlier = jnp.arange(entries)[None, None, :] < jnp.arange(entries)[None, :, None]
    rank_all = jnp.sum((same_holder & earlier).astype(jnp.int32), axis=2)
    spill = (rank_all > 0).astype(jnp.int32)
    relay_fits = (jnp.max(jnp.sum(spill, axis=1)) <= RELAY_B) & (
        jnp.max(jnp.sum(spill[:, :, None] * (holder_rows[:, :, None] == jnp.arange(req_count)), axis=(0, 1)))
        <= RELAY_A
    )
    lengths = lax.dynamic_slice_in_dim(cached_len, req_index, 1)
    flags = lax.dynamic_slice_in_dim(cont_flag, req_index, 1)
    live_len = lengths * flags
    operands = (hidden_in, qkv_weight, kv_pool, page_slot, holder_rows, rank_all, live_len)

    def branch(exchange):
        def run(ops):
            hidden, weight, pool, slots, holders, ranks, live = ops
            main_pages, main_pos, extra_pages, extra_pos = exchange(
                pool, slots, holders, ranks, req_index, req_count
            )
            query_rot, new_key, new_value = project(hidden, weight, live, local_heads, local_width)
            return attend(
                live, query_rot, main_pages, main_pos, extra_pages, extra_pos, new_key, new_value
            )

        return run

    attended = lax.cond(relay_fits, branch(exchange_relay), branch(exchange_wide), operands)
    head_term = jnp.dot(attended, out_weight, preferred_element_type=jnp.float32)
    return lax.psum_scatter(head_term.astype(jnp.bfloat16), "tp", scatter_dimension=0, tiled=True)


def solution(mesh):
    in_specs = (
        P("req", None),
        P(None, None, "tp"),
        P("tp", None),
        P("req", None, None, "tp"),
        P(),
        P(),
        P(),
        P(),
    )
    out_specs = P(("req", "tp"), None)
    return jax.shard_map(body, mesh=mesh, in_specs=in_specs, out_specs=out_specs, check_vma=False)
```

```python
import functools

import jax
import jax.numpy as jnp
from jax import lax
from jax.experimental import pallas as pl
from jax.experimental.pallas import tpu as pltpu
from jax.sharding import PartitionSpec as P

HD = 128
NEW = 1024
PAGE = 128
MAXP = 32
BLOCK_Q = 256
MESH = pl.DeviceIdType.MESH
RELAY_A = 8
RELAY_B = 1


def rotate(feature, position):
    half_width = feature.shape[-1] // 2
    indices = jnp.arange(half_width).astype(jnp.float32)
    inverse = jnp.exp(indices * (-2.0 / feature.shape[-1]) * jnp.log(jnp.float32(10000.0)))
    angles = position[:, None, None] * inverse[None, None, :]
    cosine = jnp.cos(angles)
    sine_part = jnp.sin(angles)
    first_half = feature[..., :half_width]
    second_half = feature[..., half_width:]
    return jnp.concatenate(
        [
            first_half * cosine - second_half * sine_part,
            second_half * cosine + first_half * sine_part,
        ],
        axis=-1,
    )


def attend_kernel(
    live_ref, kpm_ref, kpe_ref, q_ref, mk_ref, mv_ref, ek_ref, ev_ref, nk_ref, nv_ref, out_ref
):
    block = pl.program_id(1)
    live = live_ref[0]
    main_span = mk_ref.shape[0] * mk_ref.shape[1]
    extra_span = ek_ref.shape[0] * ek_ref.shape[1]
    query = q_ref[...]
    contract = (((1,), (1,)), ((), ()))
    scale = HD ** (-0.5)

    def scores(keys):
        return lax.dot_general(query, keys, contract, preferred_element_type=jnp.float32) * scale

    main_scores = scores(mk_ref[...].reshape(main_span, HD))
    extra_scores = scores(ek_ref[...].reshape(extra_span, HD))
    new_scores = scores(nk_ref[...])
    main_ok = kpm_ref[...] < live
    extra_ok = kpe_ref[...] < live
    query_pos = block * BLOCK_Q + lax.broadcasted_iota(jnp.int32, new_scores.shape, 0)
    new_ok = lax.broadcasted_iota(jnp.int32, new_scores.shape, 1) <= query_pos
    main_scores = jnp.where(main_ok, main_scores, -1e30)
    extra_scores = jnp.where(extra_ok, extra_scores, -1e30)
    new_scores = jnp.where(new_ok, new_scores, -1e30)
    row_top = jnp.maximum(
        jnp.maximum(
            jnp.max(main_scores, axis=1, keepdims=True),
            jnp.max(extra_scores, axis=1, keepdims=True),
        ),
        jnp.max(new_scores, axis=1, keepdims=True),
    )
    main_w = jnp.exp(main_scores - row_top)
    extra_w = jnp.exp(extra_scores - row_top)
    new_w = jnp.exp(new_scores - row_top)
    row_total = (
        jnp.sum(main_w, axis=1, keepdims=True)
        + jnp.sum(extra_w, axis=1, keepdims=True)
        + jnp.sum(new_w, axis=1, keepdims=True)
    )

    def weighted(weights, values):
        return jnp.dot(weights.astype(jnp.bfloat16), values, preferred_element_type=jnp.float32)

    summed = (
        weighted(main_w, mv_ref[...].reshape(main_span, HD))
        + weighted(extra_w, ev_ref[...].reshape(extra_span, HD))
        + weighted(new_w, nv_ref[...])
    )
    out_ref[...] = (summed / row_total).astype(out_ref.dtype)


def attend(live, query, main_pages, main_pos, extra_pages, extra_pos, new_key, new_value):
    rows, width = query.shape
    heads = width // HD
    main_n = main_pages.shape[0]
    extra_n = extra_pages.shape[0]
    grid_spec = pltpu.PrefetchScalarGridSpec(
        num_scalar_prefetch=1,
        grid=(heads, rows // BLOCK_Q),
        in_specs=[
            pl.BlockSpec((1, main_n * PAGE), lambda h, b, live: (0, 0)),
            pl.BlockSpec((1, extra_n * PAGE), lambda h, b, live: (0, 0)),
            pl.BlockSpec((BLOCK_Q, HD), lambda h, b, live: (b, h)),
            pl.BlockSpec((main_n, None, PAGE, HD), lambda h, b, live: (0, 0, 0, h)),
            pl.BlockSpec((main_n, None, PAGE, HD), lambda h, b, live: (0, 1, 0, h)),
            pl.BlockSpec((extra_n, None, PAGE, HD), lambda h, b, live: (0, 0, 0, h)),
            pl.BlockSpec((extra_n, None, PAGE, HD), lambda h, b, live: (0, 1, 0, h)),
            pl.BlockSpec((rows, HD), lambda h, b, live: (0, h)),
            pl.BlockSpec((rows, HD), lambda h, b, live: (0, h)),
        ],
        out_specs=pl.BlockSpec((BLOCK_Q, HD), lambda h, b, live: (b, h)),
    )
    keys_n = (main_n + extra_n) * PAGE + rows
    return pl.pallas_call(
        attend_kernel,
        grid_spec=grid_spec,
        out_shape=jax.ShapeDtypeStruct((rows, width), jnp.bfloat16),
        compiler_params=pltpu.CompilerParams(vmem_limit_bytes=56 * 1024 * 1024),
        cost_estimate=pl.CostEstimate(
            flops=4 * rows * keys_n * width,
            transcendentals=rows * keys_n * heads,
            bytes_accessed=2 * (2 * keys_n * width + 2 * rows * width),
        ),
    )(
        live,
        main_pos.reshape(1, -1),
        extra_pos.reshape(1, -1),
        query,
        main_pages,
        main_pages,
        extra_pages,
        extra_pages,
        new_key,
        new_value,
    )


def swap_kernel(send_ref, recv_ref, send_sems, recv_sems):
    count = send_ref.shape[0]
    me = lax.axis_index("req")
    tp_me = lax.axis_index("tp")
    barrier = pltpu.get_barrier_semaphore()

    def others(fn):
        def step(peer, carry):
            @pl.when(peer != me)
            def _():
                fn(peer)

            return carry

        lax.fori_loop(0, count, step, 0)

    def greet(peer):
        pl.semaphore_signal(barrier, inc=1, device_id=(peer, tp_me), device_id_type=MESH)

    others(greet)
    pl.semaphore_wait(barrier, count - 1)

    def outgoing(peer):
        return pltpu.make_async_remote_copy(
            src_ref=send_ref.at[peer],
            dst_ref=recv_ref.at[me],
            send_sem=send_sems.at[peer],
            recv_sem=recv_sems.at[me],
            device_id=(peer, tp_me),
            device_id_type=MESH,
        )

    def arriving(peer):
        return pltpu.make_async_remote_copy(
            src_ref=send_ref.at[peer],
            dst_ref=recv_ref.at[peer],
            send_sem=send_sems.at[peer],
            recv_sem=recv_sems.at[peer],
            device_id=(peer, tp_me),
            device_id_type=MESH,
        )

    others(lambda peer: outgoing(peer).start())
    recv_ref[pl.ds(me, 1)] = send_ref[pl.ds(me, 1)]
    others(lambda peer: outgoing(peer).wait_send())
    others(lambda peer: arriving(peer).wait_recv())


def swap_pieces(pieces):
    count = pieces.shape[0]
    return pl.pallas_call(
        swap_kernel,
        out_shape=jax.ShapeDtypeStruct(pieces.shape, pieces.dtype),
        in_specs=[pl.BlockSpec(memory_space=pltpu.VMEM)],
        out_specs=pl.BlockSpec(memory_space=pltpu.VMEM),
        scratch_shapes=[pltpu.SemaphoreType.DMA((count,)), pltpu.SemaphoreType.DMA((count,))],
        compiler_params=pltpu.CompilerParams(collective_id=0, has_side_effects=True),
    )(pieces)


def key_positions(entry_of_slot):
    tokens = jnp.arange(PAGE)[None, :]
    return jnp.where(entry_of_slot[:, None] >= 0, entry_of_slot[:, None] * PAGE + tokens, 1 << 30)


def project(hidden_in, qkv_weight, live_len, local_heads, local_width):
    token_rows = hidden_in.astype(jnp.float32)
    centre = jnp.mean(token_rows, axis=-1, keepdims=True)
    centred = token_rows - centre
    spread = jnp.mean(centred * centred, axis=-1, keepdims=True)
    normed = (centred * lax.rsqrt(spread + 1e-05)).astype(jnp.bfloat16)
    united_qkv = jnp.einsum("td,dcf->tcf", normed, qkv_weight, preferred_element_type=jnp.float32)
    positions = (live_len[:, None] + jnp.arange(NEW)[None, :]).astype(jnp.float32).reshape(-1)
    query_rot = rotate(united_qkv[:, 0].reshape(-1, local_heads, HD), positions).astype(
        jnp.bfloat16
    ).reshape(-1, local_width)
    new_key = rotate(united_qkv[:, 1].reshape(-1, local_heads, HD), positions).astype(
        jnp.bfloat16
    ).reshape(-1, local_width)
    new_value = united_qkv[:, 2].astype(jnp.bfloat16)
    return query_rot, new_key, new_value


def exchange_wide(kv_pool, page_slot, holder_rows, rank_all, req_index, req_count):
    capacity = 2
    held_here = holder_rows == req_index
    ranking = jnp.cumsum(held_here.astype(jnp.int32), axis=1) - 1
    picked = held_here[:, :, None] & (ranking[:, :, None] == jnp.arange(capacity)[None, None, :])
    send_slots = jnp.sum(jnp.where(picked, page_slot[:, :, None], 0), axis=1)
    incoming = lax.all_to_all(kv_pool[send_slots], "req", split_axis=0, concat_axis=0, tiled=True)
    incoming = incoming.reshape((req_count * capacity,) + kv_pool.shape[1:])
    own_holders = holder_rows[req_index]
    own_rank = rank_all[req_index]
    slot_of_entry = own_holders * capacity + own_rank
    hit = slot_of_entry[None, :] == jnp.arange(req_count * capacity)[:, None]
    entry_of_slot = jnp.max(jnp.where(hit, jnp.arange(hit.shape[1])[None, :], -1), axis=1)
    main_pos = key_positions(entry_of_slot)
    extra_pages = incoming[:1]
    extra_pos = key_positions(jnp.full((1,), -1, jnp.int32))
    return incoming, main_pos, extra_pages, extra_pos


def exchange_relay(kv_pool, page_slot, holder_rows, rank_all, req_index, req_count):
    rows, entries = holder_rows.shape
    spill = rank_all > 0
    frag = PAGE // req_count
    width = kv_pool.shape[-1]
    spill_flat = spill.reshape(-1)
    holders_flat = holder_rows.reshape(-1)
    slots_flat = page_slot.reshape(-1)
    spill_i = spill.astype(jnp.int32)
    named = (holder_rows[:, :, None] == jnp.arange(req_count)[None, None, :]).astype(jnp.int32)
    row_spills = jnp.sum(spill_i[:, :, None] * named, axis=1)
    before = jnp.cumsum(row_spills, axis=0) - row_spills
    holder_order = jnp.sum(named * before[:, None, :], axis=2).reshape(-1)
    req_order = jnp.cumsum(spill_i, axis=1) - spill_i
    first_hit = (holder_rows == req_index) & (rank_all == 0)
    send_slots = jnp.sum(jnp.where(first_hit, page_slot, 0), axis=1)
    wanted = jnp.arange(RELAY_A)
    match_a = (
        spill_flat[None, :]
        & (holders_flat[None, :] == req_index)
        & (holder_order[None, :] == wanted[:, None])
    )
    slot_a = jnp.sum(jnp.where(match_a, slots_flat[None, :], 0), axis=1)
    pieces = (
        kv_pool[slot_a]
        .reshape(RELAY_A, 2, req_count, frag, width)
        .transpose(2, 1, 0, 3, 4)
        .reshape(req_count, 2, RELAY_A * frag, width)
    )
    outgoing = jnp.concatenate([kv_pool[send_slots], pieces], axis=2)
    incoming = lax.all_to_all(outgoing, "req", split_axis=0, concat_axis=0, tiled=True)
    relayed = (
        incoming[:, :, PAGE:]
        .reshape(req_count, 2, RELAY_A, frag, width)
        .transpose(0, 2, 1, 3, 4)
        .reshape(req_count * RELAY_A, 2, frag, width)
    )
    match_b = spill[:, None, :] & (req_order[:, None, :] == jnp.arange(RELAY_B)[None, :, None])
    src_holder = jnp.sum(jnp.where(match_b, holder_rows[:, None, :], 0), axis=2)
    src_index = jnp.sum(
        jnp.where(match_b, holder_order.reshape(rows, entries)[:, None, :], 0), axis=2
    )
    extra = relayed[src_holder * RELAY_A + jnp.clip(src_index, 0, RELAY_A - 1)]
    extra = extra.transpose(0, 2, 1, 3, 4).reshape(rows, 2, RELAY_B * frag, width)
    returned = swap_pieces(extra)
    extra_pages = (
        returned.reshape(req_count, 2, RELAY_B, frag, width)
        .transpose(2, 1, 0, 3, 4)
        .reshape(RELAY_B, 2, PAGE, width)
    )
    own_holders = holder_rows[req_index]
    own_first = rank_all[req_index] == 0
    entry_ids = jnp.arange(entries)
    main_hit = own_first[None, :] & (own_holders[None, :] == jnp.arange(req_count)[:, None])
    main_pos = key_positions(jnp.max(jnp.where(main_hit, entry_ids[None, :], -1), axis=1))
    extra_hit = (~own_first)[None, :] & (
        req_order[req_index][None, :] == jnp.arange(RELAY_B)[:, None]
    )
    extra_pos = key_positions(jnp.max(jnp.where(extra_hit, entry_ids[None, :], -1), axis=1))
    return incoming, main_pos, extra_pages, extra_pos


def body(hidden_in, qkv_weight, out_weight, kv_pool, cached_len, page_slot, page_holder, cont_flag):
    req_count = lax.axis_size("req")
    req_index = lax.axis_index("req")
    local_width = qkv_weight.shape[2]
    local_heads = local_width // HD
    holder_rows = page_holder[:, :, 0]
    entries = holder_rows.shape[1]
    same_holder = holder_rows[:, :, None] == holder_rows[:, None, :]
    earlier = jnp.arange(entries)[None, None, :] < jnp.arange(entries)[None, :, None]
    rank_all = jnp.sum((same_holder & earlier).astype(jnp.int32), axis=2)
    spill = (rank_all > 0).astype(jnp.int32)
    relay_fits = (jnp.max(jnp.sum(spill, axis=1)) <= RELAY_B) & (
        jnp.max(jnp.sum(spill[:, :, None] * (holder_rows[:, :, None] == jnp.arange(req_count)), axis=(0, 1)))
        <= RELAY_A
    )
    lengths = lax.dynamic_slice_in_dim(cached_len, req_index, 1)
    flags = lax.dynamic_slice_in_dim(cont_flag, req_index, 1)
    live_len = lengths * flags
    main_pages, main_pos, extra_pages, extra_pos = exchange_relay(
        kv_pool, page_slot, holder_rows, rank_all, req_index, req_count
    )
    query_rot, new_key, new_value = project(hidden_in, qkv_weight, live_len, local_heads, local_width)
    attended = attend(
        live_len, query_rot, main_pages, main_pos, extra_pages, extra_pos, new_key, new_value
    )

    def keep(ops):
        return ops[0]

    def redo(ops):
        _, query, key, value, pool, slots, holders, ranks, live = ops
        pages, pos, extra, extra_at = exchange_wide(pool, slots, holders, ranks, req_index, req_count)
        return attend(live, query, pages, pos, extra, extra_at, key, value)

    attended = lax.cond(
        relay_fits,
        keep,
        redo,
        (attended, query_rot, new_key, new_value, kv_pool, page_slot, holder_rows, rank_all, live_len),
    )
    head_term = jnp.dot(attended, out_weight, preferred_element_type=jnp.float32)
    return lax.psum_scatter(head_term.astype(jnp.bfloat16), "tp", scatter_dimension=0, tiled=True)


def solution(mesh):
    in_specs = (
        P("req", None),
        P(None, None, "tp"),
        P("tp", None),
        P("req", None, None, "tp"),
        P(),
        P(),
        P(),
        P(),
    )
    out_specs = P(("req", "tp"), None)
    return jax.shard_map(body, mesh=mesh, in_specs=in_specs, out_specs=out_specs, check_vma=False)
```

```python
import functools

import jax
import jax.numpy as jnp
from jax import lax
from jax.experimental import pallas as pl
from jax.experimental.pallas import tpu as pltpu
from jax.sharding import PartitionSpec as P

HD = 128
NEW = 1024
PAGE = 128
MAXP = 32
BLOCK_Q = 256
MESH = pl.DeviceIdType.MESH
RELAY_A = 8
RELAY_B = 1


def rotate(feature, position):
    half_width = feature.shape[-1] // 2
    indices = jnp.arange(half_width).astype(jnp.float32)
    inverse = jnp.exp(indices * (-2.0 / feature.shape[-1]) * jnp.log(jnp.float32(10000.0)))
    angles = position[:, None, None] * inverse[None, None, :]
    cosine = jnp.cos(angles)
    sine_part = jnp.sin(angles)
    first_half = feature[..., :half_width]
    second_half = feature[..., half_width:]
    return jnp.concatenate(
        [
            first_half * cosine - second_half * sine_part,
            second_half * cosine + first_half * sine_part,
        ],
        axis=-1,
    )


def attend_kernel(
    live_ref, kpm_ref, kpe_ref, q_ref, mk_ref, mv_ref, ek_ref, ev_ref, nk_ref, nv_ref, w_ref,
    out_ref, acc_ref
):
    block = pl.program_id(0)
    head = pl.program_id(1)
    live = live_ref[0]
    main_span = mk_ref.shape[0] * mk_ref.shape[1]
    extra_span = ek_ref.shape[0] * ek_ref.shape[1]
    query = q_ref[...]
    contract = (((1,), (1,)), ((), ()))
    scale = HD ** (-0.5)

    def scores(keys):
        return lax.dot_general(query, keys, contract, preferred_element_type=jnp.float32) * scale

    main_scores = scores(mk_ref[...].reshape(main_span, HD))
    extra_scores = scores(ek_ref[...].reshape(extra_span, HD))
    new_scores = scores(nk_ref[...])
    main_ok = kpm_ref[...] < live
    extra_ok = kpe_ref[...] < live
    query_pos = block * BLOCK_Q + lax.broadcasted_iota(jnp.int32, new_scores.shape, 0)
    new_ok = lax.broadcasted_iota(jnp.int32, new_scores.shape, 1) <= query_pos
    main_scores = jnp.where(main_ok, main_scores, -1e30)
    extra_scores = jnp.where(extra_ok, extra_scores, -1e30)
    new_scores = jnp.where(new_ok, new_scores, -1e30)
    row_top = jnp.maximum(
        jnp.maximum(
            jnp.max(main_scores, axis=1, keepdims=True),
            jnp.max(extra_scores, axis=1, keepdims=True),
        ),
        jnp.max(new_scores, axis=1, keepdims=True),
    )
    main_w = jnp.exp(main_scores - row_top)
    extra_w = jnp.exp(extra_scores - row_top)
    new_w = jnp.exp(new_scores - row_top)
    row_total = (
        jnp.sum(main_w, axis=1, keepdims=True)
        + jnp.sum(extra_w, axis=1, keepdims=True)
        + jnp.sum(new_w, axis=1, keepdims=True)
    )

    def weighted(weights, values):
        return jnp.dot(weights.astype(jnp.bfloat16), values, preferred_element_type=jnp.float32)

    summed = (
        weighted(main_w, mv_ref[...].reshape(main_span, HD))
        + weighted(extra_w, ev_ref[...].reshape(extra_span, HD))
        + weighted(new_w, nv_ref[...])
    )
    attended = (summed / row_total).astype(jnp.bfloat16)
    part = jnp.dot(attended, w_ref[...], preferred_element_type=jnp.float32)

    @pl.when(head == 0)
    def _():
        acc_ref[...] = part

    @pl.when(head != 0)
    def _():
        acc_ref[...] += part

    @pl.when(head == pl.num_programs(1) - 1)
    def _():
        out_ref[...] = acc_ref[...].astype(out_ref.dtype)


def attend(live, query, main_pages, main_pos, extra_pages, extra_pos, new_key, new_value, out_weight):
    rows, width = query.shape
    heads = width // HD
    main_n = main_pages.shape[0]
    extra_n = extra_pages.shape[0]
    model_width = out_weight.shape[1]
    grid_spec = pltpu.PrefetchScalarGridSpec(
        num_scalar_prefetch=1,
        grid=(rows // BLOCK_Q, heads),
        in_specs=[
            pl.BlockSpec((1, main_n * PAGE), lambda b, h, live: (0, 0)),
            pl.BlockSpec((1, extra_n * PAGE), lambda b, h, live: (0, 0)),
            pl.BlockSpec((BLOCK_Q, HD), lambda b, h, live: (b, h)),
            pl.BlockSpec((main_n, None, PAGE, HD), lambda b, h, live: (0, 0, 0, h)),
            pl.BlockSpec((main_n, None, PAGE, HD), lambda b, h, live: (0, 1, 0, h)),
            pl.BlockSpec((extra_n, None, PAGE, HD), lambda b, h, live: (0, 0, 0, h)),
            pl.BlockSpec((extra_n, None, PAGE, HD), lambda b, h, live: (0, 1, 0, h)),
            pl.BlockSpec((rows, HD), lambda b, h, live: (0, h)),
            pl.BlockSpec((rows, HD), lambda b, h, live: (0, h)),
            pl.BlockSpec((HD, model_width), lambda b, h, live: (h, 0)),
        ],
        out_specs=pl.BlockSpec((BLOCK_Q, model_width), lambda b, h, live: (b, 0)),
        scratch_shapes=[pltpu.VMEM((BLOCK_Q, model_width), jnp.float32)],
    )
    keys_n = (main_n + extra_n) * PAGE + rows
    return pl.pallas_call(
        attend_kernel,
        grid_spec=grid_spec,
        out_shape=jax.ShapeDtypeStruct((rows, model_width), jnp.bfloat16),
        compiler_params=pltpu.CompilerParams(vmem_limit_bytes=56 * 1024 * 1024),
        cost_estimate=pl.CostEstimate(
            flops=4 * rows * keys_n * width + 2 * rows * width * model_width,
            transcendentals=rows * keys_n * heads,
            bytes_accessed=2 * (2 * keys_n * width + 2 * rows * width),
        ),
    )(
        live,
        main_pos.reshape(1, -1),
        extra_pos.reshape(1, -1),
        query,
        main_pages,
        main_pages,
        extra_pages,
        extra_pages,
        new_key,
        new_value,
        out_weight,
    )


def swap_kernel(send_ref, recv_ref, send_sems, recv_sems):
    count = send_ref.shape[0]
    me = lax.axis_index("req")
    tp_me = lax.axis_index("tp")
    barrier = pltpu.get_barrier_semaphore()

    def others(fn):
        def step(peer, carry):
            @pl.when(peer != me)
            def _():
                fn(peer)

            return carry

        lax.fori_loop(0, count, step, 0)

    def greet(peer):
        pl.semaphore_signal(barrier, inc=1, device_id=(peer, tp_me), device_id_type=MESH)

    others(greet)
    pl.semaphore_wait(barrier, count - 1)

    def outgoing(peer):
        return pltpu.make_async_remote_copy(
            src_ref=send_ref.at[peer],
            dst_ref=recv_ref.at[me],
            send_sem=send_sems.at[peer],
            recv_sem=recv_sems.at[me],
            device_id=(peer, tp_me),
            device_id_type=MESH,
        )

    def arriving(peer):
        return pltpu.make_async_remote_copy(
            src_ref=send_ref.at[peer],
            dst_ref=recv_ref.at[peer],
            send_sem=send_sems.at[peer],
            recv_sem=recv_sems.at[peer],
            device_id=(peer, tp_me),
            device_id_type=MESH,
        )

    others(lambda peer: outgoing(peer).start())
    recv_ref[pl.ds(me, 1)] = send_ref[pl.ds(me, 1)]
    others(lambda peer: outgoing(peer).wait_send())
    others(lambda peer: arriving(peer).wait_recv())


def swap_pieces(pieces):
    count = pieces.shape[0]
    return pl.pallas_call(
        swap_kernel,
        out_shape=jax.ShapeDtypeStruct(pieces.shape, pieces.dtype),
        in_specs=[pl.BlockSpec(memory_space=pltpu.VMEM)],
        out_specs=pl.BlockSpec(memory_space=pltpu.VMEM),
        scratch_shapes=[pltpu.SemaphoreType.DMA((count,)), pltpu.SemaphoreType.DMA((count,))],
        compiler_params=pltpu.CompilerParams(collective_id=0, has_side_effects=True),
    )(pieces)


def key_positions(entry_of_slot):
    tokens = jnp.arange(PAGE)[None, :]
    return jnp.where(entry_of_slot[:, None] >= 0, entry_of_slot[:, None] * PAGE + tokens, 1 << 30)


def project(hidden_in, qkv_weight, live_len, local_heads, local_width):
    token_rows = hidden_in.astype(jnp.float32)
    centre = jnp.mean(token_rows, axis=-1, keepdims=True)
    centred = token_rows - centre
    spread = jnp.mean(centred * centred, axis=-1, keepdims=True)
    normed = (centred * lax.rsqrt(spread + 1e-05)).astype(jnp.bfloat16)
    united_qkv = jnp.einsum("td,dcf->tcf", normed, qkv_weight, preferred_element_type=jnp.float32)
    positions = (live_len[:, None] + jnp.arange(NEW)[None, :]).astype(jnp.float32).reshape(-1)
    query_rot = rotate(united_qkv[:, 0].reshape(-1, local_heads, HD), positions).astype(
        jnp.bfloat16
    ).reshape(-1, local_width)
    new_key = rotate(united_qkv[:, 1].reshape(-1, local_heads, HD), positions).astype(
        jnp.bfloat16
    ).reshape(-1, local_width)
    new_value = united_qkv[:, 2].astype(jnp.bfloat16)
    return query_rot, new_key, new_value


def exchange_wide(kv_pool, page_slot, holder_rows, rank_all, req_index, req_count):
    capacity = 2
    held_here = holder_rows == req_index
    ranking = jnp.cumsum(held_here.astype(jnp.int32), axis=1) - 1
    picked = held_here[:, :, None] & (ranking[:, :, None] == jnp.arange(capacity)[None, None, :])
    send_slots = jnp.sum(jnp.where(picked, page_slot[:, :, None], 0), axis=1)
    incoming = lax.all_to_all(kv_pool[send_slots], "req", split_axis=0, concat_axis=0, tiled=True)
    incoming = incoming.reshape((req_count * capacity,) + kv_pool.shape[1:])
    own_holders = holder_rows[req_index]
    own_rank = rank_all[req_index]
    slot_of_entry = own_holders * capacity + own_rank
    hit = slot_of_entry[None, :] == jnp.arange(req_count * capacity)[:, None]
    entry_of_slot = jnp.max(jnp.where(hit, jnp.arange(hit.shape[1])[None, :], -1), axis=1)
    main_pos = key_positions(entry_of_slot)
    extra_pages = incoming[:1]
    extra_pos = key_positions(jnp.full((1,), -1, jnp.int32))
    return incoming, main_pos, extra_pages, extra_pos


def exchange_relay(kv_pool, page_slot, holder_rows, rank_all, req_index, req_count):
    rows, entries = holder_rows.shape
    spill = rank_all > 0
    frag = PAGE // req_count
    width = kv_pool.shape[-1]
    spill_flat = spill.reshape(-1)
    holders_flat = holder_rows.reshape(-1)
    slots_flat = page_slot.reshape(-1)
    spill_i = spill.astype(jnp.int32)
    named = (holder_rows[:, :, None] == jnp.arange(req_count)[None, None, :]).astype(jnp.int32)
    row_spills = jnp.sum(spill_i[:, :, None] * named, axis=1)
    before = jnp.cumsum(row_spills, axis=0) - row_spills
    holder_order = jnp.sum(named * before[:, None, :], axis=2).reshape(-1)
    req_order = jnp.cumsum(spill_i, axis=1) - spill_i
    first_hit = (holder_rows == req_index) & (rank_all == 0)
    send_slots = jnp.sum(jnp.where(first_hit, page_slot, 0), axis=1)
    wanted = jnp.arange(RELAY_A)
    match_a = (
        spill_flat[None, :]
        & (holders_flat[None, :] == req_index)
        & (holder_order[None, :] == wanted[:, None])
    )
    slot_a = jnp.sum(jnp.where(match_a, slots_flat[None, :], 0), axis=1)
    pieces = (
        kv_pool[slot_a]
        .reshape(RELAY_A, 2, req_count, frag, width)
        .transpose(2, 1, 0, 3, 4)
        .reshape(req_count, 2, RELAY_A * frag, width)
    )
    outgoing = jnp.concatenate([kv_pool[send_slots], pieces], axis=2)
    incoming = lax.all_to_all(outgoing, "req", split_axis=0, concat_axis=0, tiled=True)
    relayed = (
        incoming[:, :, PAGE:]
        .reshape(req_count, 2, RELAY_A, frag, width)
        .transpose(0, 2, 1, 3, 4)
        .reshape(req_count * RELAY_A, 2, frag, width)
    )
    match_b = spill[:, None, :] & (req_order[:, None, :] == jnp.arange(RELAY_B)[None, :, None])
    src_holder = jnp.sum(jnp.where(match_b, holder_rows[:, None, :], 0), axis=2)
    src_index = jnp.sum(
        jnp.where(match_b, holder_order.reshape(rows, entries)[:, None, :], 0), axis=2
    )
    extra = relayed[src_holder * RELAY_A + jnp.clip(src_index, 0, RELAY_A - 1)]
    extra = extra.transpose(0, 2, 1, 3, 4).reshape(rows, 2, RELAY_B * frag, width)
    returned = swap_pieces(extra.reshape(rows, -1, width)).reshape(extra.shape)
    extra_pages = (
        returned.reshape(req_count, 2, RELAY_B, frag, width)
        .transpose(2, 1, 0, 3, 4)
        .reshape(RELAY_B, 2, PAGE, width)
    )
    own_holders = holder_rows[req_index]
    own_first = rank_all[req_index] == 0
    entry_ids = jnp.arange(entries)
    main_hit = own_first[None, :] & (own_holders[None, :] == jnp.arange(req_count)[:, None])
    main_pos = key_positions(jnp.max(jnp.where(main_hit, entry_ids[None, :], -1), axis=1))
    extra_hit = (~own_first)[None, :] & (
        req_order[req_index][None, :] == jnp.arange(RELAY_B)[:, None]
    )
    extra_pos = key_positions(jnp.max(jnp.where(extra_hit, entry_ids[None, :], -1), axis=1))
    return incoming, main_pos, extra_pages, extra_pos


def body(hidden_in, qkv_weight, out_weight, kv_pool, cached_len, page_slot, page_holder, cont_flag):
    req_count = lax.axis_size("req")
    req_index = lax.axis_index("req")
    local_width = qkv_weight.shape[2]
    local_heads = local_width // HD
    holder_rows = page_holder[:, :, 0]
    entries = holder_rows.shape[1]
    same_holder = holder_rows[:, :, None] == holder_rows[:, None, :]
    earlier = jnp.arange(entries)[None, None, :] < jnp.arange(entries)[None, :, None]
    rank_all = jnp.sum((same_holder & earlier).astype(jnp.int32), axis=2)
    spill = (rank_all > 0).astype(jnp.int32)
    relay_fits = (jnp.max(jnp.sum(spill, axis=1)) <= RELAY_B) & (
        jnp.max(jnp.sum(spill[:, :, None] * (holder_rows[:, :, None] == jnp.arange(req_count)), axis=(0, 1)))
        <= RELAY_A
    )
    lengths = lax.dynamic_slice_in_dim(cached_len, req_index, 1)
    flags = lax.dynamic_slice_in_dim(cont_flag, req_index, 1)
    live_len = lengths * flags
    main_pages, main_pos, extra_pages, extra_pos = exchange_relay(
        kv_pool, page_slot, holder_rows, rank_all, req_index, req_count
    )
    query_rot, new_key, new_value = project(hidden_in, qkv_weight, live_len, local_heads, local_width)
    head_term = attend(
        live_len,
        query_rot,
        main_pages,
        main_pos,
        extra_pages,
        extra_pos,
        new_key,
        new_value,
        out_weight,
    )

    def keep(ops):
        return ops[0]

    def redo(ops):
        _, query, key, value, pool, slots, holders, ranks, live, weight_out = ops
        pages, pos, extra, extra_at = exchange_wide(pool, slots, holders, ranks, req_index, req_count)
        return attend(live, query, pages, pos, extra, extra_at, key, value, weight_out)

    head_term = lax.cond(
        relay_fits,
        keep,
        redo,
        (
            head_term,
            query_rot,
            new_key,
            new_value,
            kv_pool,
            page_slot,
            holder_rows,
            rank_all,
            live_len,
            out_weight,
        ),
    )
    return lax.psum_scatter(head_term, "tp", scatter_dimension=0, tiled=True)


def solution(mesh):
    in_specs = (
        P("req", None),
        P(None, None, "tp"),
        P("tp", None),
        P("req", None, None, "tp"),
        P(),
        P(),
        P(),
        P(),
    )
    out_specs = P(("req", "tp"), None)
    return jax.shard_map(body, mesh=mesh, in_specs=in_specs, out_specs=out_specs, check_vma=False)
```

```python
import functools

import jax
import jax.numpy as jnp
from jax import lax
from jax.experimental import pallas as pl
from jax.experimental.pallas import tpu as pltpu
from jax.sharding import PartitionSpec as P

HD = 128
NEW = 1024
PAGE = 128
MAXP = 32
BLOCK_Q = 256
MESH = pl.DeviceIdType.MESH
RELAY_A = 8
RELAY_B = 1


def rotate(feature, position):
    half_width = feature.shape[-1] // 2
    indices = jnp.arange(half_width).astype(jnp.float32)
    inverse = jnp.exp(indices * (-2.0 / feature.shape[-1]) * jnp.log(jnp.float32(10000.0)))
    angles = position[:, None, None] * inverse[None, None, :]
    cosine = jnp.cos(angles)
    sine_part = jnp.sin(angles)
    first_half = feature[..., :half_width]
    second_half = feature[..., half_width:]
    return jnp.concatenate(
        [
            first_half * cosine - second_half * sine_part,
            second_half * cosine + first_half * sine_part,
        ],
        axis=-1,
    )


def attend_kernel(
    live_ref, kpm_ref, kpe_ref, q_ref, mk_ref, mv_ref, ek_ref, ev_ref, nk_ref, nv_ref, out_ref
):
    block = pl.program_id(1)
    live = live_ref[0]
    main_span = mk_ref.shape[0] * mk_ref.shape[1]
    extra_span = ek_ref.shape[0] * ek_ref.shape[1]
    query = q_ref[...]
    contract = (((1,), (1,)), ((), ()))
    scale = HD ** (-0.5)

    def scores(keys):
        return lax.dot_general(query, keys, contract, preferred_element_type=jnp.float32) * scale

    main_scores = scores(mk_ref[...].reshape(main_span, HD))
    extra_scores = scores(ek_ref[...].reshape(extra_span, HD))
    new_scores = scores(nk_ref[...])
    main_ok = kpm_ref[...] < live
    extra_ok = kpe_ref[...] < live
    query_pos = block * BLOCK_Q + lax.broadcasted_iota(jnp.int32, new_scores.shape, 0)
    new_ok = lax.broadcasted_iota(jnp.int32, new_scores.shape, 1) <= query_pos
    main_scores = jnp.where(main_ok, main_scores, -1e30)
    extra_scores = jnp.where(extra_ok, extra_scores, -1e30)
    new_scores = jnp.where(new_ok, new_scores, -1e30)
    row_top = jnp.maximum(
        jnp.maximum(
            jnp.max(main_scores, axis=1, keepdims=True),
            jnp.max(extra_scores, axis=1, keepdims=True),
        ),
        jnp.max(new_scores, axis=1, keepdims=True),
    )
    main_w = jnp.exp(main_scores - row_top)
    extra_w = jnp.exp(extra_scores - row_top)
    new_w = jnp.exp(new_scores - row_top)
    row_total = (
        jnp.sum(main_w, axis=1, keepdims=True)
        + jnp.sum(extra_w, axis=1, keepdims=True)
        + jnp.sum(new_w, axis=1, keepdims=True)
    )

    def weighted(weights, values):
        return jnp.dot(weights.astype(jnp.bfloat16), values, preferred_element_type=jnp.float32)

    summed = (
        weighted(main_w, mv_ref[...].reshape(main_span, HD))
        + weighted(extra_w, ev_ref[...].reshape(extra_span, HD))
        + weighted(new_w, nv_ref[...])
    )
    out_ref[...] = (summed / row_total).astype(out_ref.dtype)


def attend(live, query, main_pages, main_pos, extra_pages, extra_pos, new_key, new_value):
    rows, width = query.shape
    heads = width // HD
    main_n = main_pages.shape[0]
    extra_n = extra_pages.shape[0]
    grid_spec = pltpu.PrefetchScalarGridSpec(
        num_scalar_prefetch=1,
        grid=(heads, rows // BLOCK_Q),
        in_specs=[
            pl.BlockSpec((1, main_n * PAGE), lambda h, b, live: (0, 0)),
            pl.BlockSpec((1, extra_n * PAGE), lambda h, b, live: (0, 0)),
            pl.BlockSpec((BLOCK_Q, HD), lambda h, b, live: (b, h)),
            pl.BlockSpec((main_n, None, PAGE, HD), lambda h, b, live: (0, 0, 0, h)),
            pl.BlockSpec((main_n, None, PAGE, HD), lambda h, b, live: (0, 1, 0, h)),
            pl.BlockSpec((extra_n, None, PAGE, HD), lambda h, b, live: (0, 0, 0, h)),
            pl.BlockSpec((extra_n, None, PAGE, HD), lambda h, b, live: (0, 1, 0, h)),
            pl.BlockSpec((rows, HD), lambda h, b, live: (0, h)),
            pl.BlockSpec((rows, HD), lambda h, b, live: (0, h)),
        ],
        out_specs=pl.BlockSpec((BLOCK_Q, HD), lambda h, b, live: (b, h)),
    )
    keys_n = (main_n + extra_n) * PAGE + rows
    return pl.pallas_call(
        attend_kernel,
        grid_spec=grid_spec,
        out_shape=jax.ShapeDtypeStruct((rows, width), jnp.bfloat16),
        compiler_params=pltpu.CompilerParams(vmem_limit_bytes=56 * 1024 * 1024),
        cost_estimate=pl.CostEstimate(
            flops=4 * rows * keys_n * width,
            transcendentals=rows * keys_n * heads,
            bytes_accessed=2 * (2 * keys_n * width + 2 * rows * width),
        ),
    )(
        live,
        main_pos.reshape(1, -1),
        extra_pos.reshape(1, -1),
        query,
        main_pages,
        main_pages,
        extra_pages,
        extra_pages,
        new_key,
        new_value,
    )


def swap_kernel(send_ref, recv_ref, send_sems, recv_sems):
    count = send_ref.shape[0]
    me = lax.axis_index("req")
    tp_me = lax.axis_index("tp")
    barrier = pltpu.get_barrier_semaphore()

    def others(fn):
        def step(peer, carry):
            @pl.when(peer != me)
            def _():
                fn(peer)

            return carry

        lax.fori_loop(0, count, step, 0)

    def greet(peer):
        pl.semaphore_signal(barrier, inc=1, device_id=(peer, tp_me), device_id_type=MESH)

    others(greet)
    pl.semaphore_wait(barrier, count - 1)

    def outgoing(peer):
        return pltpu.make_async_remote_copy(
            src_ref=send_ref.at[peer],
            dst_ref=recv_ref.at[me],
            send_sem=send_sems.at[peer],
            recv_sem=recv_sems.at[me],
            device_id=(peer, tp_me),
            device_id_type=MESH,
        )

    def arriving(peer):
        return pltpu.make_async_remote_copy(
            src_ref=send_ref.at[peer],
            dst_ref=recv_ref.at[peer],
            send_sem=send_sems.at[peer],
            recv_sem=recv_sems.at[peer],
            device_id=(peer, tp_me),
            device_id_type=MESH,
        )

    others(lambda peer: outgoing(peer).start())
    recv_ref[pl.ds(me, 1)] = send_ref[pl.ds(me, 1)]
    others(lambda peer: outgoing(peer).wait_send())
    others(lambda peer: arriving(peer).wait_recv())


def swap_pieces(pieces):
    count = pieces.shape[0]
    return pl.pallas_call(
        swap_kernel,
        out_shape=jax.ShapeDtypeStruct(pieces.shape, pieces.dtype),
        in_specs=[pl.BlockSpec(memory_space=pltpu.VMEM)],
        out_specs=pl.BlockSpec(memory_space=pltpu.VMEM),
        scratch_shapes=[pltpu.SemaphoreType.DMA((count,)), pltpu.SemaphoreType.DMA((count,))],
        compiler_params=pltpu.CompilerParams(collective_id=0, has_side_effects=True),
    )(pieces)


def key_positions(entry_of_slot):
    tokens = jnp.arange(PAGE)[None, :]
    return jnp.where(entry_of_slot[:, None] >= 0, entry_of_slot[:, None] * PAGE + tokens, 1 << 30)


def project(hidden_in, qkv_weight, live_len, local_heads, local_width):
    token_rows = hidden_in.astype(jnp.float32)
    centre = jnp.mean(token_rows, axis=-1, keepdims=True)
    centred = token_rows - centre
    spread = jnp.mean(centred * centred, axis=-1, keepdims=True)
    normed = (centred * lax.rsqrt(spread + 1e-05)).astype(jnp.bfloat16)
    united_qkv = jnp.einsum("td,dcf->tcf", normed, qkv_weight, preferred_element_type=jnp.float32)
    positions = (live_len[:, None] + jnp.arange(NEW)[None, :]).astype(jnp.float32).reshape(-1)
    query_rot = rotate(united_qkv[:, 0].reshape(-1, local_heads, HD), positions).astype(
        jnp.bfloat16
    ).reshape(-1, local_width)
    new_key = rotate(united_qkv[:, 1].reshape(-1, local_heads, HD), positions).astype(
        jnp.bfloat16
    ).reshape(-1, local_width)
    new_value = united_qkv[:, 2].astype(jnp.bfloat16)
    return query_rot, new_key, new_value


def exchange_wide(kv_pool, page_slot, holder_rows, rank_all, req_index, req_count):
    capacity = 2
    held_here = holder_rows == req_index
    ranking = jnp.cumsum(held_here.astype(jnp.int32), axis=1) - 1
    picked = held_here[:, :, None] & (ranking[:, :, None] == jnp.arange(capacity)[None, None, :])
    send_slots = jnp.sum(jnp.where(picked, page_slot[:, :, None], 0), axis=1)
    incoming = lax.all_to_all(kv_pool[send_slots], "req", split_axis=0, concat_axis=0, tiled=True)
    incoming = incoming.reshape((req_count * capacity,) + kv_pool.shape[1:])
    own_holders = holder_rows[req_index]
    own_rank = rank_all[req_index]
    slot_of_entry = own_holders * capacity + own_rank
    hit = slot_of_entry[None, :] == jnp.arange(req_count * capacity)[:, None]
    entry_of_slot = jnp.max(jnp.where(hit, jnp.arange(hit.shape[1])[None, :], -1), axis=1)
    main_pos = key_positions(entry_of_slot)
    extra_pages = incoming[:1]
    extra_pos = key_positions(jnp.full((1,), -1, jnp.int32))
    return incoming, main_pos, extra_pages, extra_pos


def exchange_relay(kv_pool, page_slot, holder_rows, rank_all, req_index, req_count):
    rows, entries = holder_rows.shape
    spill = rank_all > 0
    frag = PAGE // req_count
    width = kv_pool.shape[-1]
    spill_flat = spill.reshape(-1)
    holders_flat = holder_rows.reshape(-1)
    slots_flat = page_slot.reshape(-1)
    spill_i = spill.astype(jnp.int32)
    named = (holder_rows[:, :, None] == jnp.arange(req_count)[None, None, :]).astype(jnp.int32)
    row_spills = jnp.sum(spill_i[:, :, None] * named, axis=1)
    before = jnp.cumsum(row_spills, axis=0) - row_spills
    holder_order = jnp.sum(named * before[:, None, :], axis=2).reshape(-1)
    req_order = jnp.cumsum(spill_i, axis=1) - spill_i
    first_hit = (holder_rows == req_index) & (rank_all == 0)
    send_slots = jnp.sum(jnp.where(first_hit, page_slot, 0), axis=1)
    wanted = jnp.arange(RELAY_A)
    match_a = (
        spill_flat[None, :]
        & (holders_flat[None, :] == req_index)
        & (holder_order[None, :] == wanted[:, None])
    )
    slot_a = jnp.sum(jnp.where(match_a, slots_flat[None, :], 0), axis=1)
    pieces = (
        kv_pool[slot_a]
        .reshape(RELAY_A, 2, req_count, frag, width)
        .transpose(2, 1, 0, 3, 4)
        .reshape(req_count, 2, RELAY_A * frag, width)
    )
    padded = jnp.pad(kv_pool, ((0, 0), (0, 0), (0, RELAY_A * frag), (0, 0)))
    outgoing = padded[send_slots].at[:, :, PAGE:, :].set(pieces)
    incoming = lax.all_to_all(outgoing, "req", split_axis=0, concat_axis=0, tiled=True)
    relayed = (
        incoming[:, :, PAGE:]
        .reshape(req_count, 2, RELAY_A, frag, width)
        .transpose(0, 2, 1, 3, 4)
        .reshape(req_count * RELAY_A, 2, frag, width)
    )
    match_b = spill[:, None, :] & (req_order[:, None, :] == jnp.arange(RELAY_B)[None, :, None])
    src_holder = jnp.sum(jnp.where(match_b, holder_rows[:, None, :], 0), axis=2)
    src_index = jnp.sum(
        jnp.where(match_b, holder_order.reshape(rows, entries)[:, None, :], 0), axis=2
    )
    extra = relayed[src_holder * RELAY_A + jnp.clip(src_index, 0, RELAY_A - 1)]
    extra = extra.transpose(0, 2, 1, 3, 4).reshape(rows, 2, RELAY_B * frag, width)
    returned = swap_pieces(extra)
    extra_pages = (
        returned.reshape(req_count, 2, RELAY_B, frag, width)
        .transpose(2, 1, 0, 3, 4)
        .reshape(RELAY_B, 2, PAGE, width)
    )
    own_holders = holder_rows[req_index]
    own_first = rank_all[req_index] == 0
    entry_ids = jnp.arange(entries)
    main_hit = own_first[None, :] & (own_holders[None, :] == jnp.arange(req_count)[:, None])
    main_pos = key_positions(jnp.max(jnp.where(main_hit, entry_ids[None, :], -1), axis=1))
    extra_hit = (~own_first)[None, :] & (
        req_order[req_index][None, :] == jnp.arange(RELAY_B)[:, None]
    )
    extra_pos = key_positions(jnp.max(jnp.where(extra_hit, entry_ids[None, :], -1), axis=1))
    return incoming, main_pos, extra_pages, extra_pos


def body(hidden_in, qkv_weight, out_weight, kv_pool, cached_len, page_slot, page_holder, cont_flag):
    req_count = lax.axis_size("req")
    req_index = lax.axis_index("req")
    local_width = qkv_weight.shape[2]
    local_heads = local_width // HD
    holder_rows = page_holder[:, :, 0]
    entries = holder_rows.shape[1]
    same_holder = holder_rows[:, :, None] == holder_rows[:, None, :]
    earlier = jnp.arange(entries)[None, None, :] < jnp.arange(entries)[None, :, None]
    rank_all = jnp.sum((same_holder & earlier).astype(jnp.int32), axis=2)
    spill = (rank_all > 0).astype(jnp.int32)
    relay_fits = (jnp.max(jnp.sum(spill, axis=1)) <= RELAY_B) & (
        jnp.max(jnp.sum(spill[:, :, None] * (holder_rows[:, :, None] == jnp.arange(req_count)), axis=(0, 1)))
        <= RELAY_A
    )
    lengths = lax.dynamic_slice_in_dim(cached_len, req_index, 1)
    flags = lax.dynamic_slice_in_dim(cont_flag, req_index, 1)
    live_len = lengths * flags
    main_pages, main_pos, extra_pages, extra_pos = exchange_relay(
        kv_pool, page_slot, holder_rows, rank_all, req_index, req_count
    )
    query_rot, new_key, new_value = project(hidden_in, qkv_weight, live_len, local_heads, local_width)
    attended = attend(
        live_len, query_rot, main_pages, main_pos, extra_pages, extra_pos, new_key, new_value
    )

    def keep(ops):
        return ops[0]

    def redo(ops):
        _, query, key, value, pool, slots, holders, ranks, live = ops
        pages, pos, extra, extra_at = exchange_wide(pool, slots, holders, ranks, req_index, req_count)
        return attend(live, query, pages, pos, extra, extra_at, key, value)

    attended = lax.cond(
        relay_fits,
        keep,
        redo,
        (attended, query_rot, new_key, new_value, kv_pool, page_slot, holder_rows, rank_all, live_len),
    )
    head_term = jnp.dot(attended, out_weight, preferred_element_type=jnp.float32)
    return lax.psum_scatter(head_term.astype(jnp.bfloat16), "tp", scatter_dimension=0, tiled=True)


def solution(mesh):
    in_specs = (
        P("req", None),
        P(None, None, "tp"),
        P("tp", None),
        P("req", None, None, "tp"),
        P(),
        P(),
        P(),
        P(),
    )
    out_specs = P(("req", "tp"), None)
    return jax.shard_map(body, mesh=mesh, in_specs=in_specs, out_specs=out_specs, check_vma=False)
```

```python
import functools

import jax
import jax.numpy as jnp
from jax import lax
from jax.experimental import pallas as pl
from jax.experimental.pallas import tpu as pltpu
from jax.sharding import PartitionSpec as P

HD = 128
NEW = 1024
PAGE = 128
MAXP = 32
BLOCK_Q = 256
MESH = pl.DeviceIdType.MESH
RELAY_A = 8
RELAY_B = 1


def rotate(feature, position):
    half_width = feature.shape[-1] // 2
    indices = jnp.arange(half_width).astype(jnp.float32)
    inverse = jnp.exp(indices * (-2.0 / feature.shape[-1]) * jnp.log(jnp.float32(10000.0)))
    angles = position[:, None, None] * inverse[None, None, :]
    cosine = jnp.cos(angles)
    sine_part = jnp.sin(angles)
    first_half = feature[..., :half_width]
    second_half = feature[..., half_width:]
    return jnp.concatenate(
        [
            first_half * cosine - second_half * sine_part,
            second_half * cosine + first_half * sine_part,
        ],
        axis=-1,
    )


def attend_kernel(
    live_ref, kpm_ref, kpe_ref, q_ref, mk_ref, mv_ref, ek_ref, ev_ref, nk_ref, nv_ref, out_ref
):
    live = live_ref[0]
    main_span = mk_ref.shape[0] * mk_ref.shape[1]
    extra_span = ek_ref.shape[0] * ek_ref.shape[1]
    contract = (((1,), (1,)), ((), ()))
    scale = HD ** (-0.5)
    main_ok = kpm_ref[...] < live
    extra_ok = kpe_ref[...] < live

    for block in range(q_ref.shape[0] // BLOCK_Q):
        rows = pl.ds(block * BLOCK_Q, BLOCK_Q)
        seen = pl.ds(0, (block + 1) * BLOCK_Q)
        query = q_ref[rows, :]

        def scores(keys):
            return (
                lax.dot_general(query, keys, contract, preferred_element_type=jnp.float32) * scale
            )

        main_scores = scores(mk_ref[...].reshape(main_span, HD))
        extra_scores = scores(ek_ref[...].reshape(extra_span, HD))
        new_scores = scores(nk_ref[seen, :])
        query_pos = block * BLOCK_Q + lax.broadcasted_iota(jnp.int32, new_scores.shape, 0)
        new_ok = lax.broadcasted_iota(jnp.int32, new_scores.shape, 1) <= query_pos
        main_scores = jnp.where(main_ok, main_scores, -1e30)
        extra_scores = jnp.where(extra_ok, extra_scores, -1e30)
        new_scores = jnp.where(new_ok, new_scores, -1e30)
        row_top = jnp.maximum(
            jnp.maximum(
                jnp.max(main_scores, axis=1, keepdims=True),
                jnp.max(extra_scores, axis=1, keepdims=True),
            ),
            jnp.max(new_scores, axis=1, keepdims=True),
        )
        main_w = jnp.exp(main_scores - row_top)
        extra_w = jnp.exp(extra_scores - row_top)
        new_w = jnp.exp(new_scores - row_top)
        row_total = (
            jnp.sum(main_w, axis=1, keepdims=True)
            + jnp.sum(extra_w, axis=1, keepdims=True)
            + jnp.sum(new_w, axis=1, keepdims=True)
        )

        def weighted(weights, values):
            return jnp.dot(
                weights.astype(jnp.bfloat16), values, preferred_element_type=jnp.float32
            )

        summed = (
            weighted(main_w, mv_ref[...].reshape(main_span, HD))
            + weighted(extra_w, ev_ref[...].reshape(extra_span, HD))
            + weighted(new_w, nv_ref[seen, :])
        )
        out_ref[rows, :] = (summed / row_total).astype(out_ref.dtype)


def attend(live, query, main_pages, main_pos, extra_pages, extra_pos, new_key, new_value):
    rows, width = query.shape
    heads = width // HD
    main_n = main_pages.shape[0]
    extra_n = extra_pages.shape[0]
    grid_spec = pltpu.PrefetchScalarGridSpec(
        num_scalar_prefetch=1,
        grid=(heads,),
        in_specs=[
            pl.BlockSpec((1, main_n * PAGE), lambda h, live: (0, 0)),
            pl.BlockSpec((1, extra_n * PAGE), lambda h, live: (0, 0)),
            pl.BlockSpec((rows, HD), lambda h, live: (0, h)),
            pl.BlockSpec((main_n, None, PAGE, HD), lambda h, live: (0, 0, 0, h)),
            pl.BlockSpec((main_n, None, PAGE, HD), lambda h, live: (0, 1, 0, h)),
            pl.BlockSpec((extra_n, None, PAGE, HD), lambda h, live: (0, 0, 0, h)),
            pl.BlockSpec((extra_n, None, PAGE, HD), lambda h, live: (0, 1, 0, h)),
            pl.BlockSpec((rows, HD), lambda h, live: (0, h)),
            pl.BlockSpec((rows, HD), lambda h, live: (0, h)),
        ],
        out_specs=pl.BlockSpec((rows, HD), lambda h, live: (0, h)),
    )
    keys_n = (main_n + extra_n) * PAGE + rows // 2
    return pl.pallas_call(
        attend_kernel,
        grid_spec=grid_spec,
        out_shape=jax.ShapeDtypeStruct((rows, width), jnp.bfloat16),
        compiler_params=pltpu.CompilerParams(vmem_limit_bytes=56 * 1024 * 1024),
        cost_estimate=pl.CostEstimate(
            flops=4 * rows * keys_n * width,
            transcendentals=rows * keys_n * heads,
            bytes_accessed=2 * (2 * keys_n * width + 2 * rows * width),
        ),
    )(
        live,
        main_pos.reshape(1, -1),
        extra_pos.reshape(1, -1),
        query,
        main_pages,
        main_pages,
        extra_pages,
        extra_pages,
        new_key,
        new_value,
    )


def grid_attend_kernel(
    live_ref, kpm_ref, kpe_ref, q_ref, mk_ref, mv_ref, ek_ref, ev_ref, nk_ref, nv_ref, out_ref
):
    block = pl.program_id(1)
    live = live_ref[0]
    main_span = mk_ref.shape[0] * mk_ref.shape[1]
    extra_span = ek_ref.shape[0] * ek_ref.shape[1]
    query = q_ref[...]
    contract = (((1,), (1,)), ((), ()))
    scale = HD ** (-0.5)

    def scores(keys):
        return lax.dot_general(query, keys, contract, preferred_element_type=jnp.float32) * scale

    main_scores = scores(mk_ref[...].reshape(main_span, HD))
    extra_scores = scores(ek_ref[...].reshape(extra_span, HD))
    new_scores = scores(nk_ref[...])
    main_ok = kpm_ref[...] < live
    extra_ok = kpe_ref[...] < live
    query_pos = block * BLOCK_Q + lax.broadcasted_iota(jnp.int32, new_scores.shape, 0)
    new_ok = lax.broadcasted_iota(jnp.int32, new_scores.shape, 1) <= query_pos
    main_scores = jnp.where(main_ok, main_scores, -1e30)
    extra_scores = jnp.where(extra_ok, extra_scores, -1e30)
    new_scores = jnp.where(new_ok, new_scores, -1e30)
    row_top = jnp.maximum(
        jnp.maximum(
            jnp.max(main_scores, axis=1, keepdims=True),
            jnp.max(extra_scores, axis=1, keepdims=True),
        ),
        jnp.max(new_scores, axis=1, keepdims=True),
    )
    main_w = jnp.exp(main_scores - row_top)
    extra_w = jnp.exp(extra_scores - row_top)
    new_w = jnp.exp(new_scores - row_top)
    row_total = (
        jnp.sum(main_w, axis=1, keepdims=True)
        + jnp.sum(extra_w, axis=1, keepdims=True)
        + jnp.sum(new_w, axis=1, keepdims=True)
    )

    def weighted(weights, values):
        return jnp.dot(weights.astype(jnp.bfloat16), values, preferred_element_type=jnp.float32)

    summed = (
        weighted(main_w, mv_ref[...].reshape(main_span, HD))
        + weighted(extra_w, ev_ref[...].reshape(extra_span, HD))
        + weighted(new_w, nv_ref[...])
    )
    out_ref[...] = (summed / row_total).astype(out_ref.dtype)


def grid_attend(live, query, main_pages, main_pos, extra_pages, extra_pos, new_key, new_value):
    rows, width = query.shape
    heads = width // HD
    main_n = main_pages.shape[0]
    extra_n = extra_pages.shape[0]
    grid_spec = pltpu.PrefetchScalarGridSpec(
        num_scalar_prefetch=1,
        grid=(heads, rows // BLOCK_Q),
        in_specs=[
            pl.BlockSpec((1, main_n * PAGE), lambda h, b, live: (0, 0)),
            pl.BlockSpec((1, extra_n * PAGE), lambda h, b, live: (0, 0)),
            pl.BlockSpec((BLOCK_Q, HD), lambda h, b, live: (b, h)),
            pl.BlockSpec((main_n, None, PAGE, HD), lambda h, b, live: (0, 0, 0, h)),
            pl.BlockSpec((main_n, None, PAGE, HD), lambda h, b, live: (0, 1, 0, h)),
            pl.BlockSpec((extra_n, None, PAGE, HD), lambda h, b, live: (0, 0, 0, h)),
            pl.BlockSpec((extra_n, None, PAGE, HD), lambda h, b, live: (0, 1, 0, h)),
            pl.BlockSpec((rows, HD), lambda h, b, live: (0, h)),
            pl.BlockSpec((rows, HD), lambda h, b, live: (0, h)),
        ],
        out_specs=pl.BlockSpec((BLOCK_Q, HD), lambda h, b, live: (b, h)),
    )
    keys_n = (main_n + extra_n) * PAGE + rows
    return pl.pallas_call(
        grid_attend_kernel,
        grid_spec=grid_spec,
        out_shape=jax.ShapeDtypeStruct((rows, width), jnp.bfloat16),
        compiler_params=pltpu.CompilerParams(vmem_limit_bytes=56 * 1024 * 1024),
        cost_estimate=pl.CostEstimate(
            flops=4 * rows * keys_n * width,
            transcendentals=rows * keys_n * heads,
            bytes_accessed=2 * (2 * keys_n * width + 2 * rows * width),
        ),
    )(
        live,
        main_pos.reshape(1, -1),
        extra_pos.reshape(1, -1),
        query,
        main_pages,
        main_pages,
        extra_pages,
        extra_pages,
        new_key,
        new_value,
    )


def swap_kernel(send_ref, recv_ref, send_sems, recv_sems):
    count = send_ref.shape[0]
    me = lax.axis_index("req")
    tp_me = lax.axis_index("tp")
    barrier = pltpu.get_barrier_semaphore()

    def others(fn):
        def step(peer, carry):
            @pl.when(peer != me)
            def _():
                fn(peer)

            return carry

        lax.fori_loop(0, count, step, 0)

    def greet(peer):
        pl.semaphore_signal(barrier, inc=1, device_id=(peer, tp_me), device_id_type=MESH)

    others(greet)
    pl.semaphore_wait(barrier, count - 1)

    def outgoing(peer):
        return pltpu.make_async_remote_copy(
            src_ref=send_ref.at[peer],
            dst_ref=recv_ref.at[me],
            send_sem=send_sems.at[peer],
            recv_sem=recv_sems.at[me],
            device_id=(peer, tp_me),
            device_id_type=MESH,
        )

    def arriving(peer):
        return pltpu.make_async_remote_copy(
            src_ref=send_ref.at[peer],
            dst_ref=recv_ref.at[peer],
            send_sem=send_sems.at[peer],
            recv_sem=recv_sems.at[peer],
            device_id=(peer, tp_me),
            device_id_type=MESH,
        )

    others(lambda peer: outgoing(peer).start())
    recv_ref[pl.ds(me, 1)] = send_ref[pl.ds(me, 1)]
    others(lambda peer: outgoing(peer).wait_send())
    others(lambda peer: arriving(peer).wait_recv())


def swap_pieces(pieces):
    count = pieces.shape[0]
    return pl.pallas_call(
        swap_kernel,
        out_shape=jax.ShapeDtypeStruct(pieces.shape, pieces.dtype),
        in_specs=[pl.BlockSpec(memory_space=pltpu.VMEM)],
        out_specs=pl.BlockSpec(memory_space=pltpu.VMEM),
        scratch_shapes=[pltpu.SemaphoreType.DMA((count,)), pltpu.SemaphoreType.DMA((count,))],
        compiler_params=pltpu.CompilerParams(collective_id=0, has_side_effects=True),
    )(pieces)


def key_positions(entry_of_slot):
    tokens = jnp.arange(PAGE)[None, :]
    return jnp.where(entry_of_slot[:, None] >= 0, entry_of_slot[:, None] * PAGE + tokens, 1 << 30)


def project(hidden_in, qkv_weight, live_len, local_heads, local_width):
    token_rows = hidden_in.astype(jnp.float32)
    centre = jnp.mean(token_rows, axis=-1, keepdims=True)
    centred = token_rows - centre
    spread = jnp.mean(centred * centred, axis=-1, keepdims=True)
    normed = (centred * lax.rsqrt(spread + 1e-05)).astype(jnp.bfloat16)
    united_qkv = jnp.einsum("td,dcf->tcf", normed, qkv_weight, preferred_element_type=jnp.float32)
    positions = (live_len[:, None] + jnp.arange(NEW)[None, :]).astype(jnp.float32).reshape(-1)
    query_rot = rotate(united_qkv[:, 0].reshape(-1, local_heads, HD), positions).astype(
        jnp.bfloat16
    ).reshape(-1, local_width)
    new_key = rotate(united_qkv[:, 1].reshape(-1, local_heads, HD), positions).astype(
        jnp.bfloat16
    ).reshape(-1, local_width)
    new_value = united_qkv[:, 2].astype(jnp.bfloat16)
    return query_rot, new_key, new_value


def exchange_wide(kv_pool, page_slot, holder_rows, rank_all, req_index, req_count):
    capacity = 2
    held_here = holder_rows == req_index
    ranking = jnp.cumsum(held_here.astype(jnp.int32), axis=1) - 1
    picked = held_here[:, :, None] & (ranking[:, :, None] == jnp.arange(capacity)[None, None, :])
    send_slots = jnp.sum(jnp.where(picked, page_slot[:, :, None], 0), axis=1)
    incoming = lax.all_to_all(kv_pool[send_slots], "req", split_axis=0, concat_axis=0, tiled=True)
    incoming = incoming.reshape((req_count * capacity,) + kv_pool.shape[1:])
    own_holders = holder_rows[req_index]
    own_rank = rank_all[req_index]
    slot_of_entry = own_holders * capacity + own_rank
    hit = slot_of_entry[None, :] == jnp.arange(req_count * capacity)[:, None]
    entry_of_slot = jnp.max(jnp.where(hit, jnp.arange(hit.shape[1])[None, :], -1), axis=1)
    main_pos = key_positions(entry_of_slot)
    extra_pages = incoming[:1]
    extra_pos = key_positions(jnp.full((1,), -1, jnp.int32))
    return incoming, main_pos, extra_pages, extra_pos


def exchange_relay(kv_pool, page_slot, holder_rows, rank_all, req_index, req_count):
    rows, entries = holder_rows.shape
    spill = rank_all > 0
    frag = PAGE // req_count
    width = kv_pool.shape[-1]
    spill_flat = spill.reshape(-1)
    holders_flat = holder_rows.reshape(-1)
    slots_flat = page_slot.reshape(-1)
    spill_i = spill.astype(jnp.int32)
    named = (holder_rows[:, :, None] == jnp.arange(req_count)[None, None, :]).astype(jnp.int32)
    row_spills = jnp.sum(spill_i[:, :, None] * named, axis=1)
    before = jnp.cumsum(row_spills, axis=0) - row_spills
    holder_order = jnp.sum(named * before[:, None, :], axis=2).reshape(-1)
    req_order = jnp.cumsum(spill_i, axis=1) - spill_i
    first_hit = (holder_rows == req_index) & (rank_all == 0)
    send_slots = jnp.sum(jnp.where(first_hit, page_slot, 0), axis=1)
    wanted = jnp.arange(RELAY_A)
    match_a = (
        spill_flat[None, :]
        & (holders_flat[None, :] == req_index)
        & (holder_order[None, :] == wanted[:, None])
    )
    slot_a = jnp.sum(jnp.where(match_a, slots_flat[None, :], 0), axis=1)
    pieces = (
        kv_pool[slot_a]
        .reshape(RELAY_A, 2, req_count, frag, width)
        .transpose(2, 1, 0, 3, 4)
        .reshape(req_count, 2, RELAY_A * frag, width)
    )
    padded = jnp.pad(kv_pool, ((0, 0), (0, 0), (0, RELAY_A * frag), (0, 0)))
    outgoing = padded[send_slots].at[:, :, PAGE:, :].set(pieces)
    incoming = lax.all_to_all(outgoing, "req", split_axis=0, concat_axis=0, tiled=True)
    relayed = (
        incoming[:, :, PAGE:]
        .reshape(req_count, 2, RELAY_A, frag, width)
        .transpose(0, 2, 1, 3, 4)
        .reshape(req_count * RELAY_A, 2, frag, width)
    )
    match_b = spill[:, None, :] & (req_order[:, None, :] == jnp.arange(RELAY_B)[None, :, None])
    src_holder = jnp.sum(jnp.where(match_b, holder_rows[:, None, :], 0), axis=2)
    src_index = jnp.sum(
        jnp.where(match_b, holder_order.reshape(rows, entries)[:, None, :], 0), axis=2
    )
    extra = relayed[src_holder * RELAY_A + jnp.clip(src_index, 0, RELAY_A - 1)]
    extra = extra.transpose(0, 2, 1, 3, 4).reshape(rows, 2, RELAY_B * frag, width)
    returned = swap_pieces(extra)
    extra_pages = (
        returned.reshape(req_count, 2, RELAY_B, frag, width)
        .transpose(2, 1, 0, 3, 4)
        .reshape(RELAY_B, 2, PAGE, width)
    )
    own_holders = holder_rows[req_index]
    own_first = rank_all[req_index] == 0
    entry_ids = jnp.arange(entries)
    main_hit = own_first[None, :] & (own_holders[None, :] == jnp.arange(req_count)[:, None])
    main_pos = key_positions(jnp.max(jnp.where(main_hit, entry_ids[None, :], -1), axis=1))
    extra_hit = (~own_first)[None, :] & (
        req_order[req_index][None, :] == jnp.arange(RELAY_B)[:, None]
    )
    extra_pos = key_positions(jnp.max(jnp.where(extra_hit, entry_ids[None, :], -1), axis=1))
    return incoming, main_pos, extra_pages, extra_pos


def body(hidden_in, qkv_weight, out_weight, kv_pool, cached_len, page_slot, page_holder, cont_flag):
    req_count = lax.axis_size("req")
    req_index = lax.axis_index("req")
    local_width = qkv_weight.shape[2]
    local_heads = local_width // HD
    holder_rows = page_holder[:, :, 0]
    entries = holder_rows.shape[1]
    same_holder = holder_rows[:, :, None] == holder_rows[:, None, :]
    earlier = jnp.arange(entries)[None, None, :] < jnp.arange(entries)[None, :, None]
    rank_all = jnp.sum((same_holder & earlier).astype(jnp.int32), axis=2)
    spill = (rank_all > 0).astype(jnp.int32)
    relay_fits = (jnp.max(jnp.sum(spill, axis=1)) <= RELAY_B) & (
        jnp.max(jnp.sum(spill[:, :, None] * (holder_rows[:, :, None] == jnp.arange(req_count)), axis=(0, 1)))
        <= RELAY_A
    )
    lengths = lax.dynamic_slice_in_dim(cached_len, req_index, 1)
    flags = lax.dynamic_slice_in_dim(cont_flag, req_index, 1)
    live_len = lengths * flags
    main_pages, main_pos, extra_pages, extra_pos = exchange_relay(
        kv_pool, page_slot, holder_rows, rank_all, req_index, req_count
    )
    query_rot, new_key, new_value = project(hidden_in, qkv_weight, live_len, local_heads, local_width)
    attended = attend(
        live_len, query_rot, main_pages, main_pos, extra_pages, extra_pos, new_key, new_value
    )

    def keep(ops):
        return ops[0]

    def redo(ops):
        _, query, key, value, pool, slots, holders, ranks, live = ops
        pages, pos, extra, extra_at = exchange_wide(pool, slots, holders, ranks, req_index, req_count)
        return grid_attend(live, query, pages, pos, extra, extra_at, key, value)

    attended = lax.cond(
        relay_fits,
        keep,
        redo,
        (attended, query_rot, new_key, new_value, kv_pool, page_slot, holder_rows, rank_all, live_len),
    )
    head_term = jnp.dot(attended, out_weight, preferred_element_type=jnp.float32)
    return lax.psum_scatter(head_term.astype(jnp.bfloat16), "tp", scatter_dimension=0, tiled=True)


def solution(mesh):
    in_specs = (
        P("req", None),
        P(None, None, "tp"),
        P("tp", None),
        P("req", None, None, "tp"),
        P(),
        P(),
        P(),
        P(),
    )
    out_specs = P(("req", "tp"), None)
    return jax.shard_map(body, mesh=mesh, in_specs=in_specs, out_specs=out_specs, check_vma=False)
```

```python
import functools

import jax
import jax.numpy as jnp
from jax import lax
from jax.experimental import pallas as pl
from jax.experimental.pallas import tpu as pltpu
from jax.sharding import PartitionSpec as P

HD = 128
NEW = 1024
PAGE = 128
MAXP = 32
BLOCK_Q = 256
MESH = pl.DeviceIdType.MESH
RELAY_A = 8
RELAY_B = 1


def rotate(feature, position):
    half_width = feature.shape[-1] // 2
    indices = jnp.arange(half_width).astype(jnp.float32)
    inverse = jnp.exp(indices * (-2.0 / feature.shape[-1]) * jnp.log(jnp.float32(10000.0)))
    angles = position[:, None, None] * inverse[None, None, :]
    cosine = jnp.cos(angles)
    sine_part = jnp.sin(angles)
    first_half = feature[..., :half_width]
    second_half = feature[..., half_width:]
    return jnp.concatenate(
        [
            first_half * cosine - second_half * sine_part,
            second_half * cosine + first_half * sine_part,
        ],
        axis=-1,
    )


def attend_kernel(
    live_ref, kpm_ref, kpe_ref, q_ref, mk_ref, mv_ref, ek_ref, ev_ref, nk_ref, nv_ref, out_ref
):
    live = live_ref[0]
    main_span = mk_ref.shape[0] * mk_ref.shape[1]
    extra_span = ek_ref.shape[0] * ek_ref.shape[1]
    contract = (((1,), (1,)), ((), ()))
    scale = HD ** (-0.5)
    main_ok = kpm_ref[...] < live
    extra_ok = kpe_ref[...] < live

    for block in range(q_ref.shape[0] // BLOCK_Q):
        rows = pl.ds(block * BLOCK_Q, BLOCK_Q)
        seen = pl.ds(0, (block + 1) * BLOCK_Q)
        query = q_ref[rows, :]

        def scores(keys):
            return (
                lax.dot_general(query, keys, contract, preferred_element_type=jnp.float32) * scale
            )

        main_scores = scores(mk_ref[...].reshape(main_span, HD))
        extra_scores = scores(ek_ref[...].reshape(extra_span, HD))
        new_scores = scores(nk_ref[seen, :])
        query_pos = block * BLOCK_Q + lax.broadcasted_iota(jnp.int32, new_scores.shape, 0)
        new_ok = lax.broadcasted_iota(jnp.int32, new_scores.shape, 1) <= query_pos
        main_scores = jnp.where(main_ok, main_scores, -1e30)
        extra_scores = jnp.where(extra_ok, extra_scores, -1e30)
        new_scores = jnp.where(new_ok, new_scores, -1e30)
        row_top = jnp.maximum(
            jnp.maximum(
                jnp.max(main_scores, axis=1, keepdims=True),
                jnp.max(extra_scores, axis=1, keepdims=True),
            ),
            jnp.max(new_scores, axis=1, keepdims=True),
        )
        main_w = jnp.exp(main_scores - row_top)
        extra_w = jnp.exp(extra_scores - row_top)
        new_w = jnp.exp(new_scores - row_top)

        def weighted(weights, values):
            low = weights.astype(jnp.bfloat16)
            ones = jnp.ones((low.shape[1], HD), jnp.bfloat16)
            return (
                jnp.dot(low, values, preferred_element_type=jnp.float32),
                jnp.dot(low, ones, preferred_element_type=jnp.float32),
            )

        main_sum, main_total = weighted(main_w, mv_ref[...].reshape(main_span, HD))
        extra_sum, extra_total = weighted(extra_w, ev_ref[...].reshape(extra_span, HD))
        new_sum, new_total = weighted(new_w, nv_ref[seen, :])
        summed = main_sum + extra_sum + new_sum
        row_total = main_total + extra_total + new_total
        out_ref[rows, :] = (summed / row_total).astype(out_ref.dtype)


def attend(live, query, main_pages, main_pos, extra_pages, extra_pos, new_key, new_value):
    rows, width = query.shape
    heads = width // HD
    main_n = main_pages.shape[0]
    extra_n = extra_pages.shape[0]
    grid_spec = pltpu.PrefetchScalarGridSpec(
        num_scalar_prefetch=1,
        grid=(heads,),
        in_specs=[
            pl.BlockSpec((1, main_n * PAGE), lambda h, live: (0, 0)),
            pl.BlockSpec((1, extra_n * PAGE), lambda h, live: (0, 0)),
            pl.BlockSpec((rows, HD), lambda h, live: (0, h)),
            pl.BlockSpec((main_n, None, PAGE, HD), lambda h, live: (0, 0, 0, h)),
            pl.BlockSpec((main_n, None, PAGE, HD), lambda h, live: (0, 1, 0, h)),
            pl.BlockSpec((extra_n, None, PAGE, HD), lambda h, live: (0, 0, 0, h)),
            pl.BlockSpec((extra_n, None, PAGE, HD), lambda h, live: (0, 1, 0, h)),
            pl.BlockSpec((rows, HD), lambda h, live: (0, h)),
            pl.BlockSpec((rows, HD), lambda h, live: (0, h)),
        ],
        out_specs=pl.BlockSpec((rows, HD), lambda h, live: (0, h)),
    )
    keys_n = (main_n + extra_n) * PAGE + rows // 2
    return pl.pallas_call(
        attend_kernel,
        grid_spec=grid_spec,
        out_shape=jax.ShapeDtypeStruct((rows, width), jnp.bfloat16),
        compiler_params=pltpu.CompilerParams(vmem_limit_bytes=56 * 1024 * 1024),
        cost_estimate=pl.CostEstimate(
            flops=4 * rows * keys_n * width,
            transcendentals=rows * keys_n * heads,
            bytes_accessed=2 * (2 * keys_n * width + 2 * rows * width),
        ),
    )(
        live,
        main_pos.reshape(1, -1),
        extra_pos.reshape(1, -1),
        query,
        main_pages,
        main_pages,
        extra_pages,
        extra_pages,
        new_key,
        new_value,
    )


def grid_attend_kernel(
    live_ref, kpm_ref, kpe_ref, q_ref, mk_ref, mv_ref, ek_ref, ev_ref, nk_ref, nv_ref, out_ref
):
    block = pl.program_id(1)
    live = live_ref[0]
    main_span = mk_ref.shape[0] * mk_ref.shape[1]
    extra_span = ek_ref.shape[0] * ek_ref.shape[1]
    query = q_ref[...]
    contract = (((1,), (1,)), ((), ()))
    scale = HD ** (-0.5)

    def scores(keys):
        return lax.dot_general(query, keys, contract, preferred_element_type=jnp.float32) * scale

    main_scores = scores(mk_ref[...].reshape(main_span, HD))
    extra_scores = scores(ek_ref[...].reshape(extra_span, HD))
    new_scores = scores(nk_ref[...])
    main_ok = kpm_ref[...] < live
    extra_ok = kpe_ref[...] < live
    query_pos = block * BLOCK_Q + lax.broadcasted_iota(jnp.int32, new_scores.shape, 0)
    new_ok = lax.broadcasted_iota(jnp.int32, new_scores.shape, 1) <= query_pos
    main_scores = jnp.where(main_ok, main_scores, -1e30)
    extra_scores = jnp.where(extra_ok, extra_scores, -1e30)
    new_scores = jnp.where(new_ok, new_scores, -1e30)
    row_top = jnp.maximum(
        jnp.maximum(
            jnp.max(main_scores, axis=1, keepdims=True),
            jnp.max(extra_scores, axis=1, keepdims=True),
        ),
        jnp.max(new_scores, axis=1, keepdims=True),
    )
    main_w = jnp.exp(main_scores - row_top)
    extra_w = jnp.exp(extra_scores - row_top)
    new_w = jnp.exp(new_scores - row_top)
    row_total = (
        jnp.sum(main_w, axis=1, keepdims=True)
        + jnp.sum(extra_w, axis=1, keepdims=True)
        + jnp.sum(new_w, axis=1, keepdims=True)
    )

    def weighted(weights, values):
        return jnp.dot(weights.astype(jnp.bfloat16), values, preferred_element_type=jnp.float32)

    summed = (
        weighted(main_w, mv_ref[...].reshape(main_span, HD))
        + weighted(extra_w, ev_ref[...].reshape(extra_span, HD))
        + weighted(new_w, nv_ref[...])
    )
    out_ref[...] = (summed / row_total).astype(out_ref.dtype)


def grid_attend(live, query, main_pages, main_pos, extra_pages, extra_pos, new_key, new_value):
    rows, width = query.shape
    heads = width // HD
    main_n = main_pages.shape[0]
    extra_n = extra_pages.shape[0]
    grid_spec = pltpu.PrefetchScalarGridSpec(
        num_scalar_prefetch=1,
        grid=(heads, rows // BLOCK_Q),
        in_specs=[
            pl.BlockSpec((1, main_n * PAGE), lambda h, b, live: (0, 0)),
            pl.BlockSpec((1, extra_n * PAGE), lambda h, b, live: (0, 0)),
            pl.BlockSpec((BLOCK_Q, HD), lambda h, b, live: (b, h)),
            pl.BlockSpec((main_n, None, PAGE, HD), lambda h, b, live: (0, 0, 0, h)),
            pl.BlockSpec((main_n, None, PAGE, HD), lambda h, b, live: (0, 1, 0, h)),
            pl.BlockSpec((extra_n, None, PAGE, HD), lambda h, b, live: (0, 0, 0, h)),
            pl.BlockSpec((extra_n, None, PAGE, HD), lambda h, b, live: (0, 1, 0, h)),
            pl.BlockSpec((rows, HD), lambda h, b, live: (0, h)),
            pl.BlockSpec((rows, HD), lambda h, b, live: (0, h)),
        ],
        out_specs=pl.BlockSpec((BLOCK_Q, HD), lambda h, b, live: (b, h)),
    )
    keys_n = (main_n + extra_n) * PAGE + rows
    return pl.pallas_call(
        grid_attend_kernel,
        grid_spec=grid_spec,
        out_shape=jax.ShapeDtypeStruct((rows, width), jnp.bfloat16),
        compiler_params=pltpu.CompilerParams(vmem_limit_bytes=56 * 1024 * 1024),
        cost_estimate=pl.CostEstimate(
            flops=4 * rows * keys_n * width,
            transcendentals=rows * keys_n * heads,
            bytes_accessed=2 * (2 * keys_n * width + 2 * rows * width),
        ),
    )(
        live,
        main_pos.reshape(1, -1),
        extra_pos.reshape(1, -1),
        query,
        main_pages,
        main_pages,
        extra_pages,
        extra_pages,
        new_key,
        new_value,
    )


def swap_kernel(send_ref, recv_ref, send_sems, recv_sems):
    count = send_ref.shape[0]
    me = lax.axis_index("req")
    tp_me = lax.axis_index("tp")
    barrier = pltpu.get_barrier_semaphore()

    def others(fn):
        def step(peer, carry):
            @pl.when(peer != me)
            def _():
                fn(peer)

            return carry

        lax.fori_loop(0, count, step, 0)

    def greet(peer):
        pl.semaphore_signal(barrier, inc=1, device_id=(peer, tp_me), device_id_type=MESH)

    others(greet)
    pl.semaphore_wait(barrier, count - 1)

    def outgoing(peer):
        return pltpu.make_async_remote_copy(
            src_ref=send_ref.at[peer],
            dst_ref=recv_ref.at[me],
            send_sem=send_sems.at[peer],
            recv_sem=recv_sems.at[me],
            device_id=(peer, tp_me),
            device_id_type=MESH,
        )

    def arriving(peer):
        return pltpu.make_async_remote_copy(
            src_ref=send_ref.at[peer],
            dst_ref=recv_ref.at[peer],
            send_sem=send_sems.at[peer],
            recv_sem=recv_sems.at[peer],
            device_id=(peer, tp_me),
            device_id_type=MESH,
        )

    others(lambda peer: outgoing(peer).start())
    recv_ref[pl.ds(me, 1)] = send_ref[pl.ds(me, 1)]
    others(lambda peer: outgoing(peer).wait_send())
    others(lambda peer: arriving(peer).wait_recv())


def swap_pieces(pieces):
    count = pieces.shape[0]
    return pl.pallas_call(
        swap_kernel,
        out_shape=jax.ShapeDtypeStruct(pieces.shape, pieces.dtype),
        in_specs=[pl.BlockSpec(memory_space=pltpu.VMEM)],
        out_specs=pl.BlockSpec(memory_space=pltpu.VMEM),
        scratch_shapes=[pltpu.SemaphoreType.DMA((count,)), pltpu.SemaphoreType.DMA((count,))],
        compiler_params=pltpu.CompilerParams(collective_id=0, has_side_effects=True),
    )(pieces)


def key_positions(entry_of_slot):
    tokens = jnp.arange(PAGE)[None, :]
    return jnp.where(entry_of_slot[:, None] >= 0, entry_of_slot[:, None] * PAGE + tokens, 1 << 30)


def project(hidden_in, qkv_weight, live_len, local_heads, local_width):
    token_rows = hidden_in.astype(jnp.float32)
    centre = jnp.mean(token_rows, axis=-1, keepdims=True)
    centred = token_rows - centre
    spread = jnp.mean(centred * centred, axis=-1, keepdims=True)
    normed = (centred * lax.rsqrt(spread + 1e-05)).astype(jnp.bfloat16)
    united_qkv = jnp.einsum("td,dcf->tcf", normed, qkv_weight, preferred_element_type=jnp.float32)
    positions = (live_len[:, None] + jnp.arange(NEW)[None, :]).astype(jnp.float32).reshape(-1)
    query_rot = rotate(united_qkv[:, 0].reshape(-1, local_heads, HD), positions).astype(
        jnp.bfloat16
    ).reshape(-1, local_width)
    new_key = rotate(united_qkv[:, 1].reshape(-1, local_heads, HD), positions).astype(
        jnp.bfloat16
    ).reshape(-1, local_width)
    new_value = united_qkv[:, 2].astype(jnp.bfloat16)
    return query_rot, new_key, new_value


def exchange_wide(kv_pool, page_slot, holder_rows, rank_all, req_index, req_count):
    capacity = 2
    held_here = holder_rows == req_index
    ranking = jnp.cumsum(held_here.astype(jnp.int32), axis=1) - 1
    picked = held_here[:, :, None] & (ranking[:, :, None] == jnp.arange(capacity)[None, None, :])
    send_slots = jnp.sum(jnp.where(picked, page_slot[:, :, None], 0), axis=1)
    incoming = lax.all_to_all(kv_pool[send_slots], "req", split_axis=0, concat_axis=0, tiled=True)
    incoming = incoming.reshape((req_count * capacity,) + kv_pool.shape[1:])
    own_holders = holder_rows[req_index]
    own_rank = rank_all[req_index]
    slot_of_entry = own_holders * capacity + own_rank
    hit = slot_of_entry[None, :] == jnp.arange(req_count * capacity)[:, None]
    entry_of_slot = jnp.max(jnp.where(hit, jnp.arange(hit.shape[1])[None, :], -1), axis=1)
    main_pos = key_positions(entry_of_slot)
    extra_pages = incoming[:1]
    extra_pos = key_positions(jnp.full((1,), -1, jnp.int32))
    return incoming, main_pos, extra_pages, extra_pos


def exchange_relay(kv_pool, page_slot, holder_rows, rank_all, req_index, req_count):
    rows, entries = holder_rows.shape
    spill = rank_all > 0
    frag = PAGE // req_count
    width = kv_pool.shape[-1]
    spill_flat = spill.reshape(-1)
    holders_flat = holder_rows.reshape(-1)
    slots_flat = page_slot.reshape(-1)
    spill_i = spill.astype(jnp.int32)
    named = (holder_rows[:, :, None] == jnp.arange(req_count)[None, None, :]).astype(jnp.int32)
    row_spills = jnp.sum(spill_i[:, :, None] * named, axis=1)
    before = jnp.cumsum(row_spills, axis=0) - row_spills
    holder_order = jnp.sum(named * before[:, None, :], axis=2).reshape(-1)
    req_order = jnp.cumsum(spill_i, axis=1) - spill_i
    first_hit = (holder_rows == req_index) & (rank_all == 0)
    send_slots = jnp.sum(jnp.where(first_hit, page_slot, 0), axis=1)
    wanted = jnp.arange(RELAY_A)
    match_a = (
        spill_flat[None, :]
        & (holders_flat[None, :] == req_index)
        & (holder_order[None, :] == wanted[:, None])
    )
    slot_a = jnp.sum(jnp.where(match_a, slots_flat[None, :], 0), axis=1)
    pieces = (
        kv_pool[slot_a]
        .reshape(RELAY_A, 2, req_count, frag, width)
        .transpose(2, 1, 0, 3, 4)
        .reshape(req_count, 2, RELAY_A * frag, width)
    )
    padded = jnp.pad(kv_pool, ((0, 0), (0, 0), (0, RELAY_A * frag), (0, 0)))
    outgoing = padded[send_slots].at[:, :, PAGE:, :].set(pieces)
    incoming = lax.all_to_all(outgoing, "req", split_axis=0, concat_axis=0, tiled=True)
    relayed = (
        incoming[:, :, PAGE:]
        .reshape(req_count, 2, RELAY_A, frag, width)
        .transpose(0, 2, 1, 3, 4)
        .reshape(req_count * RELAY_A, 2, frag, width)
    )
    match_b = spill[:, None, :] & (req_order[:, None, :] == jnp.arange(RELAY_B)[None, :, None])
    src_holder = jnp.sum(jnp.where(match_b, holder_rows[:, None, :], 0), axis=2)
    src_index = jnp.sum(
        jnp.where(match_b, holder_order.reshape(rows, entries)[:, None, :], 0), axis=2
    )
    extra = relayed[src_holder * RELAY_A + jnp.clip(src_index, 0, RELAY_A - 1)]
    extra = extra.transpose(0, 2, 1, 3, 4).reshape(rows, 2, RELAY_B * frag, width)
    returned = swap_pieces(extra)
    extra_pages = (
        returned.reshape(req_count, 2, RELAY_B, frag, width)
        .transpose(2, 1, 0, 3, 4)
        .reshape(RELAY_B, 2, PAGE, width)
    )
    own_holders = holder_rows[req_index]
    own_first = rank_all[req_index] == 0
    entry_ids = jnp.arange(entries)
    main_hit = own_first[None, :] & (own_holders[None, :] == jnp.arange(req_count)[:, None])
    main_pos = key_positions(jnp.max(jnp.where(main_hit, entry_ids[None, :], -1), axis=1))
    extra_hit = (~own_first)[None, :] & (
        req_order[req_index][None, :] == jnp.arange(RELAY_B)[:, None]
    )
    extra_pos = key_positions(jnp.max(jnp.where(extra_hit, entry_ids[None, :], -1), axis=1))
    return incoming, main_pos, extra_pages, extra_pos


def body(hidden_in, qkv_weight, out_weight, kv_pool, cached_len, page_slot, page_holder, cont_flag):
    req_count = lax.axis_size("req")
    req_index = lax.axis_index("req")
    local_width = qkv_weight.shape[2]
    local_heads = local_width // HD
    holder_rows = page_holder[:, :, 0]
    entries = holder_rows.shape[1]
    same_holder = holder_rows[:, :, None] == holder_rows[:, None, :]
    earlier = jnp.arange(entries)[None, None, :] < jnp.arange(entries)[None, :, None]
    rank_all = jnp.sum((same_holder & earlier).astype(jnp.int32), axis=2)
    spill = (rank_all > 0).astype(jnp.int32)
    relay_fits = (jnp.max(jnp.sum(spill, axis=1)) <= RELAY_B) & (
        jnp.max(jnp.sum(spill[:, :, None] * (holder_rows[:, :, None] == jnp.arange(req_count)), axis=(0, 1)))
        <= RELAY_A
    )
    lengths = lax.dynamic_slice_in_dim(cached_len, req_index, 1)
    flags = lax.dynamic_slice_in_dim(cont_flag, req_index, 1)
    live_len = lengths * flags
    main_pages, main_pos, extra_pages, extra_pos = exchange_relay(
        kv_pool, page_slot, holder_rows, rank_all, req_index, req_count
    )
    query_rot, new_key, new_value = project(hidden_in, qkv_weight, live_len, local_heads, local_width)
    attended = attend(
        live_len, query_rot, main_pages, main_pos, extra_pages, extra_pos, new_key, new_value
    )

    def keep(ops):
        return ops[0]

    def redo(ops):
        _, query, key, value, pool, slots, holders, ranks, live = ops
        pages, pos, extra, extra_at = exchange_wide(pool, slots, holders, ranks, req_index, req_count)
        return grid_attend(live, query, pages, pos, extra, extra_at, key, value)

    attended = lax.cond(
        relay_fits,
        keep,
        redo,
        (attended, query_rot, new_key, new_value, kv_pool, page_slot, holder_rows, rank_all, live_len),
    )
    head_term = jnp.dot(attended, out_weight, preferred_element_type=jnp.float32)
    return lax.psum_scatter(head_term.astype(jnp.bfloat16), "tp", scatter_dimension=0, tiled=True)


def solution(mesh):
    in_specs = (
        P("req", None),
        P(None, None, "tp"),
        P("tp", None),
        P("req", None, None, "tp"),
        P(),
        P(),
        P(),
        P(),
    )
    out_specs = P(("req", "tp"), None)
    return jax.shard_map(body, mesh=mesh, in_specs=in_specs, out_specs=out_specs, check_vma=False)
```

```python
import functools

import jax
import jax.numpy as jnp
from jax import lax
from jax.experimental import pallas as pl
from jax.experimental.pallas import tpu as pltpu
from jax.sharding import PartitionSpec as P

HD = 128
NEW = 1024
PAGE = 128
MAXP = 32
BLOCK_Q = 256
MESH = pl.DeviceIdType.MESH
RELAY_A = 8
RELAY_B = 1


def rotate(feature, position):
    half_width = feature.shape[-1] // 2
    indices = jnp.arange(half_width).astype(jnp.float32)
    inverse = jnp.exp(indices * (-2.0 / feature.shape[-1]) * jnp.log(jnp.float32(10000.0)))
    angles = position[:, None, None] * inverse[None, None, :]
    cosine = jnp.cos(angles)
    sine_part = jnp.sin(angles)
    first_half = feature[..., :half_width]
    second_half = feature[..., half_width:]
    return jnp.concatenate(
        [
            first_half * cosine - second_half * sine_part,
            second_half * cosine + first_half * sine_part,
        ],
        axis=-1,
    )


def attend_kernel(
    live_ref, kpm_ref, kpe_ref, q_ref, mk_ref, mv_ref, ek_ref, ev_ref, nk_ref, nv_ref, out_ref
):
    live = live_ref[0]
    main_span = mk_ref.shape[0] * mk_ref.shape[1]
    extra_span = ek_ref.shape[0] * ek_ref.shape[1]
    contract = (((1,), (1,)), ((), ()))
    scale = HD ** (-0.5)
    main_ok = kpm_ref[...] < live
    extra_ok = kpe_ref[...] < live
    diag_ok = lax.broadcasted_iota(jnp.int32, (BLOCK_Q, BLOCK_Q), 1) <= lax.broadcasted_iota(
        jnp.int32, (BLOCK_Q, BLOCK_Q), 0
    )

    def weighted(weights, values):
        return jnp.dot(weights.astype(jnp.bfloat16), values, preferred_element_type=jnp.float32)

    def block_body(block, carry):
        start = pl.multiple_of(block * BLOCK_Q, BLOCK_Q)
        query = q_ref[pl.ds(start, BLOCK_Q), :]

        def scores(keys):
            return (
                lax.dot_general(query, keys, contract, preferred_element_type=jnp.float32) * scale
            )

        def chunk(index):
            return pl.ds(pl.multiple_of(index * BLOCK_Q, BLOCK_Q), BLOCK_Q)

        main_scores = jnp.where(main_ok, scores(mk_ref[...].reshape(main_span, HD)), -1e30)
        extra_scores = jnp.where(extra_ok, scores(ek_ref[...].reshape(extra_span, HD)), -1e30)
        diag_scores = jnp.where(diag_ok, scores(nk_ref[chunk(block), :]), -1e30)
        row_top = jnp.maximum(
            jnp.maximum(
                jnp.max(main_scores, axis=1, keepdims=True),
                jnp.max(extra_scores, axis=1, keepdims=True),
            ),
            jnp.max(diag_scores, axis=1, keepdims=True),
        )

        def past_top(index, top):
            return jnp.maximum(
                top, jnp.max(scores(nk_ref[chunk(index), :]), axis=1, keepdims=True)
            )

        row_top = lax.fori_loop(0, block, past_top, row_top)
        main_w = jnp.exp(main_scores - row_top)
        extra_w = jnp.exp(extra_scores - row_top)
        diag_w = jnp.exp(diag_scores - row_top)
        row_total = (
            jnp.sum(main_w, axis=1, keepdims=True)
            + jnp.sum(extra_w, axis=1, keepdims=True)
            + jnp.sum(diag_w, axis=1, keepdims=True)
        )
        summed = (
            weighted(main_w, mv_ref[...].reshape(main_span, HD))
            + weighted(extra_w, ev_ref[...].reshape(extra_span, HD))
            + weighted(diag_w, nv_ref[chunk(block), :])
        )

        def past_sum(index, sums):
            total, acc = sums
            past_w = jnp.exp(scores(nk_ref[chunk(index), :]) - row_top)
            return (
                total + jnp.sum(past_w, axis=1, keepdims=True),
                acc + weighted(past_w, nv_ref[chunk(index), :]),
            )

        row_total, summed = lax.fori_loop(0, block, past_sum, (row_total, summed))
        out_ref[pl.ds(start, BLOCK_Q), :] = (summed / row_total).astype(out_ref.dtype)
        return carry

    lax.fori_loop(0, q_ref.shape[0] // BLOCK_Q, block_body, 0)


def attend(live, query, main_pages, main_pos, extra_pages, extra_pos, new_key, new_value):
    rows, width = query.shape
    heads = width // HD
    main_n = main_pages.shape[0]
    extra_n = extra_pages.shape[0]
    grid_spec = pltpu.PrefetchScalarGridSpec(
        num_scalar_prefetch=1,
        grid=(heads,),
        in_specs=[
            pl.BlockSpec((1, main_n * PAGE), lambda h, live: (0, 0)),
            pl.BlockSpec((1, extra_n * PAGE), lambda h, live: (0, 0)),
            pl.BlockSpec((rows, HD), lambda h, live: (0, h)),
            pl.BlockSpec((main_n, None, PAGE, HD), lambda h, live: (0, 0, 0, h)),
            pl.BlockSpec((main_n, None, PAGE, HD), lambda h, live: (0, 1, 0, h)),
            pl.BlockSpec((extra_n, None, PAGE, HD), lambda h, live: (0, 0, 0, h)),
            pl.BlockSpec((extra_n, None, PAGE, HD), lambda h, live: (0, 1, 0, h)),
            pl.BlockSpec((rows, HD), lambda h, live: (0, h)),
            pl.BlockSpec((rows, HD), lambda h, live: (0, h)),
        ],
        out_specs=pl.BlockSpec((rows, HD), lambda h, live: (0, h)),
    )
    keys_n = (main_n + extra_n) * PAGE + rows // 2
    return pl.pallas_call(
        attend_kernel,
        grid_spec=grid_spec,
        out_shape=jax.ShapeDtypeStruct((rows, width), jnp.bfloat16),
        compiler_params=pltpu.CompilerParams(vmem_limit_bytes=56 * 1024 * 1024),
        cost_estimate=pl.CostEstimate(
            flops=4 * rows * keys_n * width,
            transcendentals=rows * keys_n * heads,
            bytes_accessed=2 * (2 * keys_n * width + 2 * rows * width),
        ),
    )(
        live,
        main_pos.reshape(1, -1),
        extra_pos.reshape(1, -1),
        query,
        main_pages,
        main_pages,
        extra_pages,
        extra_pages,
        new_key,
        new_value,
    )


def grid_attend_kernel(
    live_ref, kpm_ref, kpe_ref, q_ref, mk_ref, mv_ref, ek_ref, ev_ref, nk_ref, nv_ref, out_ref
):
    block = pl.program_id(1)
    live = live_ref[0]
    main_span = mk_ref.shape[0] * mk_ref.shape[1]
    extra_span = ek_ref.shape[0] * ek_ref.shape[1]
    query = q_ref[...]
    contract = (((1,), (1,)), ((), ()))
    scale = HD ** (-0.5)

    def scores(keys):
        return lax.dot_general(query, keys, contract, preferred_element_type=jnp.float32) * scale

    main_scores = scores(mk_ref[...].reshape(main_span, HD))
    extra_scores = scores(ek_ref[...].reshape(extra_span, HD))
    new_scores = scores(nk_ref[...])
    main_ok = kpm_ref[...] < live
    extra_ok = kpe_ref[...] < live
    query_pos = block * BLOCK_Q + lax.broadcasted_iota(jnp.int32, new_scores.shape, 0)
    new_ok = lax.broadcasted_iota(jnp.int32, new_scores.shape, 1) <= query_pos
    main_scores = jnp.where(main_ok, main_scores, -1e30)
    extra_scores = jnp.where(extra_ok, extra_scores, -1e30)
    new_scores = jnp.where(new_ok, new_scores, -1e30)
    row_top = jnp.maximum(
        jnp.maximum(
            jnp.max(main_scores, axis=1, keepdims=True),
            jnp.max(extra_scores, axis=1, keepdims=True),
        ),
        jnp.max(new_scores, axis=1, keepdims=True),
    )
    main_w = jnp.exp(main_scores - row_top)
    extra_w = jnp.exp(extra_scores - row_top)
    new_w = jnp.exp(new_scores - row_top)
    row_total = (
        jnp.sum(main_w, axis=1, keepdims=True)
        + jnp.sum(extra_w, axis=1, keepdims=True)
        + jnp.sum(new_w, axis=1, keepdims=True)
    )

    def weighted(weights, values):
        return jnp.dot(weights.astype(jnp.bfloat16), values, preferred_element_type=jnp.float32)

    summed = (
        weighted(main_w, mv_ref[...].reshape(main_span, HD))
        + weighted(extra_w, ev_ref[...].reshape(extra_span, HD))
        + weighted(new_w, nv_ref[...])
    )
    out_ref[...] = (summed / row_total).astype(out_ref.dtype)


def grid_attend(live, query, main_pages, main_pos, extra_pages, extra_pos, new_key, new_value):
    rows, width = query.shape
    heads = width // HD
    main_n = main_pages.shape[0]
    extra_n = extra_pages.shape[0]
    grid_spec = pltpu.PrefetchScalarGridSpec(
        num_scalar_prefetch=1,
        grid=(heads, rows // BLOCK_Q),
        in_specs=[
            pl.BlockSpec((1, main_n * PAGE), lambda h, b, live: (0, 0)),
            pl.BlockSpec((1, extra_n * PAGE), lambda h, b, live: (0, 0)),
            pl.BlockSpec((BLOCK_Q, HD), lambda h, b, live: (b, h)),
            pl.BlockSpec((main_n, None, PAGE, HD), lambda h, b, live: (0, 0, 0, h)),
            pl.BlockSpec((main_n, None, PAGE, HD), lambda h, b, live: (0, 1, 0, h)),
            pl.BlockSpec((extra_n, None, PAGE, HD), lambda h, b, live: (0, 0, 0, h)),
            pl.BlockSpec((extra_n, None, PAGE, HD), lambda h, b, live: (0, 1, 0, h)),
            pl.BlockSpec((rows, HD), lambda h, b, live: (0, h)),
            pl.BlockSpec((rows, HD), lambda h, b, live: (0, h)),
        ],
        out_specs=pl.BlockSpec((BLOCK_Q, HD), lambda h, b, live: (b, h)),
    )
    keys_n = (main_n + extra_n) * PAGE + rows
    return pl.pallas_call(
        grid_attend_kernel,
        grid_spec=grid_spec,
        out_shape=jax.ShapeDtypeStruct((rows, width), jnp.bfloat16),
        compiler_params=pltpu.CompilerParams(vmem_limit_bytes=56 * 1024 * 1024),
        cost_estimate=pl.CostEstimate(
            flops=4 * rows * keys_n * width,
            transcendentals=rows * keys_n * heads,
            bytes_accessed=2 * (2 * keys_n * width + 2 * rows * width),
        ),
    )(
        live,
        main_pos.reshape(1, -1),
        extra_pos.reshape(1, -1),
        query,
        main_pages,
        main_pages,
        extra_pages,
        extra_pages,
        new_key,
        new_value,
    )


def swap_kernel(send_ref, recv_ref, send_sems, recv_sems):
    count = send_ref.shape[0]
    me = lax.axis_index("req")
    tp_me = lax.axis_index("tp")
    barrier = pltpu.get_barrier_semaphore()

    def others(fn):
        def step(peer, carry):
            @pl.when(peer != me)
            def _():
                fn(peer)

            return carry

        lax.fori_loop(0, count, step, 0)

    def greet(peer):
        pl.semaphore_signal(barrier, inc=1, device_id=(peer, tp_me), device_id_type=MESH)

    others(greet)
    pl.semaphore_wait(barrier, count - 1)

    def outgoing(peer):
        return pltpu.make_async_remote_copy(
            src_ref=send_ref.at[peer],
            dst_ref=recv_ref.at[me],
            send_sem=send_sems.at[peer],
            recv_sem=recv_sems.at[me],
            device_id=(peer, tp_me),
            device_id_type=MESH,
        )

    def arriving(peer):
        return pltpu.make_async_remote_copy(
            src_ref=send_ref.at[peer],
            dst_ref=recv_ref.at[peer],
            send_sem=send_sems.at[peer],
            recv_sem=recv_sems.at[peer],
            device_id=(peer, tp_me),
            device_id_type=MESH,
        )

    others(lambda peer: outgoing(peer).start())
    recv_ref[pl.ds(me, 1)] = send_ref[pl.ds(me, 1)]
    others(lambda peer: outgoing(peer).wait_send())
    others(lambda peer: arriving(peer).wait_recv())


def swap_pieces(pieces):
    count = pieces.shape[0]
    return pl.pallas_call(
        swap_kernel,
        out_shape=jax.ShapeDtypeStruct(pieces.shape, pieces.dtype),
        in_specs=[pl.BlockSpec(memory_space=pltpu.VMEM)],
        out_specs=pl.BlockSpec(memory_space=pltpu.VMEM),
        scratch_shapes=[pltpu.SemaphoreType.DMA((count,)), pltpu.SemaphoreType.DMA((count,))],
        compiler_params=pltpu.CompilerParams(collective_id=0, has_side_effects=True),
    )(pieces)


def key_positions(entry_of_slot):
    tokens = jnp.arange(PAGE)[None, :]
    return jnp.where(entry_of_slot[:, None] >= 0, entry_of_slot[:, None] * PAGE + tokens, 1 << 30)


def project(hidden_in, qkv_weight, live_len, local_heads, local_width):
    token_rows = hidden_in.astype(jnp.float32)
    centre = jnp.mean(token_rows, axis=-1, keepdims=True)
    centred = token_rows - centre
    spread = jnp.mean(centred * centred, axis=-1, keepdims=True)
    normed = (centred * lax.rsqrt(spread + 1e-05)).astype(jnp.bfloat16)
    united_qkv = jnp.einsum("td,dcf->tcf", normed, qkv_weight, preferred_element_type=jnp.float32)
    positions = (live_len[:, None] + jnp.arange(NEW)[None, :]).astype(jnp.float32).reshape(-1)
    query_rot = rotate(united_qkv[:, 0].reshape(-1, local_heads, HD), positions).astype(
        jnp.bfloat16
    ).reshape(-1, local_width)
    new_key = rotate(united_qkv[:, 1].reshape(-1, local_heads, HD), positions).astype(
        jnp.bfloat16
    ).reshape(-1, local_width)
    new_value = united_qkv[:, 2].astype(jnp.bfloat16)
    return query_rot, new_key, new_value


def exchange_wide(kv_pool, page_slot, holder_rows, rank_all, req_index, req_count):
    capacity = 2
    held_here = holder_rows == req_index
    ranking = jnp.cumsum(held_here.astype(jnp.int32), axis=1) - 1
    picked = held_here[:, :, None] & (ranking[:, :, None] == jnp.arange(capacity)[None, None, :])
    send_slots = jnp.sum(jnp.where(picked, page_slot[:, :, None], 0), axis=1)
    incoming = lax.all_to_all(kv_pool[send_slots], "req", split_axis=0, concat_axis=0, tiled=True)
    incoming = incoming.reshape((req_count * capacity,) + kv_pool.shape[1:])
    own_holders = holder_rows[req_index]
    own_rank = rank_all[req_index]
    slot_of_entry = own_holders * capacity + own_rank
    hit = slot_of_entry[None, :] == jnp.arange(req_count * capacity)[:, None]
    entry_of_slot = jnp.max(jnp.where(hit, jnp.arange(hit.shape[1])[None, :], -1), axis=1)
    main_pos = key_positions(entry_of_slot)
    extra_pages = incoming[:1]
    extra_pos = key_positions(jnp.full((1,), -1, jnp.int32))
    return incoming, main_pos, extra_pages, extra_pos


def exchange_relay(kv_pool, page_slot, holder_rows, rank_all, req_index, req_count):
    rows, entries = holder_rows.shape
    spill = rank_all > 0
    frag = PAGE // req_count
    width = kv_pool.shape[-1]
    spill_flat = spill.reshape(-1)
    holders_flat = holder_rows.reshape(-1)
    slots_flat = page_slot.reshape(-1)
    spill_i = spill.astype(jnp.int32)
    named = (holder_rows[:, :, None] == jnp.arange(req_count)[None, None, :]).astype(jnp.int32)
    row_spills = jnp.sum(spill_i[:, :, None] * named, axis=1)
    before = jnp.cumsum(row_spills, axis=0) - row_spills
    holder_order = jnp.sum(named * before[:, None, :], axis=2).reshape(-1)
    req_order = jnp.cumsum(spill_i, axis=1) - spill_i
    first_hit = (holder_rows == req_index) & (rank_all == 0)
    send_slots = jnp.sum(jnp.where(first_hit, page_slot, 0), axis=1)
    wanted = jnp.arange(RELAY_A)
    match_a = (
        spill_flat[None, :]
        & (holders_flat[None, :] == req_index)
        & (holder_order[None, :] == wanted[:, None])
    )
    slot_a = jnp.sum(jnp.where(match_a, slots_flat[None, :], 0), axis=1)
    pieces = (
        kv_pool[slot_a]
        .reshape(RELAY_A, 2, req_count, frag, width)
        .transpose(2, 1, 0, 3, 4)
        .reshape(req_count, 2, RELAY_A * frag, width)
    )
    padded = jnp.pad(kv_pool, ((0, 0), (0, 0), (0, RELAY_A * frag), (0, 0)))
    outgoing = padded[send_slots].at[:, :, PAGE:, :].set(pieces)
    incoming = lax.all_to_all(outgoing, "req", split_axis=0, concat_axis=0, tiled=True)
    relayed = (
        incoming[:, :, PAGE:]
        .reshape(req_count, 2, RELAY_A, frag, width)
        .transpose(0, 2, 1, 3, 4)
        .reshape(req_count * RELAY_A, 2, frag, width)
    )
    match_b = spill[:, None, :] & (req_order[:, None, :] == jnp.arange(RELAY_B)[None, :, None])
    src_holder = jnp.sum(jnp.where(match_b, holder_rows[:, None, :], 0), axis=2)
    src_index = jnp.sum(
        jnp.where(match_b, holder_order.reshape(rows, entries)[:, None, :], 0), axis=2
    )
    extra = relayed[src_holder * RELAY_A + jnp.clip(src_index, 0, RELAY_A - 1)]
    extra = extra.transpose(0, 2, 1, 3, 4).reshape(rows, 2, RELAY_B * frag, width)
    returned = swap_pieces(extra)
    extra_pages = (
        returned.reshape(req_count, 2, RELAY_B, frag, width)
        .transpose(2, 1, 0, 3, 4)
        .reshape(RELAY_B, 2, PAGE, width)
    )
    own_holders = holder_rows[req_index]
    own_first = rank_all[req_index] == 0
    entry_ids = jnp.arange(entries)
    main_hit = own_first[None, :] & (own_holders[None, :] == jnp.arange(req_count)[:, None])
    main_pos = key_positions(jnp.max(jnp.where(main_hit, entry_ids[None, :], -1), axis=1))
    extra_hit = (~own_first)[None, :] & (
        req_order[req_index][None, :] == jnp.arange(RELAY_B)[:, None]
    )
    extra_pos = key_positions(jnp.max(jnp.where(extra_hit, entry_ids[None, :], -1), axis=1))
    return incoming, main_pos, extra_pages, extra_pos


def body(hidden_in, qkv_weight, out_weight, kv_pool, cached_len, page_slot, page_holder, cont_flag):
    req_count = lax.axis_size("req")
    req_index = lax.axis_index("req")
    local_width = qkv_weight.shape[2]
    local_heads = local_width // HD
    holder_rows = page_holder[:, :, 0]
    entries = holder_rows.shape[1]
    same_holder = holder_rows[:, :, None] == holder_rows[:, None, :]
    earlier = jnp.arange(entries)[None, None, :] < jnp.arange(entries)[None, :, None]
    rank_all = jnp.sum((same_holder & earlier).astype(jnp.int32), axis=2)
    spill = (rank_all > 0).astype(jnp.int32)
    relay_fits = (jnp.max(jnp.sum(spill, axis=1)) <= RELAY_B) & (
        jnp.max(jnp.sum(spill[:, :, None] * (holder_rows[:, :, None] == jnp.arange(req_count)), axis=(0, 1)))
        <= RELAY_A
    )
    lengths = lax.dynamic_slice_in_dim(cached_len, req_index, 1)
    flags = lax.dynamic_slice_in_dim(cont_flag, req_index, 1)
    live_len = lengths * flags
    main_pages, main_pos, extra_pages, extra_pos = exchange_relay(
        kv_pool, page_slot, holder_rows, rank_all, req_index, req_count
    )
    query_rot, new_key, new_value = project(hidden_in, qkv_weight, live_len, local_heads, local_width)
    attended = attend(
        live_len, query_rot, main_pages, main_pos, extra_pages, extra_pos, new_key, new_value
    )

    def keep(ops):
        return ops[0]

    def redo(ops):
        _, query, key, value, pool, slots, holders, ranks, live = ops
        pages, pos, extra, extra_at = exchange_wide(pool, slots, holders, ranks, req_index, req_count)
        return grid_attend(live, query, pages, pos, extra, extra_at, key, value)

    attended = lax.cond(
        relay_fits,
        keep,
        redo,
        (attended, query_rot, new_key, new_value, kv_pool, page_slot, holder_rows, rank_all, live_len),
    )
    head_term = jnp.dot(attended, out_weight, preferred_element_type=jnp.float32)
    return lax.psum_scatter(head_term.astype(jnp.bfloat16), "tp", scatter_dimension=0, tiled=True)


def solution(mesh):
    in_specs = (
        P("req", None),
        P(None, None, "tp"),
        P("tp", None),
        P("req", None, None, "tp"),
        P(),
        P(),
        P(),
        P(),
    )
    out_specs = P(("req", "tp"), None)
    return jax.shard_map(body, mesh=mesh, in_specs=in_specs, out_specs=out_specs, check_vma=False)
```

```python
import functools

import jax
import jax.numpy as jnp
from jax import lax
from jax.experimental import pallas as pl
from jax.experimental.pallas import tpu as pltpu
from jax.sharding import PartitionSpec as P

HD = 128
NEW = 1024
PAGE = 128
MAXP = 32
BLOCK_Q = 256
MESH = pl.DeviceIdType.MESH
RELAY_A = 8
RELAY_B = 1


def rotate(feature, position):
    half_width = feature.shape[-1] // 2
    indices = jnp.arange(half_width).astype(jnp.float32)
    inverse = jnp.exp(indices * (-2.0 / feature.shape[-1]) * jnp.log(jnp.float32(10000.0)))
    angles = position[:, None, None] * inverse[None, None, :]
    cosine = jnp.cos(angles)
    sine_part = jnp.sin(angles)
    first_half = feature[..., :half_width]
    second_half = feature[..., half_width:]
    return jnp.concatenate(
        [
            first_half * cosine - second_half * sine_part,
            second_half * cosine + first_half * sine_part,
        ],
        axis=-1,
    )


def attend_kernel(
    live_ref, kpm_ref, kpe_ref, q_ref, mk_ref, mv_ref, ek_ref, ev_ref, nk_ref, nv_ref, out_ref
):
    live = live_ref[0]
    main_span = mk_ref.shape[0] * mk_ref.shape[1]
    extra_span = ek_ref.shape[0] * ek_ref.shape[1]
    contract = (((1,), (1,)), ((), ()))
    scale = HD ** (-0.5)
    main_ok = kpm_ref[...] < live
    extra_ok = kpe_ref[...] < live

    for block in range(q_ref.shape[0] // BLOCK_Q):
        rows = pl.ds(block * BLOCK_Q, BLOCK_Q)
        seen = pl.ds(0, (block + 1) * BLOCK_Q)
        query = q_ref[rows, :]

        def scores(keys):
            return (
                lax.dot_general(query, keys, contract, preferred_element_type=jnp.float32) * scale
            )

        main_scores = scores(mk_ref[...].reshape(main_span, HD))
        extra_scores = scores(ek_ref[...].reshape(extra_span, HD))
        new_scores = scores(nk_ref[seen, :])
        query_pos = block * BLOCK_Q + lax.broadcasted_iota(jnp.int32, new_scores.shape, 0)
        new_ok = lax.broadcasted_iota(jnp.int32, new_scores.shape, 1) <= query_pos
        main_scores = jnp.where(main_ok, main_scores, -1e30)
        extra_scores = jnp.where(extra_ok, extra_scores, -1e30)
        new_scores = jnp.where(new_ok, new_scores, -1e30)
        row_top = jnp.maximum(
            jnp.maximum(
                jnp.max(main_scores, axis=1, keepdims=True),
                jnp.max(extra_scores, axis=1, keepdims=True),
            ),
            jnp.max(new_scores, axis=1, keepdims=True),
        )
        main_w = jnp.exp(main_scores - row_top)
        extra_w = jnp.exp(extra_scores - row_top)
        new_w = jnp.exp(new_scores - row_top)
        row_total = (
            jnp.sum(main_w, axis=1, keepdims=True)
            + jnp.sum(extra_w, axis=1, keepdims=True)
            + jnp.sum(new_w, axis=1, keepdims=True)
        )

        def weighted(weights, values):
            return jnp.dot(
                weights.astype(jnp.bfloat16), values, preferred_element_type=jnp.float32
            )

        summed = (
            weighted(main_w, mv_ref[...].reshape(main_span, HD))
            + weighted(extra_w, ev_ref[...].reshape(extra_span, HD))
            + weighted(new_w, nv_ref[seen, :])
        )
        out_ref[rows, :] = (summed / row_total).astype(out_ref.dtype)


def attend(live, query, main_pages, main_pos, extra_pages, extra_pos, new_key, new_value):
    rows, width = query.shape
    heads = width // HD
    main_n = main_pages.shape[0]
    extra_n = extra_pages.shape[0]
    grid_spec = pltpu.PrefetchScalarGridSpec(
        num_scalar_prefetch=1,
        grid=(heads,),
        in_specs=[
            pl.BlockSpec((1, main_n * PAGE), lambda h, live: (0, 0)),
            pl.BlockSpec((1, extra_n * PAGE), lambda h, live: (0, 0)),
            pl.BlockSpec((rows, HD), lambda h, live: (0, h)),
            pl.BlockSpec((main_n, None, PAGE, HD), lambda h, live: (0, 0, 0, h)),
            pl.BlockSpec((main_n, None, PAGE, HD), lambda h, live: (0, 1, 0, h)),
            pl.BlockSpec((extra_n, None, PAGE, HD), lambda h, live: (0, 0, 0, h)),
            pl.BlockSpec((extra_n, None, PAGE, HD), lambda h, live: (0, 1, 0, h)),
            pl.BlockSpec((rows, HD), lambda h, live: (0, h)),
            pl.BlockSpec((rows, HD), lambda h, live: (0, h)),
        ],
        out_specs=pl.BlockSpec((rows, HD), lambda h, live: (0, h)),
    )
    keys_n = (main_n + extra_n) * PAGE + rows // 2
    return pl.pallas_call(
        attend_kernel,
        grid_spec=grid_spec,
        out_shape=jax.ShapeDtypeStruct((rows, width), jnp.bfloat16),
        compiler_params=pltpu.CompilerParams(vmem_limit_bytes=56 * 1024 * 1024),
        cost_estimate=pl.CostEstimate(
            flops=4 * rows * keys_n * width,
            transcendentals=rows * keys_n * heads,
            bytes_accessed=2 * (2 * keys_n * width + 2 * rows * width),
        ),
    )(
        live,
        main_pos.reshape(1, -1),
        extra_pos.reshape(1, -1),
        query,
        main_pages,
        main_pages,
        extra_pages,
        extra_pages,
        new_key,
        new_value,
    )


def grid_attend_kernel(
    live_ref, kpm_ref, kpe_ref, q_ref, mk_ref, mv_ref, ek_ref, ev_ref, nk_ref, nv_ref, out_ref
):
    block = pl.program_id(1)
    live = live_ref[0]
    main_span = mk_ref.shape[0] * mk_ref.shape[1]
    extra_span = ek_ref.shape[0] * ek_ref.shape[1]
    query = q_ref[...]
    contract = (((1,), (1,)), ((), ()))
    scale = HD ** (-0.5)

    def scores(keys):
        return lax.dot_general(query, keys, contract, preferred_element_type=jnp.float32) * scale

    main_scores = scores(mk_ref[...].reshape(main_span, HD))
    extra_scores = scores(ek_ref[...].reshape(extra_span, HD))
    new_scores = scores(nk_ref[...])
    main_ok = kpm_ref[...] < live
    extra_ok = kpe_ref[...] < live
    query_pos = block * BLOCK_Q + lax.broadcasted_iota(jnp.int32, new_scores.shape, 0)
    new_ok = lax.broadcasted_iota(jnp.int32, new_scores.shape, 1) <= query_pos
    main_scores = jnp.where(main_ok, main_scores, -1e30)
    extra_scores = jnp.where(extra_ok, extra_scores, -1e30)
    new_scores = jnp.where(new_ok, new_scores, -1e30)
    row_top = jnp.maximum(
        jnp.maximum(
            jnp.max(main_scores, axis=1, keepdims=True),
            jnp.max(extra_scores, axis=1, keepdims=True),
        ),
        jnp.max(new_scores, axis=1, keepdims=True),
    )
    main_w = jnp.exp(main_scores - row_top)
    extra_w = jnp.exp(extra_scores - row_top)
    new_w = jnp.exp(new_scores - row_top)
    row_total = (
        jnp.sum(main_w, axis=1, keepdims=True)
        + jnp.sum(extra_w, axis=1, keepdims=True)
        + jnp.sum(new_w, axis=1, keepdims=True)
    )

    def weighted(weights, values):
        return jnp.dot(weights.astype(jnp.bfloat16), values, preferred_element_type=jnp.float32)

    summed = (
        weighted(main_w, mv_ref[...].reshape(main_span, HD))
        + weighted(extra_w, ev_ref[...].reshape(extra_span, HD))
        + weighted(new_w, nv_ref[...])
    )
    out_ref[...] = (summed / row_total).astype(out_ref.dtype)


def grid_attend(live, query, main_pages, main_pos, extra_pages, extra_pos, new_key, new_value):
    rows, width = query.shape
    heads = width // HD
    main_n = main_pages.shape[0]
    extra_n = extra_pages.shape[0]
    grid_spec = pltpu.PrefetchScalarGridSpec(
        num_scalar_prefetch=1,
        grid=(heads, rows // BLOCK_Q),
        in_specs=[
            pl.BlockSpec((1, main_n * PAGE), lambda h, b, live: (0, 0)),
            pl.BlockSpec((1, extra_n * PAGE), lambda h, b, live: (0, 0)),
            pl.BlockSpec((BLOCK_Q, HD), lambda h, b, live: (b, h)),
            pl.BlockSpec((main_n, None, PAGE, HD), lambda h, b, live: (0, 0, 0, h)),
            pl.BlockSpec((main_n, None, PAGE, HD), lambda h, b, live: (0, 1, 0, h)),
            pl.BlockSpec((extra_n, None, PAGE, HD), lambda h, b, live: (0, 0, 0, h)),
            pl.BlockSpec((extra_n, None, PAGE, HD), lambda h, b, live: (0, 1, 0, h)),
            pl.BlockSpec((rows, HD), lambda h, b, live: (0, h)),
            pl.BlockSpec((rows, HD), lambda h, b, live: (0, h)),
        ],
        out_specs=pl.BlockSpec((BLOCK_Q, HD), lambda h, b, live: (b, h)),
    )
    keys_n = (main_n + extra_n) * PAGE + rows
    return pl.pallas_call(
        grid_attend_kernel,
        grid_spec=grid_spec,
        out_shape=jax.ShapeDtypeStruct((rows, width), jnp.bfloat16),
        compiler_params=pltpu.CompilerParams(vmem_limit_bytes=56 * 1024 * 1024),
        cost_estimate=pl.CostEstimate(
            flops=4 * rows * keys_n * width,
            transcendentals=rows * keys_n * heads,
            bytes_accessed=2 * (2 * keys_n * width + 2 * rows * width),
        ),
    )(
        live,
        main_pos.reshape(1, -1),
        extra_pos.reshape(1, -1),
        query,
        main_pages,
        main_pages,
        extra_pages,
        extra_pages,
        new_key,
        new_value,
    )


def swap_kernel(send_ref, recv_ref, send_sems, recv_sems):
    count = send_ref.shape[0]
    me = lax.axis_index("req")
    tp_me = lax.axis_index("tp")
    barrier = pltpu.get_barrier_semaphore()

    def others(fn):
        def step(peer, carry):
            @pl.when(peer != me)
            def _():
                fn(peer)

            return carry

        lax.fori_loop(0, count, step, 0)

    def greet(peer):
        pl.semaphore_signal(barrier, inc=1, device_id=(peer, tp_me), device_id_type=MESH)

    others(greet)
    pl.semaphore_wait(barrier, count - 1)

    def outgoing(peer):
        return pltpu.make_async_remote_copy(
            src_ref=send_ref.at[peer],
            dst_ref=recv_ref.at[me],
            send_sem=send_sems.at[peer],
            recv_sem=recv_sems.at[me],
            device_id=(peer, tp_me),
            device_id_type=MESH,
        )

    def arriving(peer):
        return pltpu.make_async_remote_copy(
            src_ref=send_ref.at[peer],
            dst_ref=recv_ref.at[peer],
            send_sem=send_sems.at[peer],
            recv_sem=recv_sems.at[peer],
            device_id=(peer, tp_me),
            device_id_type=MESH,
        )

    others(lambda peer: outgoing(peer).start())
    recv_ref[pl.ds(me, 1)] = send_ref[pl.ds(me, 1)]
    others(lambda peer: outgoing(peer).wait_send())
    others(lambda peer: arriving(peer).wait_recv())


def swap_pieces(pieces):
    count = pieces.shape[0]
    return pl.pallas_call(
        swap_kernel,
        out_shape=jax.ShapeDtypeStruct(pieces.shape, pieces.dtype),
        in_specs=[pl.BlockSpec(memory_space=pltpu.VMEM)],
        out_specs=pl.BlockSpec(memory_space=pltpu.VMEM),
        scratch_shapes=[pltpu.SemaphoreType.DMA((count,)), pltpu.SemaphoreType.DMA((count,))],
        compiler_params=pltpu.CompilerParams(collective_id=0, has_side_effects=True),
    )(pieces)


def key_positions(entry_of_slot):
    tokens = jnp.arange(PAGE)[None, :]
    return jnp.where(entry_of_slot[:, None] >= 0, entry_of_slot[:, None] * PAGE + tokens, 1 << 30)


def project(hidden_in, qkv_weight, live_len, local_heads, local_width):
    token_rows = hidden_in.astype(jnp.float32)
    centre = jnp.mean(token_rows, axis=-1, keepdims=True)
    centred = token_rows - centre
    spread = jnp.mean(centred * centred, axis=-1, keepdims=True)
    normed = (centred * lax.rsqrt(spread + 1e-05)).astype(jnp.bfloat16)
    united_qkv = jnp.einsum("td,dcf->tcf", normed, qkv_weight, preferred_element_type=jnp.float32)
    positions = (live_len[:, None] + jnp.arange(NEW)[None, :]).astype(jnp.float32).reshape(-1)
    query_rot = rotate(united_qkv[:, 0].reshape(-1, local_heads, HD), positions).astype(
        jnp.bfloat16
    ).reshape(-1, local_width)
    new_key = rotate(united_qkv[:, 1].reshape(-1, local_heads, HD), positions).astype(
        jnp.bfloat16
    ).reshape(-1, local_width)
    new_value = united_qkv[:, 2].astype(jnp.bfloat16)
    return query_rot, new_key, new_value


def exchange_wide(kv_pool, page_slot, holder_rows, rank_all, req_index, req_count):
    capacity = 2
    held_here = holder_rows == req_index
    ranking = jnp.cumsum(held_here.astype(jnp.int32), axis=1) - 1
    picked = held_here[:, :, None] & (ranking[:, :, None] == jnp.arange(capacity)[None, None, :])
    send_slots = jnp.sum(jnp.where(picked, page_slot[:, :, None], 0), axis=1)
    incoming = lax.all_to_all(kv_pool[send_slots], "req", split_axis=0, concat_axis=0, tiled=True)
    incoming = incoming.reshape((req_count * capacity,) + kv_pool.shape[1:])
    own_holders = holder_rows[req_index]
    own_rank = rank_all[req_index]
    slot_of_entry = own_holders * capacity + own_rank
    hit = slot_of_entry[None, :] == jnp.arange(req_count * capacity)[:, None]
    entry_of_slot = jnp.max(jnp.where(hit, jnp.arange(hit.shape[1])[None, :], -1), axis=1)
    main_pos = key_positions(entry_of_slot)
    extra_pages = incoming[:1]
    extra_pos = key_positions(jnp.full((1,), -1, jnp.int32))
    return incoming, main_pos, extra_pages, extra_pos


def exchange_relay(kv_pool, page_slot, holder_rows, rank_all, req_index, req_count):
    rows, entries = holder_rows.shape
    spill = rank_all > 0
    frag = PAGE // req_count
    width = kv_pool.shape[-1]
    spill_flat = spill.reshape(-1)
    holders_flat = holder_rows.reshape(-1)
    slots_flat = page_slot.reshape(-1)
    spill_i = spill.astype(jnp.int32)
    named = (holder_rows[:, :, None] == jnp.arange(req_count)[None, None, :]).astype(jnp.int32)
    row_spills = jnp.sum(spill_i[:, :, None] * named, axis=1)
    before = jnp.cumsum(row_spills, axis=0) - row_spills
    holder_order = jnp.sum(named * before[:, None, :], axis=2).reshape(-1)
    req_order = jnp.cumsum(spill_i, axis=1) - spill_i
    first_hit = (holder_rows == req_index) & (rank_all == 0)
    send_slots = jnp.sum(jnp.where(first_hit, page_slot, 0), axis=1)
    wanted = jnp.arange(RELAY_A)
    match_a = (
        spill_flat[None, :]
        & (holders_flat[None, :] == req_index)
        & (holder_order[None, :] == wanted[:, None])
    )
    slot_a = jnp.sum(jnp.where(match_a, slots_flat[None, :], 0), axis=1)
    pieces = (
        kv_pool[slot_a]
        .reshape(RELAY_A, 2, req_count, frag, width)
        .transpose(2, 1, 0, 3, 4)
        .reshape(req_count, 2, RELAY_A * frag, width)
    )
    padded = jnp.pad(kv_pool, ((0, 0), (0, 0), (0, RELAY_A * frag), (0, 0)))
    outgoing = padded[send_slots].at[:, :, PAGE:, :].set(pieces)
    incoming = lax.all_to_all(outgoing, "req", split_axis=0, concat_axis=0, tiled=True)
    match_b = spill[:, None, :] & (req_order[:, None, :] == jnp.arange(RELAY_B)[None, :, None])
    src_holder = jnp.sum(jnp.where(match_b, holder_rows[:, None, :], 0), axis=2)
    src_index = jnp.sum(
        jnp.where(match_b, holder_order.reshape(rows, entries)[:, None, :], 0), axis=2
    )
    zero = jnp.zeros_like(src_holder)
    starts = jnp.stack(
        [src_holder, zero, PAGE + jnp.clip(src_index, 0, RELAY_A - 1) * frag, zero], axis=-1
    )

    def window(start):
        return lax.dynamic_slice(incoming, tuple(start), (1, 2, frag, width))[0]

    extra = jax.vmap(jax.vmap(window))(starts)
    extra = extra.transpose(0, 2, 1, 3, 4).reshape(rows, 2, RELAY_B * frag, width)
    returned = swap_pieces(extra)
    extra_pages = (
        returned.reshape(req_count, 2, RELAY_B, frag, width)
        .transpose(2, 1, 0, 3, 4)
        .reshape(RELAY_B, 2, PAGE, width)
    )
    own_holders = holder_rows[req_index]
    own_first = rank_all[req_index] == 0
    entry_ids = jnp.arange(entries)
    main_hit = own_first[None, :] & (own_holders[None, :] == jnp.arange(req_count)[:, None])
    main_pos = key_positions(jnp.max(jnp.where(main_hit, entry_ids[None, :], -1), axis=1))
    extra_hit = (~own_first)[None, :] & (
        req_order[req_index][None, :] == jnp.arange(RELAY_B)[:, None]
    )
    extra_pos = key_positions(jnp.max(jnp.where(extra_hit, entry_ids[None, :], -1), axis=1))
    return incoming, main_pos, extra_pages, extra_pos


def body(hidden_in, qkv_weight, out_weight, kv_pool, cached_len, page_slot, page_holder, cont_flag):
    req_count = lax.axis_size("req")
    req_index = lax.axis_index("req")
    local_width = qkv_weight.shape[2]
    local_heads = local_width // HD
    holder_rows = page_holder[:, :, 0]
    entries = holder_rows.shape[1]
    same_holder = holder_rows[:, :, None] == holder_rows[:, None, :]
    earlier = jnp.arange(entries)[None, None, :] < jnp.arange(entries)[None, :, None]
    rank_all = jnp.sum((same_holder & earlier).astype(jnp.int32), axis=2)
    spill = (rank_all > 0).astype(jnp.int32)
    relay_fits = (jnp.max(jnp.sum(spill, axis=1)) <= RELAY_B) & (
        jnp.max(jnp.sum(spill[:, :, None] * (holder_rows[:, :, None] == jnp.arange(req_count)), axis=(0, 1)))
        <= RELAY_A
    )
    lengths = lax.dynamic_slice_in_dim(cached_len, req_index, 1)
    flags = lax.dynamic_slice_in_dim(cont_flag, req_index, 1)
    live_len = lengths * flags
    main_pages, main_pos, extra_pages, extra_pos = exchange_relay(
        kv_pool, page_slot, holder_rows, rank_all, req_index, req_count
    )
    query_rot, new_key, new_value = project(hidden_in, qkv_weight, live_len, local_heads, local_width)
    attended = attend(
        live_len, query_rot, main_pages, main_pos, extra_pages, extra_pos, new_key, new_value
    )

    def keep(ops):
        return ops[0]

    def redo(ops):
        _, query, key, value, pool, slots, holders, ranks, live = ops
        pages, pos, extra, extra_at = exchange_wide(pool, slots, holders, ranks, req_index, req_count)
        return grid_attend(live, query, pages, pos, extra, extra_at, key, value)

    attended = lax.cond(
        relay_fits,
        keep,
        redo,
        (attended, query_rot, new_key, new_value, kv_pool, page_slot, holder_rows, rank_all, live_len),
    )
    head_term = jnp.dot(attended, out_weight, preferred_element_type=jnp.float32)
    return lax.psum_scatter(head_term.astype(jnp.bfloat16), "tp", scatter_dimension=0, tiled=True)


def solution(mesh):
    in_specs = (
        P("req", None),
        P(None, None, "tp"),
        P("tp", None),
        P("req", None, None, "tp"),
        P(),
        P(),
        P(),
        P(),
    )
    out_specs = P(("req", "tp"), None)
    return jax.shard_map(body, mesh=mesh, in_specs=in_specs, out_specs=out_specs, check_vma=False)
```

```python
import functools

import jax
import jax.numpy as jnp
from jax import lax
from jax.experimental import pallas as pl
from jax.experimental.pallas import tpu as pltpu
from jax.sharding import PartitionSpec as P

HD = 128
NEW = 1024
PAGE = 128
MAXP = 32
BLOCK_Q = 256
MESH = pl.DeviceIdType.MESH
RELAY_A = 8
RELAY_B = 1


def rotate(feature, position):
    half_width = feature.shape[-1] // 2
    indices = jnp.arange(half_width).astype(jnp.float32)
    inverse = jnp.exp(indices * (-2.0 / feature.shape[-1]) * jnp.log(jnp.float32(10000.0)))
    angles = position[:, None, None] * inverse[None, None, :]
    cosine = jnp.cos(angles)
    sine_part = jnp.sin(angles)
    first_half = feature[..., :half_width]
    second_half = feature[..., half_width:]
    return jnp.concatenate(
        [
            first_half * cosine - second_half * sine_part,
            second_half * cosine + first_half * sine_part,
        ],
        axis=-1,
    )


def attend_kernel(
    live_ref, kpm_ref, kpe_ref, q_ref, mk_ref, mv_ref, ek_ref, ev_ref, nk_ref, nv_ref, out_ref
):
    live = live_ref[0]
    main_span = mk_ref.shape[0] * mk_ref.shape[1]
    extra_span = ek_ref.shape[0] * ek_ref.shape[1]
    contract = (((1,), (1,)), ((), ()))
    scale = HD ** (-0.5)
    main_ok = kpm_ref[...] < live
    extra_ok = kpe_ref[...] < live

    for block in range(q_ref.shape[0] // BLOCK_Q):
        rows = pl.ds(block * BLOCK_Q, BLOCK_Q)
        seen = pl.ds(0, (block + 1) * BLOCK_Q)
        query = q_ref[rows, :]

        def scores(keys):
            return (
                lax.dot_general(query, keys, contract, preferred_element_type=jnp.float32) * scale
            )

        main_scores = scores(mk_ref[...].reshape(main_span, HD))
        extra_scores = scores(ek_ref[...].reshape(extra_span, HD))
        new_scores = scores(nk_ref[seen, :])
        query_pos = block * BLOCK_Q + lax.broadcasted_iota(jnp.int32, new_scores.shape, 0)
        new_ok = lax.broadcasted_iota(jnp.int32, new_scores.shape, 1) <= query_pos
        main_scores = jnp.where(main_ok, main_scores, -1e30)
        extra_scores = jnp.where(extra_ok, extra_scores, -1e30)
        new_scores = jnp.where(new_ok, new_scores, -1e30)
        row_top = jnp.maximum(
            jnp.maximum(
                jnp.max(main_scores, axis=1, keepdims=True),
                jnp.max(extra_scores, axis=1, keepdims=True),
            ),
            jnp.max(new_scores, axis=1, keepdims=True),
        )
        main_w = jnp.exp(main_scores - row_top)
        extra_w = jnp.exp(extra_scores - row_top)
        new_w = jnp.exp(new_scores - row_top)
        row_total = (
            jnp.sum(main_w, axis=1, keepdims=True)
            + jnp.sum(extra_w, axis=1, keepdims=True)
            + jnp.sum(new_w, axis=1, keepdims=True)
        )

        def weighted(weights, values):
            return jnp.dot(
                weights.astype(jnp.bfloat16), values, preferred_element_type=jnp.float32
            )

        summed = (
            weighted(main_w, mv_ref[...].reshape(main_span, HD))
            + weighted(extra_w, ev_ref[...].reshape(extra_span, HD))
            + weighted(new_w, nv_ref[seen, :])
        )
        out_ref[rows, :] = (summed / row_total).astype(out_ref.dtype)


def attend(live, query, main_pages, main_pos, extra_pages, extra_pos, new_key, new_value):
    rows, width = query.shape
    heads = width // HD
    main_n = main_pages.shape[0]
    extra_n = extra_pages.shape[0]
    grid_spec = pltpu.PrefetchScalarGridSpec(
        num_scalar_prefetch=1,
        grid=(heads,),
        in_specs=[
            pl.BlockSpec((1, main_n * PAGE), lambda h, live: (0, 0)),
            pl.BlockSpec((1, extra_n * PAGE), lambda h, live: (0, 0)),
            pl.BlockSpec((rows, HD), lambda h, live: (0, h)),
            pl.BlockSpec((main_n, None, PAGE, HD), lambda h, live: (0, 0, 0, h)),
            pl.BlockSpec((main_n, None, PAGE, HD), lambda h, live: (0, 1, 0, h)),
            pl.BlockSpec((extra_n, None, PAGE, HD), lambda h, live: (0, 0, 0, h)),
            pl.BlockSpec((extra_n, None, PAGE, HD), lambda h, live: (0, 1, 0, h)),
            pl.BlockSpec((rows, HD), lambda h, live: (0, h)),
            pl.BlockSpec((rows, HD), lambda h, live: (0, h)),
        ],
        out_specs=pl.BlockSpec((rows, HD), lambda h, live: (0, h)),
    )
    keys_n = (main_n + extra_n) * PAGE + rows // 2
    return pl.pallas_call(
        attend_kernel,
        grid_spec=grid_spec,
        out_shape=jax.ShapeDtypeStruct((rows, width), jnp.bfloat16),
        compiler_params=pltpu.CompilerParams(vmem_limit_bytes=56 * 1024 * 1024),
        cost_estimate=pl.CostEstimate(
            flops=4 * rows * keys_n * width,
            transcendentals=rows * keys_n * heads,
            bytes_accessed=2 * (2 * keys_n * width + 2 * rows * width),
        ),
    )(
        live,
        main_pos.reshape(1, -1),
        extra_pos.reshape(1, -1),
        query,
        main_pages,
        main_pages,
        extra_pages,
        extra_pages,
        new_key,
        new_value,
    )


def grid_attend_kernel(
    live_ref, kpm_ref, kpe_ref, q_ref, mk_ref, mv_ref, ek_ref, ev_ref, nk_ref, nv_ref, out_ref
):
    block = pl.program_id(1)
    live = live_ref[0]
    main_span = mk_ref.shape[0] * mk_ref.shape[1]
    extra_span = ek_ref.shape[0] * ek_ref.shape[1]
    query = q_ref[...]
    contract = (((1,), (1,)), ((), ()))
    scale = HD ** (-0.5)

    def scores(keys):
        return lax.dot_general(query, keys, contract, preferred_element_type=jnp.float32) * scale

    main_scores = scores(mk_ref[...].reshape(main_span, HD))
    extra_scores = scores(ek_ref[...].reshape(extra_span, HD))
    new_scores = scores(nk_ref[...])
    main_ok = kpm_ref[...] < live
    extra_ok = kpe_ref[...] < live
    query_pos = block * BLOCK_Q + lax.broadcasted_iota(jnp.int32, new_scores.shape, 0)
    new_ok = lax.broadcasted_iota(jnp.int32, new_scores.shape, 1) <= query_pos
    main_scores = jnp.where(main_ok, main_scores, -1e30)
    extra_scores = jnp.where(extra_ok, extra_scores, -1e30)
    new_scores = jnp.where(new_ok, new_scores, -1e30)
    row_top = jnp.maximum(
        jnp.maximum(
            jnp.max(main_scores, axis=1, keepdims=True),
            jnp.max(extra_scores, axis=1, keepdims=True),
        ),
        jnp.max(new_scores, axis=1, keepdims=True),
    )
    main_w = jnp.exp(main_scores - row_top)
    extra_w = jnp.exp(extra_scores - row_top)
    new_w = jnp.exp(new_scores - row_top)
    row_total = (
        jnp.sum(main_w, axis=1, keepdims=True)
        + jnp.sum(extra_w, axis=1, keepdims=True)
        + jnp.sum(new_w, axis=1, keepdims=True)
    )

    def weighted(weights, values):
        return jnp.dot(weights.astype(jnp.bfloat16), values, preferred_element_type=jnp.float32)

    summed = (
        weighted(main_w, mv_ref[...].reshape(main_span, HD))
        + weighted(extra_w, ev_ref[...].reshape(extra_span, HD))
        + weighted(new_w, nv_ref[...])
    )
    out_ref[...] = (summed / row_total).astype(out_ref.dtype)


def grid_attend(live, query, main_pages, main_pos, extra_pages, extra_pos, new_key, new_value):
    rows, width = query.shape
    heads = width // HD
    main_n = main_pages.shape[0]
    extra_n = extra_pages.shape[0]
    grid_spec = pltpu.PrefetchScalarGridSpec(
        num_scalar_prefetch=1,
        grid=(heads, rows // BLOCK_Q),
        in_specs=[
            pl.BlockSpec((1, main_n * PAGE), lambda h, b, live: (0, 0)),
            pl.BlockSpec((1, extra_n * PAGE), lambda h, b, live: (0, 0)),
            pl.BlockSpec((BLOCK_Q, HD), lambda h, b, live: (b, h)),
            pl.BlockSpec((main_n, None, PAGE, HD), lambda h, b, live: (0, 0, 0, h)),
            pl.BlockSpec((main_n, None, PAGE, HD), lambda h, b, live: (0, 1, 0, h)),
            pl.BlockSpec((extra_n, None, PAGE, HD), lambda h, b, live: (0, 0, 0, h)),
            pl.BlockSpec((extra_n, None, PAGE, HD), lambda h, b, live: (0, 1, 0, h)),
            pl.BlockSpec((rows, HD), lambda h, b, live: (0, h)),
            pl.BlockSpec((rows, HD), lambda h, b, live: (0, h)),
        ],
        out_specs=pl.BlockSpec((BLOCK_Q, HD), lambda h, b, live: (b, h)),
    )
    keys_n = (main_n + extra_n) * PAGE + rows
    return pl.pallas_call(
        grid_attend_kernel,
        grid_spec=grid_spec,
        out_shape=jax.ShapeDtypeStruct((rows, width), jnp.bfloat16),
        compiler_params=pltpu.CompilerParams(vmem_limit_bytes=56 * 1024 * 1024),
        cost_estimate=pl.CostEstimate(
            flops=4 * rows * keys_n * width,
            transcendentals=rows * keys_n * heads,
            bytes_accessed=2 * (2 * keys_n * width + 2 * rows * width),
        ),
    )(
        live,
        main_pos.reshape(1, -1),
        extra_pos.reshape(1, -1),
        query,
        main_pages,
        main_pages,
        extra_pages,
        extra_pages,
        new_key,
        new_value,
    )


def swap_kernel(send_ref, recv_ref, send_sems, recv_sems):
    count = send_ref.shape[0]
    me = lax.axis_index("req")
    tp_me = lax.axis_index("tp")
    barrier = pltpu.get_barrier_semaphore()

    def others(fn):
        def step(peer, carry):
            @pl.when(peer != me)
            def _():
                fn(peer)

            return carry

        lax.fori_loop(0, count, step, 0)

    def greet(peer):
        pl.semaphore_signal(barrier, inc=1, device_id=(peer, tp_me), device_id_type=MESH)

    others(greet)
    pl.semaphore_wait(barrier, count - 1)

    def outgoing(peer):
        return pltpu.make_async_remote_copy(
            src_ref=send_ref.at[peer],
            dst_ref=recv_ref.at[me],
            send_sem=send_sems.at[peer],
            recv_sem=recv_sems.at[me],
            device_id=(peer, tp_me),
            device_id_type=MESH,
        )

    def arriving(peer):
        return pltpu.make_async_remote_copy(
            src_ref=send_ref.at[peer],
            dst_ref=recv_ref.at[peer],
            send_sem=send_sems.at[peer],
            recv_sem=recv_sems.at[peer],
            device_id=(peer, tp_me),
            device_id_type=MESH,
        )

    others(lambda peer: outgoing(peer).start())
    recv_ref[pl.ds(me, 1)] = send_ref[pl.ds(me, 1)]
    others(lambda peer: outgoing(peer).wait_send())
    others(lambda peer: arriving(peer).wait_recv())


def swap_pieces(pieces):
    count = pieces.shape[0]
    return pl.pallas_call(
        swap_kernel,
        out_shape=jax.ShapeDtypeStruct(pieces.shape, pieces.dtype),
        in_specs=[pl.BlockSpec(memory_space=pltpu.VMEM)],
        out_specs=pl.BlockSpec(memory_space=pltpu.VMEM),
        scratch_shapes=[pltpu.SemaphoreType.DMA((count,)), pltpu.SemaphoreType.DMA((count,))],
        compiler_params=pltpu.CompilerParams(collective_id=0, has_side_effects=True),
    )(pieces)


def key_positions(entry_of_slot):
    tokens = jnp.arange(PAGE)[None, :]
    return jnp.where(entry_of_slot[:, None] >= 0, entry_of_slot[:, None] * PAGE + tokens, 1 << 30)


def project(hidden_in, qkv_weight, live_len, local_heads, local_width):
    token_rows = hidden_in.astype(jnp.float32)
    centre = jnp.mean(token_rows, axis=-1, keepdims=True)
    centred = token_rows - centre
    spread = jnp.mean(centred * centred, axis=-1, keepdims=True)
    normed = (centred * lax.rsqrt(spread + 1e-05)).astype(jnp.bfloat16)
    united_qkv = jnp.einsum("td,dcf->tcf", normed, qkv_weight, preferred_element_type=jnp.float32)
    positions = (live_len[:, None] + jnp.arange(NEW)[None, :]).astype(jnp.float32).reshape(-1)
    query_rot = rotate(united_qkv[:, 0].reshape(-1, local_heads, HD), positions).astype(
        jnp.bfloat16
    ).reshape(-1, local_width)
    new_key = rotate(united_qkv[:, 1].reshape(-1, local_heads, HD), positions).astype(
        jnp.bfloat16
    ).reshape(-1, local_width)
    new_value = united_qkv[:, 2].astype(jnp.bfloat16)
    return query_rot, new_key, new_value


def exchange_wide(kv_pool, page_slot, holder_rows, rank_all, req_index, req_count):
    capacity = 2
    held_here = holder_rows == req_index
    ranking = jnp.cumsum(held_here.astype(jnp.int32), axis=1) - 1
    picked = held_here[:, :, None] & (ranking[:, :, None] == jnp.arange(capacity)[None, None, :])
    send_slots = jnp.sum(jnp.where(picked, page_slot[:, :, None], 0), axis=1)
    incoming = lax.all_to_all(kv_pool[send_slots], "req", split_axis=0, concat_axis=0, tiled=True)
    incoming = incoming.reshape((req_count * capacity,) + kv_pool.shape[1:])
    own_holders = holder_rows[req_index]
    own_rank = rank_all[req_index]
    slot_of_entry = own_holders * capacity + own_rank
    hit = slot_of_entry[None, :] == jnp.arange(req_count * capacity)[:, None]
    entry_of_slot = jnp.max(jnp.where(hit, jnp.arange(hit.shape[1])[None, :], -1), axis=1)
    main_pos = key_positions(entry_of_slot)
    extra_pages = incoming[:1]
    extra_pos = key_positions(jnp.full((1,), -1, jnp.int32))
    return incoming, main_pos, extra_pages, extra_pos


def exchange_relay(kv_pool, page_slot, holder_rows, rank_all, req_index, req_count):
    rows, entries = holder_rows.shape
    spill = rank_all > 0
    frag = PAGE // req_count
    width = kv_pool.shape[-1]
    spill_flat = spill.reshape(-1)
    holders_flat = holder_rows.reshape(-1)
    slots_flat = page_slot.reshape(-1)
    spill_i = spill.astype(jnp.int32)
    named = (holder_rows[:, :, None] == jnp.arange(req_count)[None, None, :]).astype(jnp.int32)
    row_spills = jnp.sum(spill_i[:, :, None] * named, axis=1)
    before = jnp.cumsum(row_spills, axis=0) - row_spills
    holder_order = jnp.sum(named * before[:, None, :], axis=2).reshape(-1)
    req_order = jnp.cumsum(spill_i, axis=1) - spill_i
    first_hit = (holder_rows == req_index) & (rank_all == 0)
    send_slots = jnp.sum(jnp.where(first_hit, page_slot, 0), axis=1)
    wanted = jnp.arange(RELAY_A)
    match_a = (
        spill_flat[None, :]
        & (holders_flat[None, :] == req_index)
        & (holder_order[None, :] == wanted[:, None])
    )
    slot_a = jnp.sum(jnp.where(match_a, slots_flat[None, :], 0), axis=1)
    pieces = (
        kv_pool[slot_a]
        .reshape(RELAY_A, 2, req_count, frag, width)
        .transpose(2, 1, 0, 3, 4)
        .reshape(req_count, 2, RELAY_A * frag, width)
    )
    padded = jnp.pad(kv_pool, ((0, 0), (0, 0), (0, RELAY_A * frag), (0, 0)))
    outgoing = padded[send_slots].at[:, :, PAGE:, :].set(pieces)
    incoming = lax.all_to_all(outgoing, "req", split_axis=0, concat_axis=0, tiled=True)
    match_b = spill[:, None, :] & (req_order[:, None, :] == jnp.arange(RELAY_B)[None, :, None])
    src_holder = jnp.sum(jnp.where(match_b, holder_rows[:, None, :], 0), axis=2)
    src_index = jnp.sum(
        jnp.where(match_b, holder_order.reshape(rows, entries)[:, None, :], 0), axis=2
    )
    zero = jnp.zeros_like(src_holder)
    starts = jnp.stack(
        [src_holder, zero, jnp.clip(src_index, 0, RELAY_A - 1) * frag, zero], axis=-1
    )

    relayed = incoming[:, :, PAGE:]

    def window(start):
        return lax.dynamic_slice(relayed, tuple(start), (1, 2, frag, width))[0]

    extra = jax.vmap(jax.vmap(window))(starts)
    extra = extra.transpose(0, 2, 1, 3, 4).reshape(rows, 2, RELAY_B * frag, width)
    returned = swap_pieces(extra)
    extra_pages = (
        returned.reshape(req_count, 2, RELAY_B, frag, width)
        .transpose(2, 1, 0, 3, 4)
        .reshape(RELAY_B, 2, PAGE, width)
    )
    own_holders = holder_rows[req_index]
    own_first = rank_all[req_index] == 0
    entry_ids = jnp.arange(entries)
    main_hit = own_first[None, :] & (own_holders[None, :] == jnp.arange(req_count)[:, None])
    main_pos = key_positions(jnp.max(jnp.where(main_hit, entry_ids[None, :], -1), axis=1))
    extra_hit = (~own_first)[None, :] & (
        req_order[req_index][None, :] == jnp.arange(RELAY_B)[:, None]
    )
    extra_pos = key_positions(jnp.max(jnp.where(extra_hit, entry_ids[None, :], -1), axis=1))
    return incoming, main_pos, extra_pages, extra_pos


def body(hidden_in, qkv_weight, out_weight, kv_pool, cached_len, page_slot, page_holder, cont_flag):
    req_count = lax.axis_size("req")
    req_index = lax.axis_index("req")
    local_width = qkv_weight.shape[2]
    local_heads = local_width // HD
    holder_rows = page_holder[:, :, 0]
    entries = holder_rows.shape[1]
    same_holder = holder_rows[:, :, None] == holder_rows[:, None, :]
    earlier = jnp.arange(entries)[None, None, :] < jnp.arange(entries)[None, :, None]
    rank_all = jnp.sum((same_holder & earlier).astype(jnp.int32), axis=2)
    spill = (rank_all > 0).astype(jnp.int32)
    relay_fits = (jnp.max(jnp.sum(spill, axis=1)) <= RELAY_B) & (
        jnp.max(jnp.sum(spill[:, :, None] * (holder_rows[:, :, None] == jnp.arange(req_count)), axis=(0, 1)))
        <= RELAY_A
    )
    lengths = lax.dynamic_slice_in_dim(cached_len, req_index, 1)
    flags = lax.dynamic_slice_in_dim(cont_flag, req_index, 1)
    live_len = lengths * flags
    main_pages, main_pos, extra_pages, extra_pos = exchange_relay(
        kv_pool, page_slot, holder_rows, rank_all, req_index, req_count
    )
    query_rot, new_key, new_value = project(hidden_in, qkv_weight, live_len, local_heads, local_width)
    attended = attend(
        live_len, query_rot, main_pages, main_pos, extra_pages, extra_pos, new_key, new_value
    )

    def keep(ops):
        return ops[0]

    def redo(ops):
        _, query, key, value, pool, slots, holders, ranks, live = ops
        pages, pos, extra, extra_at = exchange_wide(pool, slots, holders, ranks, req_index, req_count)
        return grid_attend(live, query, pages, pos, extra, extra_at, key, value)

    attended = lax.cond(
        relay_fits,
        keep,
        redo,
        (attended, query_rot, new_key, new_value, kv_pool, page_slot, holder_rows, rank_all, live_len),
    )
    head_term = jnp.dot(attended, out_weight, preferred_element_type=jnp.float32)
    return lax.psum_scatter(head_term.astype(jnp.bfloat16), "tp", scatter_dimension=0, tiled=True)


def solution(mesh):
    in_specs = (
        P("req", None),
        P(None, None, "tp"),
        P("tp", None),
        P("req", None, None, "tp"),
        P(),
        P(),
        P(),
        P(),
    )
    out_specs = P(("req", "tp"), None)
    return jax.shard_map(body, mesh=mesh, in_specs=in_specs, out_specs=out_specs, check_vma=False)
```
